32 devices in a mesh: dp: 2 (over x), ctx: 4 (over z), tp: 4 (over y, core).
Axes of the slice: x: 2, y: 2, z: 4, core: 2. Of those that a mesh axis runs over, the one named last changes fastest.
Arguments:
- inputs: bfloat16 [16, 1024, 512], P('dp', 'ctx'), may hold values from -6 to 6
- memory: bfloat16 [16, 1024, 512], P('dp', 'ctx'), may hold values from -6 to 6
- cotangent: bfloat16 [16, 1024, 512], P('dp', 'ctx'), may hold values from -6 to 6
- wq_self: bfloat16 [512, 512], P(('dp', 'ctx'), 'tp'), may hold values from -0.25 to 0.25
- wk_self: bfloat16 [512, 512], P(('dp', 'ctx'), 'tp'), may hold values from -0.25 to 0.25
- wv_self: bfloat16 [512, 512], P(('dp', 'ctx'), 'tp'), may hold values from -0.25 to 0.25
- wo_self: bfloat16 [512, 512], P('tp', ('dp', 'ctx')), may hold values from -1 to 1
- wq_cross: bfloat16 [512, 512], P(('dp', 'ctx'), 'tp'), may hold values from -0.25 to 0.25
- wk_cross: bfloat16 [512, 512], P(('dp', 'ctx'), 'tp'), may hold values from -0.25 to 0.25
- wv_cross: bfloat16 [512, 512], P(('dp', 'ctx'), 'tp'), may hold values from -0.25 to 0.25
- wo_cross: bfloat16 [512, 512], P('tp', ('dp', 'ctx')), may hold values from -1 to 1
- w_in: bfloat16 [512, 2048], P(('dp', 'ctx'), 'tp'), may hold values from -0.25 to 0.25
- w_out: bfloat16 [2048, 512], P('tp', ('dp', 'ctx')), may hold values from -0.125 to 0.125
- gains: bfloat16 [3, 512], P(None, ('dp', 'ctx', 'tp')), may hold values from 0.25 to 1.75
- shifts: bfloat16 [10, 512], P(None, ('dp', 'ctx', 'tp')), may hold values from -1 to 1
- ffn_bias: bfloat16 [2048], P(('dp', 'ctx', 'tp')), may hold values from -1 to 1
Outputs:
- output: bfloat16 [16, 1024, 512], P('dp', 'ctx')
- grad_inputs: float32 [16, 1024, 512], P('dp', 'ctx')
- grad_memory: float32 [16, 1024, 512], P('dp', 'ctx')
- grad_wq_self: float32 [512, 512], P(('dp', 'ctx'), 'tp')
- grad_wk_self: float32 [512, 512], P(('dp', 'ctx'), 'tp')
- grad_wv_self: float32 [512, 512], P(('dp', 'ctx'), 'tp')
- grad_wo_self: float32 [512, 512], P('tp', ('dp', 'ctx'))
- grad_wq_cross: float32 [512, 512], P(('dp', 'ctx'), 'tp')
- grad_wk_cross: float32 [512, 512], P(('dp', 'ctx'), 'tp')
- grad_wv_cross: float32 [512, 512], P(('dp', 'ctx'), 'tp')
- grad_wo_cross: float32 [512, 512], P('tp', ('dp', 'ctx'))
- grad_w_in: float32 [512, 2048], P(('dp', 'ctx'), 'tp')
- grad_w_out: float32 [2048, 512], P('tp', ('dp', 'ctx'))
- grad_gains: float32 [3, 512], P(None, ('dp', 'ctx', 'tp'))
- grad_shifts: float32 [10, 512], P(None, ('dp', 'ctx', 'tp'))
- grad_ffn_bias: float32 [2048], P(('dp', 'ctx', 'tp'))
The draws below stay inside these ranges and needn't reach their ends.
All inputs are finite; a program needn't handle non-finite values.
Results may differ from the reference program's by a relative error of at most 0.022.
Values may be sent and summed in bfloat16 or wider, within the bound.
No kernel may reach another device: no remote copies, remote signals or barrier semaphores. Data moves between devices by JAX's collectives and lax.ppermute only.
A program may use at most 128 MiB of HBM per device.

```python
import jax
import jax.numpy as jnp
from jax import lax

D = 512
HEADS = 8
HD = 64
FF = 2048
BLOCK = 256
SEQ_DEV = 8
LEN = 1024
MEM = 1024
SEQS = 16
N_DP = 2


def draw_shifts(key, part):
    spread = jnp.array([0.2, 0.02, 0.2, 0.2, 0.2, 0.02, 0.2, 0.2, 0.2, 0.2], jnp.float32)[:, None]
    sample = jax.random.truncated_normal(key, -5.0, 5.0, (10, D), jnp.float32)
    return (spread * sample).astype(jnp.bfloat16)


def block_levels(key, dims, pieces, smallest, top_value):
    gain, own = 1.0, jax.random.fold_in(key, 6)
    for axis_at, parts in pieces:
        heights = jnp.exp(jax.random.uniform(jax.random.fold_in(own, axis_at), (parts,), jnp.float32, smallest / len(pieces), top_value / len(pieces)))
        gain = gain * jnp.repeat(heights, dims[axis_at] // parts).reshape([-1 if axis == axis_at else 1 for axis in range(len(dims))])
    return gain


def normal_values(key, dims, deviation, reach, cuts=(), dtype=jnp.bfloat16):
    drawn = jax.random.normal(key, dims, jnp.float32) * deviation
    if len(cuts) > 0:
        drawn = block_levels(key, dims, cuts, -0.22, 0.18) * drawn
    return jnp.clip(drawn, min=-reach, max=reach).astype(dtype)


def setup_inputs(seed: int = 0) -> dict:
    key_of = jax.random.split(jax.random.key(seed), 17)
    return {
        "inputs": normal_values(key_of[0], (SEQS, LEN, D), 1.0, 6.0, ((0, 2), (1, 4))),
        "memory": normal_values(key_of[1], (SEQS, MEM, D), 1.0, 6.0, ((0, 2), (1, 4))),
        "cotangent": normal_values(key_of[2], (SEQS, LEN, D), 1.0, 6.0, ((0, 2), (1, 4))),
        "wq_self": normal_values(key_of[3], (D, D), D ** -0.5, 0.25, ((0, 8), (1, 4))),
        "wk_self": normal_values(key_of[4], (D, D), D ** -0.5, 0.25, ((0, 8), (1, 4))),
        "wv_self": normal_values(key_of[5], (D, D), D ** -0.5, 0.25, ((0, 8), (1, 4))),
        "wo_self": normal_values(key_of[6], (D, D), (D // 16) ** -0.5, 1.0, ((0, 4), (1, 8))),
        "wq_cross": normal_values(key_of[7], (D, D), D ** -0.5, 0.25, ((0, 8), (1, 4))),
        "wk_cross": normal_values(key_of[8], (D, D), D ** -0.5, 0.25, ((0, 8), (1, 4))),
        "wv_cross": normal_values(key_of[9], (D, D), D ** -0.5, 0.25, ((0, 8), (1, 4))),
        "wo_cross": normal_values(key_of[10], (D, D), (D // 16) ** -0.5, 1.0, ((0, 4), (1, 8))),
        "w_in": normal_values(key_of[11], (D, FF), D ** -0.5, 0.25, ((0, 8), (1, 4))),
        "w_out": normal_values(key_of[12], (FF, D), FF ** -0.5, 0.125, ((0, 4), (1, 8))),
        "gains": jnp.clip(1.0 + 0.15 * jax.random.normal(key_of[13], (3, D), jnp.float32), 0.25, 1.75).astype(jnp.bfloat16),
        "shifts": draw_shifts(jax.random.fold_in(key_of[16], 71), 0),
        "ffn_bias": normal_values(key_of[15], (FF,), 0.2, 1.0, ((0, 32),)),
    }


@jax.custom_vjp
def low(v):
    return lax.optimization_barrier(v.astype(jnp.bfloat16)).astype(jnp.float32)

@jax.custom_vjp
def low_back(v):
    return v

def low_keep(v):
    return (low(v), None)

def low_pass(kept, grad):
    return (grad,)

def back_keep(v):
    return (v, None)

def back_low(kept, grad):
    return (low(grad),)
low.defvjp(low_keep, low_pass)
low_back.defvjp(back_keep, back_low)
EPS = 1e-05

def matmul_full(left, right):
    return jnp.dot(left, right, precision=lax.Precision.HIGHEST)

def layer_norm(values, weight, offset):
    average = lax.optimization_barrier(jnp.mean(values, axis=-1, keepdims=True))
    centered = values - average
    variance = lax.optimization_barrier(jnp.mean(centered * centered, axis=-1, keepdims=True))
    return centered * lax.rsqrt(variance + EPS) * weight + offset

def attend(queries, key_rows, values, allowed):
    raw_scores = low_back(jnp.einsum('qhe,khe->hqk', queries, key_rows, precision=lax.Precision.HIGHEST))
    scores = jnp.where(allowed[None], raw_scores * HD ** (-0.5), -1e+30)
    soft_weights = jax.nn.softmax(scores, axis=-1)
    mixed_heads = jnp.einsum('hqk,khe->qhe', low(soft_weights), values, precision=lax.Precision.HIGHEST)
    return low_back(low(mixed_heads))

def forward(inputs, memory, params):
    wq_self, wk_self, wv_self, wo_self, wq_cross, wk_cross, wv_cross, wo_cross, w_in, w_out, gains, shifts, ffn_bias = params
    number = inputs.shape[0]
    flat_x = inputs.reshape(number * LEN, D)
    flat_m = memory.reshape(number * MEM, D)
    queries = low_back(low(matmul_full(flat_x, wq_self) + shifts[0]))
    key_rows = low_back(low(matmul_full(flat_x, wk_self)))
    value_rows = low_back(low(matmul_full(flat_x, wv_self) + shifts[1]))
    places = jnp.arange(LEN) // BLOCK
    causal = places[None, :] <= places[:, None]
    open_mask = jnp.ones((LEN, MEM), jnp.bool_)

    def self_block(triple):
        return attend(triple[0], triple[1], triple[2], causal)

    def cross_block(triple):
        return attend(triple[0], triple[1], triple[2], open_mask)
    self_view = (number, LEN, HEADS, HD)
    mem_view = (number, MEM, HEADS, HD)
    attended = lax.map(jax.checkpoint(self_block), (queries.reshape(self_view), key_rows.reshape(self_view), value_rows.reshape(self_view)))
    branch = low_back(matmul_full(attended.reshape(number * LEN, D), wo_self))
    normed_one = layer_norm(flat_x + branch + shifts[2], gains[0], shifts[3])
    cross_q = low_back(low(matmul_full(low(normed_one), wq_cross) + shifts[4]))
    cross_k = low_back(low(matmul_full(flat_m, wk_cross)))
    cross_v = low_back(low(matmul_full(flat_m, wv_cross) + shifts[5]))
    cross_att = lax.map(jax.checkpoint(cross_block), (cross_q.reshape(self_view), cross_k.reshape(mem_view), cross_v.reshape(mem_view)))
    cross_branch = low_back(matmul_full(cross_att.reshape(number * LEN, D), wo_cross))
    normed_two = layer_norm(normed_one + cross_branch + shifts[6], gains[1], shifts[7])
    pre_act = low_back(matmul_full(low(normed_two), w_in) + ffn_bias)
    activated = low_back(low(jax.nn.gelu(pre_act)))
    ffn_branch = low_back(matmul_full(activated, w_out))
    result = layer_norm(normed_two + ffn_branch + shifts[8], gains[2], shifts[9])
    return result.reshape(number, LEN, D)

def reference(inputs, memory, cotangent, wq_self, wk_self, wv_self, wo_self, wq_cross, wk_cross, wv_cross, wo_cross, w_in, w_out, gains, shifts, ffn_bias):
    params = tuple((item.astype(jnp.float32) for item in (wq_self, wk_self, wv_self, wo_self, wq_cross, wk_cross, wv_cross, wo_cross, w_in, w_out, gains, shifts, ffn_bias)))
    group_x = inputs.astype(jnp.float32).reshape(N_DP, SEQ_DEV, LEN, D)
    group_m = memory.astype(jnp.float32).reshape(N_DP, SEQ_DEV, MEM, D)
    group_g = cotangent.astype(jnp.float32).reshape(N_DP, SEQ_DEV, LEN, D)

    def one_group(totals, slices):
        x_part, m_part, g_part = slices
        result, pullback = jax.vjp(forward, x_part, m_part, params)
        grad_x, grad_m, grad_p = pullback(g_part)
        totals = jax.tree.map(jnp.add, totals, grad_p)
        return (totals, (result.astype(jnp.bfloat16), grad_x, grad_m))
    zeros_start = jax.tree.map(jnp.zeros_like, params)
    totals, (outputs, grad_x, grad_m) = lax.scan(one_group, zeros_start, (group_x, group_m, group_g))
    return (outputs.reshape(SEQS, LEN, D), grad_x.reshape(SEQS, LEN, D), grad_m.reshape(SEQS, MEM, D), totals[0], totals[1], totals[2], totals[3], totals[4], totals[5], totals[6], totals[7], totals[8], totals[9], totals[10], totals[11], totals[12])
```

```python
import functools

import jax
import jax.numpy as jnp
from jax import lax
from jax.experimental import pallas as pl
from jax.experimental.pallas import tpu as pltpu
from jax.sharding import PartitionSpec as P

HD = 64
EPS = 1e-05
BF = jnp.bfloat16
F32 = jnp.float32
PAIR = 2 * HD
VMEM_LIMIT = 56 << 20
GELU_C = 0.7978845608028654
GELU_A = 0.044715


def nn(left, right):
    return lax.dot_general(left, right, (((1,), (0,)), ((), ())), preferred_element_type=F32)


def nt(left, right):
    return lax.dot_general(left, right, (((1,), (1,)), ((), ())), preferred_element_type=F32)


def params(**kw):
    return pltpu.CompilerParams(vmem_limit_bytes=VMEM_LIMIT, dimension_semantics=kw.pop("sem"), **kw)


def full(shape):
    return pl.BlockSpec(shape, lambda *_: (0,) * len(shape))


def norm_stats(z):
    mean = jnp.mean(z, axis=-1, keepdims=True)
    cent = z - mean
    var = jnp.mean(cent * cent, axis=-1, keepdims=True)
    inv = lax.rsqrt(var + EPS)
    return cent * inv, inv


def norm_back(grad, gain, normed, inv):
    e = grad * gain
    me = jnp.mean(e, axis=-1, keepdims=True)
    men = jnp.mean(e * normed, axis=-1, keepdims=True)
    return inv * (e - me - normed * men)


def rows_sum(a):
    return jnp.sum(a, axis=0, keepdims=True)


def split_pair(block):
    lane = lax.broadcasted_iota(jnp.int32, block.shape, 1)
    zero = jnp.zeros_like(block)
    return jnp.concatenate(
        [jnp.where(lane < HD, block, zero), jnp.where(lane < HD, zero, block)], axis=0
    )


def join_pair(both):
    q = both.shape[1] // 2
    row = lax.broadcasted_iota(jnp.int32, (both.shape[0], q), 0)
    return jnp.where(row < HD, both[:, :q], both[:, q:])


def attn_fwd_body(
    causal, q_rows, kv_parts, w_ref, vecp_ref, q_row, v_row,
    q_ref, k_ref, v_ref, p_refs, ot_ref, o_ref, il_ref, acc_ref,
):
    d = q_rows.shape[1]
    wq = w_ref[:, 0, 0].reshape(d, PAIR)
    wkv = jnp.concatenate(
        [w_ref[:, 0, 1].reshape(d, PAIR), w_ref[:, 0, 2].reshape(d, PAIR)], axis=1
    )
    wo = w_ref[:, 0, 3].reshape(d, PAIR)
    kv = nn(kv_parts, wkv)
    k = kv[:, :PAIR].astype(BF)
    v = (kv[:, PAIR:] + vecp_ref[v_row : v_row + 1]).astype(BF)
    q = (nn(q_rows, wq) + vecp_ref[q_row : q_row + 1]).astype(BF) * HD ** (-0.5)
    q_ref[0] = q
    k_ref[0] = k
    v_ref[0] = v
    vt = v.T
    blocks = len(p_refs)
    rows = q.shape[0] // blocks
    keys = k.shape[0]
    for b in range(blocks):
        n = keys // blocks * (b + 1) if causal else keys
        s = nt(k[:n], split_pair(q[b * rows : (b + 1) * rows]))
        top = jnp.max(s, axis=0, keepdims=True)
        p = jnp.exp(s - top)
        inv = 1.0 / jnp.sum(p, axis=0, keepdims=True)
        pb = p.astype(BF)
        p_refs[b][0] = pb
        ot = join_pair(nn(vt[:, :n], pb) * inv)
        span = slice(b * rows, (b + 1) * rows)
        ot_ref[0, :, span] = ot.astype(BF)
        o_ref[0, span, :] = ot.T.astype(BF)
        il_ref[0, 0:1, span] = inv[:, :rows]
        il_ref[0, 1:2, span] = inv[:, rows:]
    acc_ref[...] += nt(o_ref[0], wo)


def self_fwd(xo_ref, xp_ref, w_ref, vecp_ref, vec_ref, q_ref, k_ref, v_ref, p0, p1, p2, p3,
             ot_ref, o_ref, il_ref, n_ref, r_ref, x_all, acc_ref):
    t = pl.program_id(0)
    blocks = 4
    half = xo_ref.shape[0] // blocks

    @pl.when(t == 0)
    def _():
        for b in range(blocks):
            x_all[2 * b * half : (2 * b + 1) * half] = xo_ref[b * half : (b + 1) * half]
            x_all[(2 * b + 1) * half : (2 * b + 2) * half] = xp_ref[b * half : (b + 1) * half]
        acc_ref[...] = xo_ref[...].astype(F32) + vec_ref[5:6]

    attn_fwd_body(True, xo_ref[...], x_all[...], w_ref, vecp_ref, 3, 4,
                  q_ref, k_ref, v_ref, (p0, p1, p2, p3), ot_ref, o_ref, il_ref, acc_ref)

    @pl.when(t == pl.num_programs(0) - 1)
    def _():
        normed, inv = norm_stats(acc_ref[...])
        n_ref[...] = normed
        r_ref[...] = jnp.broadcast_to(inv, r_ref.shape)


def cross_fwd(n1_ref, mo_ref, mp_ref, w_ref, vecp_ref, vec_ref, q_ref, k_ref, v_ref, p0, p1, p2, p3,
              ot_ref, o_ref, il_ref, n_ref, r_ref, m_all, h_low, acc_ref):
    t = pl.program_id(0)
    half = mo_ref.shape[0]

    @pl.when(t == 0)
    def _():
        m_all[:half] = mo_ref[...]
        m_all[half:] = mp_ref[...]
        h1 = n1_ref[...] * vec_ref[0:1] + vec_ref[6:7]
        h_low[...] = h1.astype(BF)
        acc_ref[...] = h1 + vec_ref[9:10]

    attn_fwd_body(False, h_low[...], m_all[...], w_ref, vecp_ref, 7, 8,
                  q_ref, k_ref, v_ref, (p0, p1, p2, p3), ot_ref, o_ref, il_ref, acc_ref)

    @pl.when(t == pl.num_programs(0) - 1)
    def _():
        normed, inv = norm_stats(acc_ref[...])
        n_ref[...] = normed
        r_ref[...] = jnp.broadcast_to(inv, r_ref.shape)


def ffn_both(n2_ref, r2_ref, cot_ref, w_ref, bias_ref, vec_ref,
             out_ref, gin_ref, gout_ref, dz2_ref, vg_ref, bg_ref,
             h_low, h_t, act, slope, acc, dz3_low, dz3_t, dh2):
    phase = pl.program_id(0)
    t = pl.program_id(1)
    d = n2_ref.shape[1]
    last = pl.num_programs(1) - 1
    w_in = w_ref[:, 0, 0].reshape(d, -1)
    w_out = w_ref[:, 0, 1].reshape(d, -1)

    @pl.when((phase == 0) & (t == 0))
    def _():
        h2 = n2_ref[...] * vec_ref[1:2] + vec_ref[10:11]
        h_low[...] = h2.astype(BF)
        h_t[...] = h2.astype(BF).T
        acc[...] = h2 + vec_ref[11:12]

    @pl.when(phase == 0)
    def _():
        u = nn(h_low[...], w_in) + bias_ref[0]
        cube = GELU_A * u * u
        th = jnp.tanh(GELU_C * u * (1.0 + cube))
        low = 0.5 * (1.0 + th)
        f = (u * low).astype(BF)
        act[t] = f
        slope[t] = low + 0.5 * u * (1.0 - th * th) * (GELU_C * (1.0 + 3.0 * cube))
        acc[...] += nt(f, w_out)

    @pl.when((phase == 0) & (t == last))
    def _():
        n3, r3 = norm_stats(acc[...])
        out_ref[...] = (n3 * vec_ref[2:3] + vec_ref[12:13]).astype(BF)
        g = cot_ref[...].astype(F32)
        vg_ref[0:1] = rows_sum(g * n3)
        vg_ref[1:2] = rows_sum(g)
        dz3 = norm_back(g, vec_ref[2:3], n3, r3)
        vg_ref[2:3] = rows_sum(dz3)
        low = dz3.astype(BF)
        dz3_low[...] = low
        dz3_t[...] = low.T
        dh2[...] = dz3

    @pl.when(phase == 1)
    def _():
        f = act[t]
        df = nn(dz3_low[...], w_out).astype(BF).astype(F32)
        du = (df * slope[t]).astype(BF)
        gout_ref[...] = nn(dz3_t[...], f).astype(BF).reshape(gout_ref.shape)
        gin_ref[...] = nn(h_t[...], du).astype(BF).reshape(gin_ref.shape)
        bg_ref[0] = rows_sum(du.astype(F32))
        dh2[...] += nt(du, w_in)

    @pl.when((phase == 1) & (t == last))
    def _():
        g = dh2[...]
        n2 = n2_ref[...]
        vg_ref[3:4] = rows_sum(g * n2)
        vg_ref[4:5] = rows_sum(g)
        dz2 = norm_back(g, vec_ref[1:2], n2, r2_ref[:, 0:1])
        vg_ref[5:6] = rows_sum(dz2)
        vg_ref[6:8] = jnp.zeros_like(vg_ref[6:8])
        dz2_ref[...] = dz2


def attn_bwd(causal, act_ref, dz_ref, w_ref, vec_ref, q_ref, k_ref, v_ref, p0, p1, p2, p3,
             ot_ref, o_ref, il_ref, n_ref, r_ref,
             gq_ref, go_ref, own_ref, peer_ref, out_ref, vg_ref, qg_ref,
             dy, dy_t, act_t, acc, dk_ref, dv_ref):
    t = pl.program_id(0)
    d = dz_ref.shape[1]
    p_refs = (p0, p1, p2, p3)
    blocks = len(p_refs)
    wq = w_ref[:, 0, 0].reshape(d, PAIR)
    wo = w_ref[:, 0, 3].reshape(d, PAIR)

    @pl.when(t == 0)
    def _():
        dz = dz_ref[...]
        low = dz.astype(BF)
        dy[...] = low
        dy_t[...] = low.T
        acc[...] = dz
        if causal:
            act_t[...] = act_ref[...].T
        else:
            h = n_ref[...] * vec_ref[0:1] + vec_ref[6:7]
            act_t[...] = h.astype(BF).T

    q = q_ref[0]
    k = k_ref[0]
    v = v_ref[0]
    keys = k.shape[0]
    rows = q.shape[0] // blocks
    do = nn(dy[...], wo).astype(BF)
    go_ref[...] = nn(dy_t[...], o_ref[0]).astype(BF).reshape(go_ref.shape)
    do_t = do.T.astype(F32)
    prod = do_t * ot_ref[0].astype(F32)
    inv_a, inv_b = il_ref[0, 0:1], il_ref[0, 1:2]
    inner_a = jnp.sum(prod[:HD], axis=0, keepdims=True) * inv_a
    inner_b = jnp.sum(prod[HD:], axis=0, keepdims=True) * inv_b
    row = lax.broadcasted_iota(jnp.int32, do_t.shape, 0)
    dos = (do_t * jnp.where(row < HD, inv_a, inv_b)).astype(BF).T
    kt = k.T
    dqs = [None] * blocks
    for b in reversed(range(blocks)):
        n = keys // blocks * (b + 1) if causal else keys
        span = slice(b * rows, (b + 1) * rows)
        dob = split_pair(dos[span])
        qb = split_pair(q[span])
        pb = p_refs[b][0]
        dp = nt(v[:n], dob)
        inner = jnp.concatenate([inner_a[:, span], inner_b[:, span]], axis=1)
        ds = (pb.astype(F32) * (dp - inner)).astype(BF)
        dv = nn(pb, dob)
        dk = nn(ds, qb)
        if b == blocks - 1:
            dv_ref[...] = dv
            dk_ref[...] = dk
        else:
            dv_ref[:n] += dv
            dk_ref[:n] += dk
        dqs[b] = (join_pair(nn(kt[:, :n], ds)) * HD ** (-0.5)).T.astype(BF)
    dq = jnp.concatenate(dqs, axis=0)
    gq_ref[...] = nn(act_t[...], dq).astype(BF).reshape(gq_ref.shape)
    qg_ref[0] = rows_sum(dq.astype(F32))
    acc[...] += nt(dq, wq)
    for i, ref in enumerate((dk_ref, dv_ref)):
        if causal:
            for b in range(blocks):
                at = 2 * b * rows
                own_ref[i, 0, b * rows : (b + 1) * rows] = ref[at : at + rows]
                peer_ref[i, 0, b * rows : (b + 1) * rows] = ref[at + rows : at + 2 * rows].astype(BF)
        else:
            own_ref[i, 0] = ref[: keys // 2]
            peer_ref[i, 0] = ref[keys // 2 :].astype(BF)

    @pl.when(t == pl.num_programs(0) - 1)
    def _():
        g = acc[...]
        if causal:
            out_ref[...] = g
            vg_ref[...] = jnp.zeros_like(vg_ref)
        else:
            normed = n_ref[...]
            vg_ref[0:1] = rows_sum(g * normed)
            vg_ref[1:2] = rows_sum(g)
            dz1 = norm_back(g, vec_ref[0:1], normed, r_ref[:, 0:1])
            vg_ref[2:3] = rows_sum(dz1)
            vg_ref[3:8] = jnp.zeros_like(vg_ref[3:8])
            out_ref[...] = dz1


def kv_back(with_base, act_ref, own_ref, got_ref, w_ref, *rest):
    if with_base:
        base_ref, out_ref, gk_ref, gv_ref, vgrad_ref, act_t, acc = rest
    else:
        out_ref, gk_ref, gv_ref, vgrad_ref, act_t, acc = rest
    t = pl.program_id(0)
    d = act_ref.shape[1]
    wk = w_ref[:, 0, 1].reshape(d, PAIR)
    wv = w_ref[:, 0, 2].reshape(d, PAIR)

    @pl.when(t == 0)
    def _():
        act_t[...] = act_ref[...].T
        if with_base:
            acc[...] = base_ref[...]
        else:
            acc[...] = jnp.zeros_like(acc)

    dk = (own_ref[0, 0] + got_ref[0, 0].astype(F32)).astype(BF)
    dv = (own_ref[1, 0] + got_ref[1, 0].astype(F32)).astype(BF)
    dkv = jnp.concatenate([dk, dv], axis=1)
    gkv = nn(act_t[...], dkv).astype(BF)
    gk_ref[...] = gkv[:, :PAIR].reshape(gk_ref.shape)
    gv_ref[...] = gkv[:, PAIR:].reshape(gv_ref.shape)
    vgrad_ref[0] = rows_sum(dv.astype(F32))
    acc[...] += nt(dkv, jnp.concatenate([wk, wv], axis=1))

    @pl.when(t == pl.num_programs(0) - 1)
    def _():
        out_ref[...] = acc[...].astype(BF)


def pair_spec(rows):
    return pl.BlockSpec((1, rows, PAIR), lambda t: (t, 0, 0))


def struct(shape, dtype):
    return jax.ShapeDtypeStruct(shape, dtype)


def weight_spec(w):
    return pl.BlockSpec((w.shape[0], 1) + w.shape[2:], lambda t: (0, t, 0, 0, 0))


def grad_spec(dc, rows):
    return pl.BlockSpec((dc, 1, rows, PAIR), lambda t: (0, t, 0, 0))


def run_attn_fwd(causal, rows_in, w, vec):
    d = vec.shape[1]
    own = rows_in[0].shape[0]
    keys = 2 * own
    pairs = w.shape[1]
    blocks = 4
    ns = [keys // blocks * (b + 1) if causal else keys for b in range(blocks)]
    qn = 2 * own // blocks
    out_shape = (
        struct((pairs, own, PAIR), BF),
        struct((pairs, keys, PAIR), BF),
        struct((pairs, keys, PAIR), BF),
        *[struct((pairs, n, qn), BF) for n in ns],
        struct((pairs, PAIR, own), BF),
        struct((pairs, own, PAIR), BF),
        struct((pairs, 8, own), F32),
        struct((own, d), F32),
        struct((own, PAIR), F32),
    )
    out_specs = (
        pair_spec(own),
        pair_spec(keys),
        pair_spec(keys),
        *[pl.BlockSpec((1, n, qn), lambda t: (t, 0, 0)) for n in ns],
        pl.BlockSpec((1, PAIR, own), lambda t: (t, 0, 0)),
        pair_spec(own),
        pl.BlockSpec((1, 8, own), lambda t: (t, 0, 0)),
        full((own, d)),
        full((own, PAIR)),
    )
    in_specs = [full(a.shape) for a in rows_in] + [
        weight_spec(w),
        pl.BlockSpec((vec.shape[0], PAIR), lambda t: (0, t)),
        full(vec.shape),
    ]
    scratch = [pltpu.VMEM((keys, d), BF)]
    if not causal:
        scratch.append(pltpu.VMEM((own, d), BF))
    scratch.append(pltpu.VMEM((own, d), F32))
    area = sum(ns) * qn
    return pl.pallas_call(
        self_fwd if causal else cross_fwd,
        grid=(pairs,),
        in_specs=in_specs,
        out_specs=out_specs,
        out_shape=out_shape,
        scratch_shapes=scratch,
        compiler_params=params(sem=("arbitrary",)),
        cost_estimate=pl.CostEstimate(
            flops=2 * own * d * d * 6 + 4 * area * PAIR * pairs,
            bytes_accessed=2 * area * pairs + 8 * own * d,
            transcendentals=area * pairs,
        ),
        name="self_fwd" if causal else "cross_fwd",
    )(*rows_in, w, vec, vec)


def run_ffn(n2, r2, cot, w, bias, vec):
    own, d = n2.shape
    dc, parts, _, prows, hid = w.shape
    back = lambda p, t: (0, p * t, 0, 0)
    return pl.pallas_call(
        ffn_both,
        grid=(2, parts),
        in_specs=[
            full(n2.shape),
            full(r2.shape),
            full(cot.shape),
            pl.BlockSpec((dc, 1, 2, prows, hid), lambda p, t: (0, t, 0, 0, 0)),
            pl.BlockSpec((1, 1, hid), lambda p, t: (t, 0, 0)),
            full(vec.shape),
        ],
        out_specs=(
            full((own, d)),
            pl.BlockSpec((dc, 1, prows, hid), back),
            pl.BlockSpec((dc, 1, prows, hid), back),
            full((own, d)),
            full((8, d)),
            pl.BlockSpec((1, 1, hid), lambda p, t: (p * t, 0, 0)),
        ),
        out_shape=(
            struct((own, d), BF),
            struct((dc, parts, prows, hid), BF),
            struct((dc, parts, prows, hid), BF),
            struct((own, d), F32),
            struct((8, d), F32),
            struct((parts, 1, hid), F32),
        ),
        scratch_shapes=[
            pltpu.VMEM((own, d), BF),
            pltpu.VMEM((d, own), BF),
            pltpu.VMEM((parts, own, hid), BF),
            pltpu.VMEM((parts, own, hid), F32),
            pltpu.VMEM((own, d), F32),
            pltpu.VMEM((own, d), BF),
            pltpu.VMEM((d, own), BF),
            pltpu.VMEM((own, d), F32),
        ],
        compiler_params=params(sem=("arbitrary", "arbitrary")),
        cost_estimate=pl.CostEstimate(
            flops=12 * own * d * hid * parts,
            bytes_accessed=4 * dc * parts * 2 * prows * hid + 20 * own * d,
            transcendentals=own * hid * parts,
        ),
        name="ffn_both",
    )(n2, r2, cot, w, bias, vec)


def run_attn_bwd(causal, act, dz, w, vec, saved, n, r):
    q, k, v, p0, p1, p2, p3, ot, o, il = saved
    pairs, own, _ = q.shape
    keys = k.shape[1]
    d = dz.shape[1]
    dc, _, _, prows, _ = w.shape
    ps = (p0, p1, p2, p3)
    area = sum(p.shape[1] * p.shape[2] for p in ps)
    kv_spec = pl.BlockSpec((2, 1, own, PAIR), lambda t: (0, t, 0, 0))
    return pl.pallas_call(
        functools.partial(attn_bwd, causal),
        grid=(pairs,),
        in_specs=[
            full(act.shape),
            full(dz.shape),
            weight_spec(w),
            full(vec.shape),
            pair_spec(own),
            pair_spec(keys),
            pair_spec(keys),
            *[pl.BlockSpec((1,) + p.shape[1:], lambda t: (t, 0, 0)) for p in ps],
            pl.BlockSpec((1, PAIR, own), lambda t: (t, 0, 0)),
            pair_spec(own),
            pl.BlockSpec((1, 8, own), lambda t: (t, 0, 0)),
            full(n.shape),
            full(r.shape),
        ],
        out_specs=(
            grad_spec(dc, prows),
            grad_spec(dc, prows),
            kv_spec,
            kv_spec,
            full((own, d)),
            full((8, d)),
            pl.BlockSpec((1, 1, PAIR), lambda t: (t, 0, 0)),
        ),
        out_shape=(
            struct((dc, pairs, prows, PAIR), BF),
            struct((dc, pairs, prows, PAIR), BF),
            struct((2, pairs, own, PAIR), F32),
            struct((2, pairs, own, PAIR), BF),
            struct((own, d), F32),
            struct((8, d), F32),
            struct((pairs, 1, PAIR), F32),
        ),
        scratch_shapes=[
            pltpu.VMEM((own, d), BF),
            pltpu.VMEM((d, own), BF),
            pltpu.VMEM((d, own), BF),
            pltpu.VMEM((own, d), F32),
            pltpu.VMEM((keys, PAIR), F32),
            pltpu.VMEM((keys, PAIR), F32),
        ],
        compiler_params=params(sem=("arbitrary",)),
        cost_estimate=pl.CostEstimate(
            flops=2 * own * d * d * 4 + 8 * area * PAIR * pairs,
            bytes_accessed=2 * area * pairs + 16 * own * d,
            transcendentals=0,
        ),
        name="self_bwd" if causal else "cross_bwd",
    )(act, dz, w, vec, *saved, n, r)


def run_kv_back(name, act, own_part, got, w, base):
    own, d = act.shape
    dc, pairs, _, prows, _ = w.shape
    kv_spec = pl.BlockSpec((2, 1, own, PAIR), lambda t: (0, t, 0, 0))
    ins = [act, own_part, got, w]
    specs = [full(act.shape), kv_spec, kv_spec, weight_spec(w)]
    if base is not None:
        ins.append(base)
        specs.append(full(base.shape))
    return pl.pallas_call(
        functools.partial(kv_back, base is not None),
        grid=(pairs,),
        in_specs=specs,
        out_specs=(
            full((own, d)),
            grad_spec(dc, prows),
            grad_spec(dc, prows),
            pl.BlockSpec((1, 1, PAIR), lambda t: (t, 0, 0)),
        ),
        out_shape=(
            struct((own, d), BF),
            struct((dc, pairs, prows, PAIR), BF),
            struct((dc, pairs, prows, PAIR), BF),
            struct((pairs, 1, PAIR), F32),
        ),
        scratch_shapes=[pltpu.VMEM((d, own), BF), pltpu.VMEM((own, d), F32)],
        compiler_params=params(sem=("arbitrary",)),
        cost_estimate=pl.CostEstimate(
            flops=8 * own * d * d, bytes_accessed=20 * own * d, transcendentals=0
        ),
        name=name,
    )(*ins)


ALL = ("dp", "ctx", "ty", "tc")


def shards(
    inputs, memory, cotangent, wq_self, wk_self, wv_self, wo_self, wq_cross, wk_cross, wv_cross,
    wo_cross, w_in, w_out, gains, shifts, ffn_bias,
):
    seqs, block, d = inputs.shape
    n_dp, n_ctx, n_y, n_c = (lax.axis_size(a) for a in ALL)
    dc, pairs = n_dp * n_ctx, n_y * n_c
    half = block // n_c
    y_rank, c_rank = lax.axis_index("ty"), lax.axis_index("tc")
    own = n_ctx * half
    swap = [(i, i ^ 1) for i in range(n_c)]

    def mine(array):
        part = lax.dynamic_slice(array, (y_rank * n_ctx, c_rank * half, 0), (n_ctx, half, d))
        return lax.all_to_all(part, "ctx", 0, 0, tiled=True).reshape(own, d)

    def peer(array):
        return lax.ppermute(array, "tc", swap)

    def gather(array):
        got = lax.all_gather(array, ALL, axis=0, tiled=False)
        return got.reshape(dc, pairs, *array.shape)

    prows = wq_self.shape[0]
    vec_local = jnp.concatenate([gains.reshape(-1), shifts.reshape(-1), ffn_bias.reshape(-1)])
    used = vec_local.shape[0]
    vec_rows = -(-used // (8 * PAIR)) * 8
    vec_pack = jnp.pad(vec_local, (0, vec_rows * PAIR - used)).reshape(vec_rows, PAIR)
    first = jnp.concatenate([wq_self, wk_self, wv_self, wo_self.T, vec_pack], axis=0)
    got = gather(first)
    w_self = got[:, :, : 4 * prows].reshape(dc, pairs, 4, prows, PAIR)
    vec_all = got[:, :, 4 * prows :].reshape(dc * pairs, -1)[:, :used].astype(F32)
    lanes = gains.shape[1]
    cut = 13 * lanes
    vec = vec_all[:, :cut].reshape(-1, 13, lanes).transpose(1, 0, 2).reshape(13, d)
    vec = jnp.pad(vec, ((0, 3), (0, 0)))
    bias = vec_all[:, cut:].reshape(pairs, 1, -1)
    w_cross = gather(jnp.stack([wq_cross, wk_cross, wv_cross, wo_cross.T]))
    w_ffn = gather(jnp.stack([w_in, w_out.T]))

    xo = mine(inputs)
    xp = peer(xo)
    mo = mine(memory)
    mp = peer(mo)
    cot = mine(cotangent)

    *saved_self, n1, r1 = run_attn_fwd(True, (xo, xp), w_self, vec)
    *saved_cross, n2, r2 = run_attn_fwd(False, (n1, mo, mp), w_cross, vec)
    out, g_in, g_out, dz2, vg_ffn, bg = run_ffn(n2, r2, cot, w_ffn, bias, vec)
    gqc, goc, ownc, peerc, dz1, vg_cross, qgc = run_attn_bwd(
        False, mo, dz2, w_cross, vec, saved_cross, n1, r1
    )
    gotc = peer(peerc)
    gqs, gos, owns, peers, base, _, qgs = run_attn_bwd(
        True, xo, dz1, w_self, vec, saved_self, n1, r1
    )
    gots = peer(peers)
    gmem, gkc, gvc, vgc = run_kv_back("mem_back", mo, ownc, gotc, w_cross, None)
    gx, gks, gvs, vgs = run_kv_back("in_back", xo, owns, gots, w_self, base)

    def home(array, dtype):
        part = lax.all_to_all(array.reshape(n_ctx, half, d), "ctx", 0, 0, tiled=True)
        every = lax.all_gather(part, ("ty", "tc"), axis=0, tiled=False)
        every = every.reshape(n_y, n_c, n_ctx, half, d).transpose(0, 2, 1, 3, 4)
        return every.reshape(seqs, block, d).astype(dtype)

    def scatter(array):
        return lax.psum_scatter(
            array.reshape(dc * pairs, *array.shape[2:]), ALL, scatter_dimension=0, tiled=False
        )

    ffn_sum = scatter(jnp.stack([g_in, g_out], axis=2)).astype(F32)

    def line(a):
        return a.reshape(1, -1)

    vec_grads = jnp.concatenate(
        [
            vg_cross[0:1], vg_ffn[3:4], vg_ffn[0:1],
            line(qgs), line(vgs), vg_cross[2:3], vg_cross[1:2], line(qgc), line(vgc),
            vg_ffn[5:6], vg_ffn[4:5], vg_ffn[2:3], vg_ffn[1:2],
        ],
        axis=0,
    )
    vec_grads = vec_grads.reshape(13, dc * pairs, lanes).transpose(1, 0, 2).reshape(dc * pairs, cut)
    vec_grads = jnp.concatenate([vec_grads, bg.reshape(dc * pairs, -1)], axis=1)
    vec_grads = jnp.pad(vec_grads, ((0, 0), (0, vec_rows * PAIR - used)))
    vec_grads = vec_grads.reshape(dc, pairs, vec_rows, PAIR).astype(BF)
    rest = jnp.concatenate([gqs, gks, gvs, gos, gqc, gkc, gvc, goc, vec_grads], axis=2)
    rest = scatter(rest).astype(F32)
    mats = [rest[i * prows : (i + 1) * prows] for i in range(8)]
    vec_mine = rest[8 * prows :].reshape(-1)[:used]
    n_gain, n_shift = gains.size, shifts.size
    return (
        home(out, BF),
        home(gx, F32),
        home(gmem, F32),
        mats[0],
        mats[1],
        mats[2],
        mats[3].T,
        mats[4],
        mats[5],
        mats[6],
        mats[7].T,
        ffn_sum[0],
        ffn_sum[1].T,
        vec_mine[:n_gain].reshape(gains.shape),
        vec_mine[n_gain : n_gain + n_shift].reshape(shifts.shape),
        vec_mine[n_gain + n_shift :],
    )


def solution(mesh):
    sizes = mesh.devices.shape
    inner = jax.sharding.Mesh(
        mesh.devices.reshape(sizes[0], sizes[1], sizes[2] // 2, 2), ALL
    )
    rows = P("dp", "ctx", None)
    tp = ("ty", "tc")
    col = P(("dp", "ctx"), tp)
    row = P(tp, ("dp", "ctx"))
    small = P(None, ALL)
    weights = (col, col, col, row, col, col, col, row, col, row)
    tail = (small, small, P(ALL))
    return jax.shard_map(
        shards,
        mesh=inner,
        in_specs=(rows, rows, rows) + weights + tail,
        out_specs=(rows, rows, rows) + weights + tail,
        check_vma=False,
    )
```

```python
import functools

import jax
import jax.numpy as jnp
from jax import lax
from jax.experimental import pallas as pl
from jax.experimental.pallas import tpu as pltpu
from jax.sharding import PartitionSpec as P

HD = 64
EPS = 1e-05
BF = jnp.bfloat16
F32 = jnp.float32
PAIR = 2 * HD
VMEM_LIMIT = 40 << 20
SMALL_LIMIT = 16 << 20
GELU_C = 0.7978845608028654
GELU_A = 0.044715


def nn(left, right):
    return lax.dot_general(left, right, (((1,), (0,)), ((), ())), preferred_element_type=F32)


def nt(left, right):
    return lax.dot_general(left, right, (((1,), (1,)), ((), ())), preferred_element_type=F32)


def norm_stats(z):
    mean = jnp.mean(z, axis=-1, keepdims=True)
    cent = z - mean
    var = jnp.mean(cent * cent, axis=-1, keepdims=True)
    inv = lax.rsqrt(var + EPS)
    return cent * inv, inv


def norm_back(grad, gain, normed, inv):
    e = grad * gain
    me = jnp.mean(e, axis=-1, keepdims=True)
    men = jnp.mean(e * normed, axis=-1, keepdims=True)
    return inv * (e - me - normed * men)


def rows_sum(a):
    return jnp.sum(a, axis=0, keepdims=True)


def split_pair(block):
    lane = lax.broadcasted_iota(jnp.int32, block.shape, 1)
    zero = jnp.zeros_like(block)
    return jnp.concatenate(
        [jnp.where(lane < HD, block, zero), jnp.where(lane < HD, zero, block)], axis=0
    )


def join_pair(both):
    q = both.shape[1] // 2
    row = lax.broadcasted_iota(jnp.int32, (both.shape[0], q), 0)
    return jnp.where(row < HD, both[:, :q], both[:, q:])


def vrow(vec_ref, row):
    return jnp.concatenate([vec_ref[j, row : row + 1] for j in range(vec_ref.shape[0])], axis=1)


def pick(own_ref, peer_ref, mat, odd):
    shape = own_ref.shape
    own = own_ref[0, mat].reshape(shape[2] * shape[3], shape[4])
    other = peer_ref[0, mat].reshape(shape[2] * shape[3], shape[4])
    return jnp.where(odd, other, own)


def put_pieces(ref, at, first, value, ranks_ref):
    n_x, n_z = ref.shape[1], ref.shape[2]
    rows = value.shape[0] // (n_x * n_z)
    for d in range(n_x):
        for z in range(n_z):
            i = d * n_z + z
            ref[at, d ^ ranks_ref[0], z ^ ranks_ref[1], first : first + rows] = value[
                i * rows : (i + 1) * rows
            ]


def attn_fwd_body(
    causal, q_rows, kv_parts, w, biases,
    q_ref, k_ref, v_ref, p_refs, ot_ref, o_ref, il_ref, acc_ref,
):
    wq, wk, wv, wo = w
    kv = nn(kv_parts, jnp.concatenate([wk, wv], axis=1))
    k = kv[:, :PAIR].astype(BF)
    v = (kv[:, PAIR:] + biases[1]).astype(BF)
    q = (nn(q_rows, wq) + biases[0]).astype(BF) * HD ** (-0.5)
    q_ref[0] = q
    k_ref[0] = k
    v_ref[0] = v
    vt = v.T
    blocks = len(p_refs)
    rows = q.shape[0] // blocks
    keys = k.shape[0]
    for b in range(blocks):
        n = keys // blocks * (b + 1) if causal else keys
        s = nt(k[:n], split_pair(q[b * rows : (b + 1) * rows]))
        top = jnp.max(s, axis=0, keepdims=True)
        p = jnp.exp(s - top)
        inv = 1.0 / jnp.sum(p, axis=0, keepdims=True)
        pb = p.astype(BF)
        p_refs[b][0] = pb
        ot = join_pair(nn(vt[:, :n], pb) * inv)
        span = slice(b * rows, (b + 1) * rows)
        ot_ref[0, :, span] = ot.astype(BF)
        o_ref[0, span, :] = ot.T.astype(BF)
        il_ref[0, 0:1, span] = inv[:, :rows]
        il_ref[0, 1:2, span] = inv[:, rows:]
    acc_ref[...] += nt(o_ref[0], wo)


def self_fwd(ranks_ref, xo_ref, xp_ref, wa_ref, wb_ref, va_ref, vb_ref,
             q_ref, k_ref, v_ref, p0, p1, p2, p3, ot_ref, o_ref, il_ref,
             n_ref, r_ref, vec_ref, bias_ref, x_all, acc_ref):
    s = pl.program_id(0)
    blocks = 4
    half = xo_ref.shape[0] // blocks
    tiles = vec_ref.shape[0]

    @pl.when(s == 0)
    def _():
        for b in range(blocks):
            x_all[2 * b * half : (2 * b + 1) * half] = xo_ref[b * half : (b + 1) * half]
            x_all[(2 * b + 1) * half : (2 * b + 2) * half] = xp_ref[b * half : (b + 1) * half]
        both = va_ref[...].astype(F32) + vb_ref[...].astype(F32)
        vec_ref[...] = both[:tiles]
        bias_ref[...] = both[tiles]
        acc_ref[...] = xo_ref[...].astype(F32) + vrow(vec_ref, 5)

    odd = s % 2 == 1
    w = [pick(wa_ref, wb_ref, i, odd) for i in range(4)]
    t = s ^ ranks_ref[4]
    attn_fwd_body(True, xo_ref[...], x_all[...], w, (vec_ref[t, 3:4], vec_ref[t, 4:5]),
                  q_ref, k_ref, v_ref, (p0, p1, p2, p3), ot_ref, o_ref, il_ref, acc_ref)

    @pl.when(s == pl.num_programs(0) - 1)
    def _():
        normed, inv = norm_stats(acc_ref[...])
        n_ref[...] = normed
        r_ref[...] = jnp.broadcast_to(inv, r_ref.shape)


def cross_fwd(ranks_ref, n1_ref, mo_ref, mp_ref, wa_ref, wb_ref, vec_ref,
              q_ref, k_ref, v_ref, p0, p1, p2, p3, ot_ref, o_ref, il_ref,
              n_ref, r_ref, m_all, h_low, acc_ref):
    s = pl.program_id(0)
    half = mo_ref.shape[0]

    @pl.when(s == 0)
    def _():
        m_all[:half] = mo_ref[...]
        m_all[half:] = mp_ref[...]
        h1 = n1_ref[...] * vrow(vec_ref, 0) + vrow(vec_ref, 6)
        h_low[...] = h1.astype(BF)
        acc_ref[...] = h1 + vrow(vec_ref, 9)

    odd = s % 2 == 1
    w = [pick(wa_ref, wb_ref, i, odd) for i in range(4)]
    t = s ^ ranks_ref[4]
    attn_fwd_body(False, h_low[...], m_all[...], w, (vec_ref[t, 7:8], vec_ref[t, 8:9]),
                  q_ref, k_ref, v_ref, (p0, p1, p2, p3), ot_ref, o_ref, il_ref, acc_ref)

    @pl.when(s == pl.num_programs(0) - 1)
    def _():
        normed, inv = norm_stats(acc_ref[...])
        n_ref[...] = normed
        r_ref[...] = jnp.broadcast_to(inv, r_ref.shape)


def ffn_both(ranks_ref, n2_ref, r2_ref, cot_ref, w_ref, bias_ref, vec_ref,
             h0, h1, h2, h3, keep_ref, send_ref, dz2_ref, vg_ref, bg_ref,
             h_low, h_t, act, slope, acc, dz3_low, dz3_t, dh2):
    phase = pl.program_id(0)
    t = pl.program_id(1)
    d = n2_ref.shape[1]
    last = pl.num_programs(1) - 1
    w_in = w_ref[:, 0, 0].reshape(d, -1)
    w_out = w_ref[:, 0, 1].reshape(d, -1)
    hid = w_in.shape[1]
    strips = hid // PAIR

    @pl.when((phase == 0) & (t == 0))
    def _():
        h = n2_ref[...] * vrow(vec_ref, 1) + vrow(vec_ref, 10)
        h_low[...] = h.astype(BF)
        h_t[...] = h.astype(BF).T
        acc[...] = h + vrow(vec_ref, 11)

    @pl.when(phase == 0)
    def _():
        bias = jnp.concatenate(
            [bias_ref[pl.ds(t * strips + j, 1), :] for j in range(strips)], axis=1
        )
        u = nn(h_low[...], w_in) + bias
        cube = GELU_A * u * u
        th = jnp.tanh(GELU_C * u * (1.0 + cube))
        low = 0.5 * (1.0 + th)
        f = (u * low).astype(BF)
        act[t] = f
        slope[t] = low + 0.5 * u * (1.0 - th * th) * (GELU_C * (1.0 + 3.0 * cube))
        acc[...] += nt(f, w_out)

    @pl.when((phase == 0) & (t == last))
    def _():
        n3, r3 = norm_stats(acc[...])
        acc[...] = n3 * vrow(vec_ref, 2) + vrow(vec_ref, 12)
        put_home(acc, (h0, h1, h2, h3), ranks_ref)
        g = cot_ref[...].astype(F32)
        vg_ref[0:1] = rows_sum(g * n3)
        vg_ref[1:2] = rows_sum(g)
        dz3 = norm_back(g, vrow(vec_ref, 2), n3, r3)
        vg_ref[2:3] = rows_sum(dz3)
        low = dz3.astype(BF)
        dz3_low[...] = low
        dz3_t[...] = low.T
        dh2[...] = dz3

    @pl.when(phase == 1)
    def _():
        f = act[t]
        df = nn(dz3_low[...], w_out).astype(BF).astype(F32)
        du = (df * slope[t]).astype(BF)
        g_out = nn(dz3_t[...], f).astype(BF)
        g_in = nn(h_t[...], du).astype(BF)
        sums = rows_sum(du.astype(F32))
        for j in range(strips):
            bg_ref[pl.ds(t * strips + j, 1), :] = sums[:, j * PAIR : (j + 1) * PAIR]
        dh2[...] += nt(du, w_in)
        mine = t % 2 == ranks_ref[3]
        shape = keep_ref.shape[:1] + keep_ref.shape[3:]

        @pl.when(mine)
        def _():
            keep_ref[:, 0, 0] = g_in.reshape(shape)
            keep_ref[:, 0, 1] = g_out.reshape(shape)

        @pl.when(jnp.logical_not(mine))
        def _():
            send_ref[:, 0, 0] = g_in.reshape(shape)
            send_ref[:, 0, 1] = g_out.reshape(shape)

    @pl.when((phase == 1) & (t == last))
    def _():
        g = dh2[...]
        n2 = n2_ref[...]
        vg_ref[3:4] = rows_sum(g * n2)
        vg_ref[4:5] = rows_sum(g)
        dz2 = norm_back(g, vrow(vec_ref, 1), n2, r2_ref[:, 0:1])
        vg_ref[5:6] = rows_sum(dz2)
        vg_ref[6:8] = jnp.zeros_like(vg_ref[6:8])
        dz2_ref[...] = dz2


def put_home(acc, refs, ranks_ref):
    rows = refs[0].shape[0]
    for r, ref in enumerate(refs):
        at = pl.multiple_of((r ^ ranks_ref[1]) * rows, rows)
        ref[...] = acc[pl.ds(at, rows), :].astype(BF)


def attn_bwd(causal, ranks_ref, act_ref, dz_ref, wa_ref, wb_ref, vec_ref,
             q_ref, k_ref, v_ref, p0, p1, p2, p3, ot_ref, o_ref, il_ref, n_ref, r_ref,
             keep_ref, send_ref, own_ref, peer_ref, out_ref, vg_ref, qg_ref,
             dy, dy_t, act_t, acc, dk_ref, dv_ref):
    s = pl.program_id(0)
    p_refs = (p0, p1, p2, p3)
    blocks = len(p_refs)
    odd = s % 2 == 1
    wq = pick(wa_ref, wb_ref, 0, odd)
    wo = pick(wa_ref, wb_ref, 3, odd)

    @pl.when(s == 0)
    def _():
        dz = dz_ref[...]
        low = dz.astype(BF)
        dy[...] = low
        dy_t[...] = low.T
        acc[...] = dz
        if causal:
            act_t[...] = act_ref[...].T
        else:
            h = n_ref[...] * vrow(vec_ref, 0) + vrow(vec_ref, 6)
            act_t[...] = h.astype(BF).T

    q = q_ref[0]
    k = k_ref[0]
    v = v_ref[0]
    keys = k.shape[0]
    rows = q.shape[0] // blocks
    do = nn(dy[...], wo).astype(BF)
    g_o = nn(dy_t[...], o_ref[0]).astype(BF)
    do_t = do.T.astype(F32)
    prod = do_t * ot_ref[0].astype(F32)
    inv_a, inv_b = il_ref[0, 0:1], il_ref[0, 1:2]
    inner_a = jnp.sum(prod[:HD], axis=0, keepdims=True) * inv_a
    inner_b = jnp.sum(prod[HD:], axis=0, keepdims=True) * inv_b
    row = lax.broadcasted_iota(jnp.int32, do_t.shape, 0)
    dos = (do_t * jnp.where(row < HD, inv_a, inv_b)).astype(BF).T
    kt = k.T
    dqs = [None] * blocks
    for b in reversed(range(blocks)):
        n = keys // blocks * (b + 1) if causal else keys
        span = slice(b * rows, (b + 1) * rows)
        dob = split_pair(dos[span])
        qb = split_pair(q[span])
        pb = p_refs[b][0]
        dp = nt(v[:n], dob)
        inner = jnp.concatenate([inner_a[:, span], inner_b[:, span]], axis=1)
        ds = (pb.astype(F32) * (dp - inner)).astype(BF)
        dv = nn(pb, dob)
        dk = nn(ds, qb)
        if b == blocks - 1:
            dv_ref[...] = dv
            dk_ref[...] = dk
        else:
            dv_ref[:n] += dv
            dk_ref[:n] += dk
        dqs[b] = (join_pair(nn(kt[:, :n], ds)) * HD ** (-0.5)).T.astype(BF)
    dq = jnp.concatenate(dqs, axis=0)
    g_q = nn(act_t[...], dq).astype(BF)
    piece = keep_ref.shape[3] // 2

    @pl.when(jnp.logical_not(odd))
    def _():
        put_pieces(keep_ref, 0, 0, g_q, ranks_ref)
        put_pieces(keep_ref, 0, piece, g_o, ranks_ref)

    @pl.when(odd)
    def _():
        put_pieces(send_ref, 0, 0, g_q, ranks_ref)
        put_pieces(send_ref, 0, piece, g_o, ranks_ref)

    qg_ref[0] = rows_sum(dq.astype(F32))
    acc[...] += nt(dq, wq)
    for i, ref in enumerate((dk_ref, dv_ref)):
        if causal:
            for b in range(blocks):
                at = 2 * b * rows
                own_ref[i, 0, b * rows : (b + 1) * rows] = ref[at : at + rows]
                peer_ref[i, 0, b * rows : (b + 1) * rows] = ref[at + rows : at + 2 * rows].astype(BF)
        else:
            own_ref[i, 0] = ref[: keys // 2]
            peer_ref[i, 0] = ref[keys // 2 :].astype(BF)

    @pl.when(s == pl.num_programs(0) - 1)
    def _():
        g = acc[...]
        if causal:
            out_ref[...] = g
            vg_ref[...] = jnp.zeros_like(vg_ref)
        else:
            normed = n_ref[...]
            vg_ref[0:1] = rows_sum(g * normed)
            vg_ref[1:2] = rows_sum(g)
            dz1 = norm_back(g, vrow(vec_ref, 0), normed, r_ref[:, 0:1])
            vg_ref[2:3] = rows_sum(dz1)
            vg_ref[3:8] = jnp.zeros_like(vg_ref[3:8])
            out_ref[...] = dz1


def kv_back(final, lanes, blen, ranks_ref, act_ref, own_ref, got_ref, wa_ref, wb_ref, *rest):
    if final:
        (base_ref, vgc_ref, vgf_ref, bg_ref, qgs_ref, qgc_ref, vg_mem_ref,
         h0, h1, h2, h3, keep_ref, send_ref, act_t, acc, vg_self, tiles) = rest
    else:
        h0, h1, h2, h3, keep_ref, send_ref, vgrad_ref, act_t, acc = rest
    s = pl.program_id(0)
    odd = s % 2 == 1
    wk = pick(wa_ref, wb_ref, 1, odd)
    wv = pick(wa_ref, wb_ref, 2, odd)

    @pl.when(s == 0)
    def _():
        act_t[...] = act_ref[...].T
        if final:
            acc[...] = base_ref[...]
        else:
            acc[...] = jnp.zeros_like(acc)

    dk = (own_ref[0, 0] + got_ref[0, 0].astype(F32)).astype(BF)
    dv = (own_ref[1, 0] + got_ref[1, 0].astype(F32)).astype(BF)
    dkv = jnp.concatenate([dk, dv], axis=1)
    gkv = nn(act_t[...], dkv).astype(BF)
    piece = gkv.shape[0] // (keep_ref.shape[1] * keep_ref.shape[2])
    at = s // 2 if final else 0

    @pl.when(jnp.logical_not(odd))
    def _():
        put_pieces(keep_ref, at, 0, gkv[:, :PAIR], ranks_ref)
        put_pieces(keep_ref, at, piece, gkv[:, PAIR:], ranks_ref)

    @pl.when(odd)
    def _():
        put_pieces(send_ref, at, 0, gkv[:, :PAIR], ranks_ref)
        put_pieces(send_ref, at, piece, gkv[:, PAIR:], ranks_ref)

    sums = rows_sum(dv.astype(F32))
    acc[...] += nt(dkv, jnp.concatenate([wk, wv], axis=1))
    if not final:
        vgrad_ref[0] = sums
    else:
        vg_self[s] = sums
        pairs = vg_self.shape[0]

        @pl.when(s == 0)
        def _():
            for j in range(pairs):
                at = slice(j * PAIR, (j + 1) * PAIR)
                rel = j ^ ranks_ref[4]
                tiles[j, 0:1] = vgc_ref[0:1, at]
                tiles[j, 1:2] = vgf_ref[3:4, at]
                tiles[j, 2:3] = vgf_ref[0:1, at]
                tiles[j, 3:4] = qgs_ref[rel]
                tiles[j, 5:6] = vgc_ref[2:3, at]
                tiles[j, 6:7] = vgc_ref[1:2, at]
                tiles[j, 7:8] = qgc_ref[rel]
                tiles[j, 8:9] = vg_mem_ref[rel]
                tiles[j, 9:10] = vgf_ref[5:6, at]
                tiles[j, 10:11] = vgf_ref[4:5, at]
                tiles[j, 11:12] = vgf_ref[2:3, at]
                tiles[j, 12:13] = vgf_ref[1:2, at]
                tiles[j, 13:16] = jnp.zeros((3, PAIR), F32)

        tiles[s ^ ranks_ref[4], 4:5] = sums
        rows_at = lax.broadcasted_iota(jnp.int32, (16, PAIR), 0)
        n_x, n_z = keep_ref.shape[1], keep_ref.shape[2]

        @pl.when(s == pairs - 1)
        def _():
            for ry in range(2):
                for rc, ref in enumerate((keep_ref, send_ref)):
                    for i in range(n_x):
                        for k in range(n_z):
                            dc = (i ^ ranks_ref[0]) * n_z + (k ^ ranks_ref[1])
                            p = dc * pairs + ((2 * ry + rc) ^ ranks_ref[4])
                            tile = tiles[lax.div(p * lanes, PAIR)]
                            bias = bg_ref[pl.ds(lax.div(p * blen, PAIR), 1), :]
                            both = jnp.where(rows_at == 13, bias, tile).astype(BF)
                            ref[ry, i, k, 2 * piece : 2 * piece + 16] = both

    @pl.when(s == pl.num_programs(0) - 1)
    def _():
        put_home(acc, (h0, h1, h2, h3), ranks_ref)


def pack_rows(*refs):
    ins, outs = refs[1 : 1 + len(refs) // 2], refs[1 + len(refs) // 2 :]
    for ref, out in zip(ins, outs):
        out[...] = ref[0]


def pack_pairs(*refs):
    m_refs, c_refs, outs = refs[1:5], refs[5:9], refs[9:13]
    for m, c, out in zip(m_refs, c_refs, outs):
        out[0] = m[0]
        out[1] = c[0]


def pack_weights(lanes, blen, ranks_ref, wqs, wks, wvs, wos, wqc, wkc, wvc, woc, win, wout,
                 gains, shifts, bias, s_ref, c_ref, f_ref, va, vb):
    n = wqs.shape[0]
    for i, ref in enumerate((wqs, wks, wvs, wos)):
        s_ref[i * n : (i + 1) * n] = ref[...]
    for i, ref in enumerate((wqc, wkc, wvc, woc)):
        c_ref[i * n : (i + 1) * n] = ref[...]
    p = (ranks_ref[0] * 4 + ranks_ref[1]) * 4 + ranks_ref[4]
    at = 4 * n
    va[...] = jnp.zeros_like(va)
    va[0:3, 0:lanes] = gains[...].astype(F32)
    va[3:13, 0:lanes] = shifts[...].astype(F32)
    s_ref[at : at + 16] = pltpu.roll(va[...], lax.rem(p * lanes, PAIR), 1).astype(BF)
    vb[...] = jnp.zeros_like(vb)
    vb[pl.ds(lax.div(p * blen, PAIR), 1), 0:blen] = bias[...].astype(F32)
    s_ref[at + 16 : at + 32] = pltpu.roll(vb[...], lax.rem(p * blen, PAIR), 1).astype(BF)
    f_ref[0] = win[...]
    f_ref[1] = wout[...]


def whole(a):
    return pl.BlockSpec(a.shape, lambda *_: (0,) * len(a.shape))


def without(body, at, count):
    return lambda *refs: body(*refs[:at], *refs[at + count :])


def launch(body, name, grid, ranks, ins, outs, scratch=(), deps=(), limit=VMEM_LIMIT, cost=(0, 0, 0)):
    first = 0 if ranks is None else 1
    deps = list(deps)
    if deps:
        body = without(body, first + len(ins), len(deps))
    call = pl.pallas_call(
        body,
        grid_spec=pltpu.PrefetchScalarGridSpec(
            num_scalar_prefetch=first,
            grid=grid,
            in_specs=[i[1] for i in ins] + [pl.BlockSpec(memory_space=pl.ANY)] * len(deps),
            out_specs=tuple(o[1] for o in outs),
            scratch_shapes=list(scratch),
        ),
        out_shape=tuple(
            pltpu.HBM(o[0].shape, o[0].dtype) if len(o) > 2 else o[0] for o in outs
        ),
        compiler_params=pltpu.CompilerParams(
            vmem_limit_bytes=limit, dimension_semantics=("arbitrary",) * len(grid)
        ),
        cost_estimate=pl.CostEstimate(
            flops=cost[0], bytes_accessed=cost[1], transcendentals=cost[2]
        ),
        name=name,
    )
    args = [
        pltpu.with_memory_space_constraint(i[0], pltpu.HBM) if len(i) > 2 else i[0] for i in ins
    ] + deps
    return call(*args) if ranks is None else call(ranks, *args)


def local(body, name, outs, *ins, ranks=None, scratch=(), in_specs=None, deps=()):
    specs = in_specs or [whole(a) for a in ins]
    size = sum(o.size * o.dtype.itemsize for o in outs)
    return launch(
        body, name, (1,), ranks, list(zip(ins, specs)), [(o, whole(o)) for o in outs],
        scratch, deps, SMALL_LIMIT, (size, 2 * size, 0),
    )


def struct(shape, dtype):
    return jax.ShapeDtypeStruct(shape, dtype)


def restack(ins, outs, cuts):
    for out, (lo, hi) in zip(outs, cuts):
        for r, ref in enumerate(ins):
            out[0, 0, r] = ref[lo:hi]


def double(own, got, out, axis):
    m = own.shape[axis]
    if axis == 0:
        out[:m] = own[...]
        out[m:] = got[...]
    else:
        out[:, :m] = own[...]
        out[:, m:] = got[...]


def order(ranks_ref, parts, outs):
    for r, ref in enumerate(parts):
        rows = ref.shape[-2]
        at = pl.multiple_of((r ^ ranks_ref[1]) * rows, rows)
        for i, out in enumerate(outs):
            out[pl.ds(at, rows), :] = ref[...] if len(outs) == 1 else ref[i]


def assemble(lanes, ranks_ref, a0, a1, b0, b1, w_ref, v_ref=None, scr=None):
    pairs = 4
    n_x, n_z = a0.shape[1], a0.shape[2]
    prows = w_ref.shape[3]
    if v_ref is not None:
        scr[...] = jnp.zeros_like(scr)
    for ry in range(2):
        a_ref = (a0, a1)[ry]
        for i in range(n_x):
            for k in range(n_z):
                dc = (i ^ ranks_ref[0]) * n_z + (k ^ ranks_ref[1])
                b_ref, bi = (b0, i) if i < n_x // 2 else (b1, i - n_x // 2)
                for m in range(2):
                    span = slice(m * prows, (m + 1) * prows)
                    w_ref[ry, m, dc] = a_ref[0, i, k, span]
                    w_ref[ry, 2 + m, dc] = b_ref[ry, bi, k, span]
                if v_ref is not None:
                    at = 2 * prows
                    p = dc * pairs + ((2 * ry) ^ ranks_ref[4])
                    tile = lax.div(p * lanes, PAIR)
                    scr[tile] += b_ref[ry, bi, k, at : at + 16].astype(F32)
                    scr[pairs] += b_ref[ry, bi, k, at + 16 : at + 32].astype(F32)
    if v_ref is not None:
        v_ref[...] = scr[...].astype(BF)


def start_one(cuts, ranks_ref, *refs):
    restack(refs[0:4], refs[8:10], cuts)
    order(ranks_ref, refs[4:8], refs[10:11])


def start_two(axes, cuts, a, ga, b, gb, *refs):
    double(a, ga, refs[4], axes[0])
    double(b, gb, refs[5], axes[1])
    restack(refs[0:4], refs[6:8], cuts)


def double_both(axes, a, ga, b, gb, out_a, out_b):
    double(a, ga, out_a, axes[0])
    double(b, gb, out_b, axes[1])


def start_five(lanes, ranks_ref, *refs):
    assemble(lanes, ranks_ref, *refs[0:4], refs[8])
    order(ranks_ref, refs[4:8], refs[9:11])


def order_home(ranks_ref, *refs):
    order(ranks_ref, refs[:4], refs[4:])


def add_body(keep, got, out):
    out[...] = (keep[...].astype(F32) + got[...].astype(F32)).astype(BF)


def halve_body(axis_a, axis_b, cuts, *refs):
    n = len(cuts)
    ins, (sa, ka, sb, kb) = refs[: len(refs) - 4], refs[len(refs) - 4 :]

    def place(axis, send, keep, at, value):
        rows = value.shape[3]
        m = value.shape[axis] // 2
        lo = value[:m] if axis == 0 else value[:, :m]
        hi = value[m:] if axis == 0 else value[:, m:]
        keep[:, :, :, at : at + rows] = lo
        send[:, :, :, at : at + rows] = hi.astype(BF)

    at_a = at_b = 0
    for i, cut in enumerate(cuts):
        if cut is None:
            continue
        keep, got = ins[2 * i], ins[2 * i + 1]
        total = keep[...].astype(F32) + got[...].astype(F32)
        place(axis_a, sa, ka, at_a, total[:, :, :, :cut])
        place(axis_b, sb, kb, at_b, total[:, :, :, cut:])
        at_a += cut
        at_b += total.shape[3] - cut
    if cuts[0] is None:
        place(axis_a, sa, ka, 0, ins[0][...] + ins[1][...].astype(F32))
        place(axis_b, sb, kb, 0, ins[2][...] + ins[3][...].astype(F32))


def spread_body(ka, ra, kb, rb, s1, s2, s3, keep):
    rows = ka.shape[3]
    for r, ref in enumerate((keep, s1, s2, s3)):
        ref[:rows] = (ka[0, 0, r] + ra[0, 0, r].astype(F32)).astype(ref.dtype)
        ref[rows:] = (kb[0, 0, r] + rb[0, 0, r].astype(F32)).astype(ref.dtype)


def finish_body(plan, lanes, blen, ranks_ref, keep, r1, r2, r3, *outs):
    total = keep[...] + r1[...].astype(F32) + r2[...].astype(F32) + r3[...].astype(F32)
    at = 0
    outs = list(outs)
    for turn, rows in plan:
        part = total[at : at + rows]
        at += rows
        if turn == 2:
            p = (ranks_ref[0] * 4 + ranks_ref[1]) * 4 + ranks_ref[4]
            vec = pltpu.roll(part, lax.rem(PAIR - lax.rem(p * lanes, PAIR), PAIR), 1)
            outs.pop(0)[...] = vec[0:3, :lanes]
            outs.pop(0)[...] = vec[3:13, :lanes]
            own = pltpu.roll(part, lax.rem(PAIR - lax.rem(p * blen, PAIR), PAIR), 1)
            outs.pop(0)[...] = own[13:14, :blen]
        else:
            outs.pop(0)[...] = part


def home_body(ranks_ref, own, other, got_own, got_other, out_ref):
    y = pl.program_id(0)
    n_z, rows, _ = own.shape
    here = pl.multiple_of(ranks_ref[3] * rows, rows)
    there = pl.multiple_of((1 - ranks_ref[3]) * rows, rows)
    for same, a, b in ((True, own, got_own), (False, other, got_other)):
        @pl.when((y == ranks_ref[2]) == same)
        def _():
            for z in range(n_z):
                out_ref[z, pl.ds(here, rows), :] = a[z].astype(out_ref.dtype)
                out_ref[z, pl.ds(there, rows), :] = b[z].astype(out_ref.dtype)


def pair_spec(rows):
    return pl.BlockSpec((1, rows, PAIR), lambda s, _: (s, 0, 0))


def half_spec(w):
    return pl.BlockSpec((1,) + w.shape[1:], lambda s, _: (s // 2, 0, 0, 0, 0))


def slot_shape(n_x, n_z, rows):
    return struct((2, n_x, n_z, rows, PAIR), BF)


def slot_spec(n_x, n_z, rows):
    return pl.BlockSpec((1, n_x, n_z, rows, PAIR), lambda s, _: (s // 2, 0, 0, 0, 0))


def full(shape):
    return pl.BlockSpec(shape, lambda *_: (0,) * len(shape))


def run_attn_fwd(causal, ranks, rows_in, w_own, w_peer, vecs, pairs, deps):
    own, d = rows_in[0].shape
    keys = 2 * own
    blocks = 4
    ns = [keys // blocks * (b + 1) if causal else keys for b in range(blocks)]
    qn = 2 * own // blocks
    outs = [
        (struct((pairs, own, PAIR), BF), pair_spec(own), True),
        (struct((pairs, keys, PAIR), BF), pair_spec(keys), True),
        (struct((pairs, keys, PAIR), BF), pair_spec(keys), True),
        *[
            (struct((pairs, n, qn), BF), pl.BlockSpec((1, n, qn), lambda s, _: (s, 0, 0)), True)
            for n in ns
        ],
        (struct((pairs, PAIR, own), BF), pl.BlockSpec((1, PAIR, own), lambda s, _: (s, 0, 0)), True),
        (struct((pairs, own, PAIR), BF), pair_spec(own), True),
        (struct((pairs, 8, own), F32), pl.BlockSpec((1, 8, own), lambda s, _: (s, 0, 0)), True),
        (struct((own, d), F32), full((own, d))),
        (struct((own, PAIR), F32), full((own, PAIR))),
    ]
    if causal:
        outs.append((struct((pairs, 16, PAIR), F32), full((pairs, 16, PAIR))))
        outs.append((struct((16, PAIR), F32), full((16, PAIR))))
    scratch = [pltpu.VMEM((keys, d), BF)]
    if not causal:
        scratch.append(pltpu.VMEM((own, d), BF))
    scratch.append(pltpu.VMEM((own, d), F32))
    area = sum(ns) * qn
    ins = [(a, whole(a)) for a in rows_in] + [(w_own, half_spec(w_own)), (w_peer, half_spec(w_peer))]
    return launch(
        self_fwd if causal else cross_fwd,
        "self_fwd" if causal else "cross_fwd",
        (pairs,), ranks, ins + [(a, whole(a)) for a in vecs], outs, scratch, deps,
        cost=(
            2 * own * d * d * 6 + 4 * area * PAIR * pairs,
            2 * area * pairs + 8 * own * d,
            area * pairs,
        ),
    )


def run_ffn(ranks, n2, r2, cot, w, bias, vec):
    own, d = n2.shape
    dc, parts, _, prows, hid = w.shape
    half = own // 4
    back = lambda p, t, _: (0, p * (t // 2), 0, 0, 0)
    outs = [(struct((half, d), BF), full((half, d)))] * 4 + [
        (struct((dc, 2, 2, prows, hid), BF), pl.BlockSpec((dc, 1, 2, prows, hid), back)),
        (struct((dc, 2, 2, prows, hid), BF), pl.BlockSpec((dc, 1, 2, prows, hid), back)),
        (struct((own, d), F32), full((own, d))),
        (struct((8, d), F32), full((8, d))),
        (struct((16, PAIR), F32), full((16, PAIR))),
    ]
    ins = [
        (n2, whole(n2)),
        (r2, whole(r2)),
        (cot, whole(cot)),
        (w, pl.BlockSpec((dc, 1, 2, prows, hid), lambda p, t, _: (0, t, 0, 0, 0)), True),
        (bias, whole(bias)),
        (vec, whole(vec)),
    ]
    scratch = [
        pltpu.VMEM((own, d), BF),
        pltpu.VMEM((d, own), BF),
        pltpu.VMEM((parts, own, hid), BF),
        pltpu.VMEM((parts, own, hid), F32),
        pltpu.VMEM((own, d), F32),
        pltpu.VMEM((own, d), BF),
        pltpu.VMEM((d, own), BF),
        pltpu.VMEM((own, d), F32),
    ]
    return launch(
        ffn_both, "ffn_both", (2, parts), ranks, ins, outs, scratch,
        cost=(
            12 * own * d * hid * parts,
            4 * dc * parts * 2 * prows * hid + 20 * own * d,
            own * hid * parts,
        ),
    )


def run_attn_bwd(causal, ranks, act, dz, w_own, w_peer, vec, saved, n, r, n_x, n_z, deps):
    q, k, v, p0, p1, p2, p3, ot, o, il = saved
    pairs, own, _ = q.shape
    keys = k.shape[1]
    d = dz.shape[1]
    prows = w_own.shape[3]
    ps = (p0, p1, p2, p3)
    area = sum(p.shape[1] * p.shape[2] for p in ps)
    kv_spec = pl.BlockSpec((2, 1, own, PAIR), lambda s, _: (0, s, 0, 0))
    outs = [
        (slot_shape(n_x, n_z, 2 * prows), slot_spec(n_x, n_z, 2 * prows)),
        (slot_shape(n_x, n_z, 2 * prows), slot_spec(n_x, n_z, 2 * prows)),
        (struct((2, pairs, own, PAIR), F32), kv_spec),
        (struct((2, pairs, own, PAIR), BF), kv_spec),
        (struct((own, d), F32), full((own, d))),
        (struct((8, d), F32), full((8, d))),
        (struct((pairs, 1, PAIR), F32), pl.BlockSpec((1, 1, PAIR), lambda s, _: (s, 0, 0))),
    ]
    ins = [
        (act, whole(act)),
        (dz, whole(dz)),
        (w_own, half_spec(w_own)),
        (w_peer, half_spec(w_peer)),
        (vec, whole(vec)),
        (q, pair_spec(own), True),
        (k, pair_spec(keys), True),
        (v, pair_spec(keys), True),
        *[(p, pl.BlockSpec((1,) + p.shape[1:], lambda s, _: (s, 0, 0)), True) for p in ps],
        (ot, pl.BlockSpec((1, PAIR, own), lambda s, _: (s, 0, 0)), True),
        (o, pair_spec(own), True),
        (il, pl.BlockSpec((1, 8, own), lambda s, _: (s, 0, 0)), True),
        (n, whole(n)),
        (r, whole(r)),
    ]
    scratch = [
        pltpu.VMEM((own, d), BF),
        pltpu.VMEM((d, own), BF),
        pltpu.VMEM((d, own), BF),
        pltpu.VMEM((own, d), F32),
        pltpu.VMEM((keys, PAIR), F32),
        pltpu.VMEM((keys, PAIR), F32),
    ]
    return launch(
        functools.partial(attn_bwd, causal), "self_bwd" if causal else "cross_bwd",
        (pairs,), ranks, ins, outs, scratch, deps,
        cost=(
            2 * own * d * d * 4 + 8 * area * PAIR * pairs,
            2 * area * pairs + 16 * own * d,
            0,
        ),
    )


def run_kv_back(name, ranks, act, own_part, got, w_own, w_peer, extra, lanes, blen, n_x, n_z,
                deps):
    own, d = act.shape
    pairs = own_part.shape[1]
    prows = w_own.shape[3]
    final = bool(extra)
    rows = 2 * prows + (16 if final else 0)
    half = own // 4
    outs = [(struct((half, d), BF), full((half, d)))] * 4
    scratch = [pltpu.VMEM((d, own), BF), pltpu.VMEM((own, d), F32)]
    if final:
        outs += [(slot_shape(n_x, n_z, rows), full((2, n_x, n_z, rows, PAIR)))] * 2
        scratch += [pltpu.VMEM((pairs, 1, PAIR), F32), pltpu.VMEM((pairs, 16, PAIR), F32)]
    else:
        outs += [(slot_shape(n_x, n_z, rows), slot_spec(n_x, n_z, rows))] * 2
        outs.append(
            (struct((pairs, 1, PAIR), F32), pl.BlockSpec((1, 1, PAIR), lambda s, _: (s, 0, 0)))
        )
    ins = [
        (act, whole(act)),
        (own_part, pl.BlockSpec((2, 1, own, PAIR), lambda s, _: (0, s, 0, 0))),
        (got, pl.BlockSpec((2, 1, own, PAIR), lambda s, _: (0, s ^ 1, 0, 0))),
        (w_own, half_spec(w_own)),
        (w_peer, half_spec(w_peer)),
    ] + [(a, whole(a)) for a in extra]
    return launch(
        functools.partial(kv_back, final, lanes, blen), name, (pairs,), ranks, ins, outs,
        scratch, deps, cost=(8 * own * d * d, 20 * own * d, 0),
    )


ALL = ("dp", "ctx", "ty", "tc")


def shards(
    inputs, memory, cotangent, wq_self, wk_self, wv_self, wo_self, wq_cross, wk_cross, wv_cross,
    wo_cross, w_in, w_out, gains, shifts, ffn_bias,
):
    seqs, block, d = inputs.shape
    n_x, n_z, n_y, n_c = (lax.axis_size(a) for a in ALL)
    pairs = n_y * n_c
    half = block // n_c
    own = n_z * half
    x_rank, z_rank, y_rank, c_rank = (lax.axis_index(a) for a in ALL)
    ranks = jnp.stack([x_rank, z_rank, y_rank, c_rank, y_rank * n_c + c_rank]).astype(jnp.int32)
    prows, lanes, blen = wq_self.shape[0], gains.shape[1], ffn_bias.shape[0]
    hid = w_in.shape[1]
    x_bits = [1 << i for i in range((n_x - 1).bit_length())]

    def send(array, axis, bit):
        return lax.ppermute(array, axis, [(i, i ^ bit) for i in range(lax.axis_size(axis))])

    def rows_of(r):
        return pl.BlockSpec((1, half, d), lambda i, ref: (ref[2] * 4 + (ref[1] ^ r), ref[3], 0))

    def packed_rows(array, turns):
        return [(array, rows_of(r), True) for r in turns]

    def around_z(parts):
        return [parts[0]] + [send(parts[r], "ctx", r) for r in range(1, n_z)]

    row_part = struct((half, d), BF)
    pair_part = struct((2, half, d), BF)
    turns = range(n_z)
    xs = launch(
        pack_rows, "pack_rows", (1,), ranks, packed_rows(inputs, turns),
        [(row_part, whole(row_part))] * n_z, limit=SMALL_LIMIT,
    )
    x_got = around_z(xs)
    weights = (wq_self, wk_self, wv_self, wo_self.T, wq_cross, wk_cross, wv_cross, wo_cross.T,
               w_in, w_out.T, gains, shifts, ffn_bias.reshape(1, -1))
    s_pack, c_pack, f_pack = local(
        functools.partial(pack_weights, lanes, blen), "pack_weights",
        [struct((4 * prows + 32, PAIR), BF), struct((4 * prows, PAIR), BF),
         struct((2, prows, hid), BF)],
        *weights, ranks=ranks, deps=[xs[0]],
        scratch=[pltpu.VMEM((16, PAIR), F32), pltpu.VMEM((16, PAIR), F32)],
    )
    s_got = around_z([s_pack] * n_z)
    w_ffn = lax.all_gather(f_pack, ALL, axis=0, tiled=False).reshape(
        n_x * n_z, pairs, 2, prows, hid
    )
    cuts_s = ((0, 2 * prows), (2 * prows, 4 * prows + 32))
    cuts_c = ((0, 2 * prows), (2 * prows, 4 * prows))

    def z_slots(cuts):
        return [struct((1, 1, n_z, hi - lo, PAIR), BF) for lo, hi in cuts]

    def doubled(array, axis):
        shape = list(array.shape)
        shape[axis] *= 2
        return struct(tuple(shape), BF)

    steps_a = [("dp", bit) for bit in x_bits] + [("ty", 1)]
    steps_b = [("ty", 1)] + [("dp", bit) for bit in x_bits]
    axis_of = {"ty": 0, "dp": 1}
    axes_at = [(axis_of[sa[0]], axis_of[sb[0]]) for sa, sb in zip(steps_a, steps_b)]

    def step(i, a, b):
        return [a, send(a, *steps_a[i]), b, send(b, *steps_b[i])]

    def more(i, a, b):
        while i < len(steps_a) - 1:
            ga, gb = axes_at[i]
            a, b = local(
                functools.partial(double_both, axes_at[i]), "double",
                [doubled(a, ga), doubled(b, gb)], *step(i, a, b),
            )
            i += 1
        return a, b

    sa, sb, xo = local(
        functools.partial(start_one, cuts_s), "start_one",
        z_slots(cuts_s) + [struct((own, d), BF)], *s_got, *x_got, ranks=ranks,
    )
    xp = send(xo, "tc", 1)
    c_parts = around_z([c_pack] * n_z)
    sa, sb, ca, cb = local(
        functools.partial(start_two, axes_at[0], cuts_c), "start_two",
        [doubled(sa, axes_at[0][0]), doubled(sb, axes_at[0][1])] + z_slots(cuts_c),
        *step(0, sa, sb), *c_parts,
    )
    sa, sb = more(1, sa, sb)
    s_last = step(len(steps_a) - 1, sa, sb)
    mcs = launch(
        pack_pairs, "pack_pairs", (1,), ranks,
        packed_rows(memory, turns) + packed_rows(cotangent, turns),
        [(pair_part, whole(pair_part))] * n_z, deps=[sa], limit=SMALL_LIMIT,
    )
    mc_got = around_z(mcs)
    w_shape = struct((2, 4, n_x * n_z, prows, PAIR), BF)
    ws_own, v_own = local(
        functools.partial(assemble, lanes), "assemble",
        [w_shape, struct((pairs + 1, 16, PAIR), BF)], *s_last, ranks=ranks,
        scratch=[pltpu.VMEM((pairs + 1, 16, PAIR), F32)], deps=[mcs[0]],
    )
    ws_peer, v_peer = send(ws_own, "tc", 1), send(v_own, "tc", 1)
    ca, cb = more(0, ca, cb)
    c_last = step(len(steps_a) - 1, ca, cb)
    *saved_self, n1, r1, vec, bias = run_attn_fwd(
        True, ranks, (xo, xp), ws_own, ws_peer, (v_own, v_peer), pairs, [ca]
    )
    wc_own, mo, cot = local(
        functools.partial(start_five, lanes), "start_five",
        [w_shape, struct((own, d), BF), struct((own, d), BF)], *c_last, *mc_got,
        ranks=ranks, deps=[r1],
    )
    wc_peer = send(wc_own, "tc", 1)
    mp = send(mo, "tc", 1)
    *saved_cross, n2, r2 = run_attn_fwd(
        False, ranks, (n1, mo, mp), wc_own, wc_peer, (vec,), pairs, []
    )
    *out_rows, f_keep, f_send, dz2, vg_ffn, bg = run_ffn(ranks, n2, r2, cot, w_ffn, bias, vec)

    def home_rows(got, deps):
        (here,) = local(
            order_home, "order_home", [struct((own, d), BF)], *got, ranks=ranks, deps=deps
        )
        return here.reshape(n_z, half, d)

    def home_last(here, there, dtype, deps):
        ins = [here, there, send(here, "tc", 1), send(there, "tc", 1)]
        (result,) = launch(
            home_body, "home", (n_y,), ranks, [(a, whole(a)) for a in ins],
            [(struct((seqs, block, d), dtype),
              pl.BlockSpec((n_z, block, d), lambda y, _: (y, 0, 0)), True)],
            deps=deps, limit=2 * SMALL_LIMIT,
            cost=(seqs * block * d, 6 * seqs * block * d, 0),
        )
        return result

    back_a = [("ty", 1)] + [("dp", bit) for bit in reversed(x_bits)]
    back_b = [("dp", bit) for bit in reversed(x_bits)] + [("ty", 1)]

    def shape_at(i, rows, steps):
        shape = [2, n_x, n_z, rows, PAIR]
        for axis, _ in steps[: i + 1]:
            shape[axis_of[axis]] //= 2
        return tuple(shape)

    def halve(i, ins, cuts, rows, deps):
        shape_a, shape_b = shape_at(i, rows[0], back_a), shape_at(i, rows[1], back_b)
        to_a, keep_a, to_b, keep_b = local(
            functools.partial(
                halve_body, axis_of[back_a[i][0]], axis_of[back_b[i][0]], cuts
            ),
            "halve",
            [struct(shape_a, BF), struct(shape_a, F32), struct(shape_b, BF), struct(shape_b, F32)],
            *ins, deps=deps,
        )
        return [keep_a, send(to_a, *back_a[i]), keep_b, send(to_b, *back_b[i])]

    def halve_more(i, ins, rows, stop, deps):
        while i < stop:
            ins = halve(i, ins, (None,), rows, deps)
            i, deps = i + 1, []
        return ins

    def spread(ins, deps):
        rows = ins[0].shape[3] + ins[2].shape[3]
        *sends, keep = local(
            spread_body, "spread",
            [struct((rows, PAIR), BF)] * 3 + [struct((rows, PAIR), F32)], *ins, deps=deps,
        )
        return [keep] + [send(sends[r - 1], "ctx", r) for r in range(1, n_z)]

    def finish(ins, plan, extra, deps):
        outs = [struct((size, PAIR), F32) for turn, size in plan if turn != 2] + extra
        return local(
            functools.partial(finish_body, plan, lanes, blen), "finish", outs, *ins,
            ranks=ranks, deps=deps,
        )

    rounds = len(back_a)
    out_got = around_z(out_rows)
    f_shape = f_keep.shape
    f_block = pl.BlockSpec((f_shape[0] // 2,) + f_shape[1:], lambda i: (i, 0, 0, 0, 0))
    (f_sum,) = launch(
        add_body, "add", (2,), None,
        [(f_keep, f_block), (send(f_send, "tc", 1), f_block)], [(struct(f_shape, BF), f_block, True)],
        cost=(f_keep.size, 6 * f_keep.size, 0),
    )
    f_done = lax.psum_scatter(
        f_sum.reshape(-1, 2, prows, hid), ("dp", "ctx", "ty"), scatter_dimension=0, tiled=False
    ).astype(F32)
    c_keep, c_send, c_own, c_peer, dz1, vg_cross, qgc = run_attn_bwd(
        False, ranks, mo, dz2, wc_own, wc_peer, vec, saved_cross, n1, r1, n_x, n_z, [f_sum]
    )
    c_got, c_add = send(c_peer, "tc", 1), send(c_send, "tc", 1)
    out_here = home_rows(out_got, [dz1])
    out_there = send(out_here, "ty", 1)
    s_keep, s_send, s_own, s_peer, base, _, qgs = run_attn_bwd(
        True, ranks, xo, dz1, ws_own, ws_peer, vec, saved_self, n1, r1, n_x, n_z, [out_here]
    )
    s_got, s_add = send(s_peer, "tc", 1), send(s_send, "tc", 1)
    *mem_rows, m_keep, m_send, vgc = run_kv_back(
        "mem_back", ranks, mo, c_own, c_got, wc_own, wc_peer, (), lanes, blen, n_x, n_z, [base]
    )
    mem_got, m_add = around_z(mem_rows), send(m_send, "tc", 1)
    rows_one = (2 * prows, 2 * prows)
    rows_two = (2 * prows, 2 * prows + 16)
    one = halve(0, [c_keep, c_add, s_keep, s_add], (prows, prows), rows_one, [vgc])
    *in_rows, i_keep, i_send = run_kv_back(
        "in_back", ranks, xo, s_own, s_got, ws_own, ws_peer,
        (base, vg_cross, vg_ffn, bg, qgs, qgc, vgc), lanes, blen, n_x, n_z, [one[0]],
    )
    in_got, i_add = around_z(in_rows), send(i_send, "tc", 1)
    mem_here = home_rows(mem_got, [in_rows[0]])
    mem_there = send(mem_here, "ty", 1)
    one = halve_more(1, one, rows_one, rounds, [mem_here])
    two = halve(0, [m_keep, m_add, i_keep, i_add], (prows, prows), rows_two, [one[0]])
    one = spread(one, [two[0]])
    in_here = home_rows(in_got, [one[0]])
    in_there = send(in_here, "ty", 1)
    two = halve_more(1, two, rows_two, rounds, [in_here])
    out = home_last(out_here, out_there, BF, [two[0]])
    gqc, gqs, goc, gos = finish(one, ((0, prows),) * 4, [], [out])
    two = spread(two, [gqc])
    grad_memory = home_last(mem_here, mem_there, F32, [two[0]])
    grad_inputs = home_last(in_here, in_there, F32, [grad_memory])
    gkc, gks, gvc, gvs, g_gains, g_shifts, g_bias = finish(
        two, ((0, prows),) * 4 + ((2, 16),),
        [struct(gains.shape, F32), struct(shifts.shape, F32), struct((1, blen), F32)],
        [grad_inputs],
    )
    return (
        out, grad_inputs, grad_memory, gqs, gks, gvs, gos.T, gqc, gkc, gvc, goc.T,
        f_done[0], f_done[1].T, g_gains, g_shifts, g_bias.reshape(-1),
    )


def solution(mesh):
    sizes = mesh.devices.shape
    inner = jax.sharding.Mesh(
        mesh.devices.reshape(sizes[0], sizes[1], sizes[2] // 2, 2), ALL
    )
    rows = P("dp", "ctx", None)
    tp = ("ty", "tc")
    col = P(("dp", "ctx"), tp)
    row = P(tp, ("dp", "ctx"))
    small = P(None, ALL)
    weights = (col, col, col, row, col, col, col, row, col, row)
    tail = (small, small, P(ALL))
    return jax.shard_map(
        shards,
        mesh=inner,
        in_specs=(rows, rows, rows) + weights + tail,
        out_specs=(rows, rows, rows) + weights + tail,
        check_vma=False,
    )
```

```python
import functools

import jax
import jax.numpy as jnp
from jax import lax
from jax.experimental import pallas as pl
from jax.experimental.pallas import tpu as pltpu
from jax.sharding import PartitionSpec as P

HD = 64
EPS = 1e-05
BF = jnp.bfloat16
F32 = jnp.float32
PAIR = 2 * HD
VMEM_LIMIT = 40 << 20
SMALL_LIMIT = 16 << 20
SMALL_COST = 1_000_000_000
COVER = 10 * SMALL_COST
COSTS = dict(
    self_fwd=24_000_000_000, cross_fwd=28_000_000_000, ffn_both=25_000_000_000,
    cross_bwd=30_000_000_000, self_bwd=16_000_000_000, mem_back=9_000_000_000,
    in_back=9_000_000_000,
)
GELU_C = 0.7978845608028654
GELU_A = 0.044715


def nn(left, right):
    return lax.dot_general(left, right, (((1,), (0,)), ((), ())), preferred_element_type=F32)


def nt(left, right):
    return lax.dot_general(left, right, (((1,), (1,)), ((), ())), preferred_element_type=F32)


def norm_stats(z):
    mean = jnp.mean(z, axis=-1, keepdims=True)
    cent = z - mean
    var = jnp.mean(cent * cent, axis=-1, keepdims=True)
    inv = lax.rsqrt(var + EPS)
    return cent * inv, inv


def norm_back(grad, gain, normed, inv):
    e = grad * gain
    me = jnp.mean(e, axis=-1, keepdims=True)
    men = jnp.mean(e * normed, axis=-1, keepdims=True)
    return inv * (e - me - normed * men)


def rows_sum(a):
    return jnp.sum(a, axis=0, keepdims=True)


def split_pair(block):
    lane = lax.broadcasted_iota(jnp.int32, block.shape, 1)
    zero = jnp.zeros_like(block)
    return jnp.concatenate(
        [jnp.where(lane < HD, block, zero), jnp.where(lane < HD, zero, block)], axis=0
    )


def join_pair(both):
    q = both.shape[1] // 2
    row = lax.broadcasted_iota(jnp.int32, (both.shape[0], q), 0)
    return jnp.where(row < HD, both[:, :q], both[:, q:])


def vrow(vec_ref, row):
    return jnp.concatenate([vec_ref[j, row : row + 1] for j in range(vec_ref.shape[0])], axis=1)


def swap(pair):
    return (pair % 2) * 2 + pair // 2


def pick(own_ref, peer_ref, mat, other_half):
    shape = own_ref.shape
    own = own_ref[0, mat].reshape(shape[2] * shape[3], shape[4])
    other = peer_ref[0, mat].reshape(shape[2] * shape[3], shape[4])
    return jnp.where(other_half, other, own)


def put_pieces(ref, at, first, value, ranks_ref):
    n_x, n_z = ref.shape[1], ref.shape[2]
    rows = value.shape[0] // (n_x * n_z)
    for d in range(n_x):
        for z in range(n_z):
            i = d * n_z + z
            ref[at, d ^ ranks_ref[0], z ^ ranks_ref[1], first : first + rows] = value[
                i * rows : (i + 1) * rows
            ]


def attn_fwd_body(
    causal, q_rows, kv_parts, w, biases,
    q_ref, k_ref, v_ref, p_refs, ot_ref, o_ref, il_ref, acc_ref,
):
    wq, wk, wv, wo = w
    kv = nn(kv_parts, jnp.concatenate([wk, wv], axis=1))
    k = kv[:, :PAIR].astype(BF)
    v = (kv[:, PAIR:] + biases[1]).astype(BF)
    q = (nn(q_rows, wq) + biases[0]).astype(BF) * HD ** (-0.5)
    q_ref[0] = q
    k_ref[0] = k
    v_ref[0] = v
    vt = v.T
    blocks = len(p_refs)
    rows = q.shape[0] // blocks
    keys = k.shape[0]
    for b in range(blocks):
        n = keys // blocks * (b + 1) if causal else keys
        s = nt(k[:n], split_pair(q[b * rows : (b + 1) * rows]))
        top = jnp.max(s, axis=0, keepdims=True)
        p = jnp.exp(s - top)
        inv = 1.0 / jnp.sum(p, axis=0, keepdims=True)
        pb = p.astype(BF)
        p_refs[b][0] = pb
        ot = join_pair(nn(vt[:, :n], pb) * inv)
        span = slice(b * rows, (b + 1) * rows)
        ot_ref[0, :, span] = ot.astype(BF)
        o_ref[0, span, :] = ot.T.astype(BF)
        il_ref[0, 0:1, span] = inv[:, :rows]
        il_ref[0, 1:2, span] = inv[:, rows:]
    acc_ref[...] += nt(o_ref[0], wo)


def finish_norm(acc_ref, n_ref, r_ref):
    normed, inv = norm_stats(acc_ref[...])
    n_ref[...] = normed
    r_ref[...] = jnp.broadcast_to(inv, r_ref.shape)


def self_fwd(ranks_ref, xo_ref, xp_ref, wa_ref, wb_ref, va_ref, vb_ref, *refs):
    saved, (n_ref, r_ref, vec_ref, bias_ref, x_all, acc_ref) = refs[:10], refs[10:]
    q_ref, k_ref, v_ref, *p_refs, ot_ref, o_ref, il_ref = saved
    s = pl.program_id(0)
    blocks = 4
    half = xo_ref.shape[0] // blocks
    tiles = vec_ref.shape[0]

    @pl.when(s == 0)
    def _():
        for b in range(blocks):
            x_all[2 * b * half : (2 * b + 1) * half] = xo_ref[b * half : (b + 1) * half]
            x_all[(2 * b + 1) * half : (2 * b + 2) * half] = xp_ref[b * half : (b + 1) * half]
        both = va_ref[...].astype(F32) + vb_ref[...].astype(F32)
        vec_ref[...] = both[:tiles]
        bias_ref[...] = both[tiles]
        acc_ref[...] = xo_ref[...].astype(F32) + vrow(vec_ref, 5)

    w = [pick(wa_ref, wb_ref, i, s >= 2) for i in range(4)]
    t = swap(s) ^ ranks_ref[4]
    attn_fwd_body(True, xo_ref[...], x_all[...], w, (vec_ref[t, 3:4], vec_ref[t, 4:5]),
                  q_ref, k_ref, v_ref, p_refs, ot_ref, o_ref, il_ref, acc_ref)

    @pl.when(s == pl.num_programs(0) - 1)
    def _():
        finish_norm(acc_ref, n_ref, r_ref)


def cross_fwd(ranks_ref, n1_ref, mo_ref, mp_ref, wa_ref, wb_ref, vec_ref, *refs):
    saved, (n_ref, r_ref, m_all, h_low, acc_ref) = refs[:10], refs[10:]
    q_ref, k_ref, v_ref, *p_refs, ot_ref, o_ref, il_ref = saved
    s = pl.program_id(0)
    half = mo_ref.shape[0]

    @pl.when(s == 0)
    def _():
        m_all[:half] = mo_ref[...]
        m_all[half:] = mp_ref[...]
        h1 = n1_ref[...] * vrow(vec_ref, 0) + vrow(vec_ref, 6)
        h_low[...] = h1.astype(BF)
        acc_ref[...] = h1 + vrow(vec_ref, 9)

    w = [pick(wa_ref, wb_ref, i, s >= 2) for i in range(4)]
    t = swap(s) ^ ranks_ref[4]
    attn_fwd_body(False, h_low[...], m_all[...], w, (vec_ref[t, 7:8], vec_ref[t, 8:9]),
                  q_ref, k_ref, v_ref, p_refs, ot_ref, o_ref, il_ref, acc_ref)

    @pl.when(s == pl.num_programs(0) - 1)
    def _():
        finish_norm(acc_ref, n_ref, r_ref)


def ffn_both(ranks_ref, n2_ref, r2_ref, c0, c1, c2, c3, w_ref, bias_ref, vec_ref,
             h0, h1, h2, h3, keep_ref, send_ref, dz2_ref, vg_ref, bg_ref,
             h_low, h_t, act, slope, acc, dz3_low, dz3_t, dh2):
    phase = pl.program_id(0)
    t = pl.program_id(1)
    d = n2_ref.shape[1]
    last = pl.num_programs(1) - 1
    w_in = w_ref[:, 0, 0].reshape(d, -1)
    w_out = w_ref[:, 0, 1].reshape(d, -1)
    hid = w_in.shape[1]
    strips = hid // PAIR

    @pl.when((phase == 0) & (t == 0))
    def _():
        h = n2_ref[...] * vrow(vec_ref, 1) + vrow(vec_ref, 10)
        h_low[...] = h.astype(BF)
        h_t[...] = h.astype(BF).T
        acc[...] = h + vrow(vec_ref, 11)

    @pl.when(phase == 0)
    def _():
        bias = jnp.concatenate(
            [bias_ref[pl.ds(t * strips + j, 1), :] for j in range(strips)], axis=1
        )
        u = nn(h_low[...], w_in) + bias
        cube = GELU_A * u * u
        th = jnp.tanh(GELU_C * u * (1.0 + cube))
        low = 0.5 * (1.0 + th)
        f = (u * low).astype(BF)
        act[t] = f
        slope[t] = low + 0.5 * u * (1.0 - th * th) * (GELU_C * (1.0 + 3.0 * cube))
        acc[...] += nt(f, w_out)

    @pl.when((phase == 0) & (t == last))
    def _():
        n3, r3 = norm_stats(acc[...])
        acc[...] = n3 * vrow(vec_ref, 2) + vrow(vec_ref, 12)
        put_home(acc, (h0, h1, h2, h3), ranks_ref)
        for r, ref in enumerate((c0, c1, c2, c3)):
            rows = ref.shape[0]
            at = pl.multiple_of((r ^ ranks_ref[1]) * rows, rows)
            dh2[pl.ds(at, rows), :] = ref[...].astype(F32)
        g = dh2[...]
        vg_ref[0:1] = rows_sum(g * n3)
        vg_ref[1:2] = rows_sum(g)
        dz3 = norm_back(g, vrow(vec_ref, 2), n3, r3)
        vg_ref[2:3] = rows_sum(dz3)
        low = dz3.astype(BF)
        dz3_low[...] = low
        dz3_t[...] = low.T
        dh2[...] = dz3

    @pl.when(phase == 1)
    def _():
        f = act[t]
        df = nn(dz3_low[...], w_out).astype(BF).astype(F32)
        du = (df * slope[t]).astype(BF)
        g_out = nn(dz3_t[...], f).astype(BF)
        g_in = nn(h_t[...], du).astype(BF)
        sums = rows_sum(du.astype(F32))
        for j in range(strips):
            bg_ref[pl.ds(t * strips + j, 1), :] = sums[:, j * PAIR : (j + 1) * PAIR]
        dh2[...] += nt(du, w_in)
        mine = t % 2 == ranks_ref[3]
        piece = keep_ref.shape[3] // 2

        @pl.when(mine)
        def _():
            put_pieces(keep_ref, 0, 0, g_in, ranks_ref)
            put_pieces(keep_ref, 0, piece, g_out, ranks_ref)

        @pl.when(jnp.logical_not(mine))
        def _():
            put_pieces(send_ref, 0, 0, g_in, ranks_ref)
            put_pieces(send_ref, 0, piece, g_out, ranks_ref)

    @pl.when((phase == 1) & (t == last))
    def _():
        g = dh2[...]
        n2 = n2_ref[...]
        vg_ref[3:4] = rows_sum(g * n2)
        vg_ref[4:5] = rows_sum(g)
        dz2 = norm_back(g, vrow(vec_ref, 1), n2, r2_ref[:, 0:1])
        vg_ref[5:6] = rows_sum(dz2)
        vg_ref[6:8] = jnp.zeros_like(vg_ref[6:8])
        dz2_ref[...] = dz2


def put_home(acc, refs, ranks_ref):
    rows = refs[0].shape[0]
    for r, ref in enumerate(refs):
        at = pl.multiple_of((r ^ ranks_ref[1]) * rows, rows)
        ref[...] = acc[pl.ds(at, rows), :].astype(BF)


def self_bwd(ranks_ref, act_ref, dz_ref, part_ref, w_ref, *refs):
    saved, (slot_ref, own_ref, peer_ref, out_ref, qg_ref, *scratch) = refs[:10], refs[10:]
    shape = w_ref.shape
    w = [w_ref[0, i].reshape(shape[2] * shape[3], shape[4]) for i in (0, 3)]

    def first():
        dz = dz_ref[...]
        return act_ref[...].T, dz, part_ref[...]

    def store(g_q, g_o, piece):
        put_pieces(slot_ref, 0, 0, g_q, ranks_ref)
        put_pieces(slot_ref, 0, piece, g_o, ranks_ref)

    def last(total):
        out_ref[...] = total

    attn_bwd(True, first, w, saved, store, last, slot_ref.shape[3] // 2,
             own_ref, peer_ref, qg_ref, *scratch)


def cross_bwd(ranks_ref, n_ref, r_ref, dz_ref, wa_ref, wb_ref, vec_ref, *refs):
    saved = refs[:10]
    keep_ref, send_ref, own_ref, peer_ref, out_ref, vg_ref, qg_ref, *scratch = refs[10:]
    s = pl.program_id(0)
    odd = s >= 2

    def first():
        h = n_ref[...] * vrow(vec_ref, 0) + vrow(vec_ref, 6)
        dz = dz_ref[...]
        return h.astype(BF).T, dz, dz

    def store(g_q, g_o, piece):
        @pl.when(jnp.logical_not(odd))
        def _():
            put_pieces(keep_ref, 0, 0, g_q, ranks_ref)
            put_pieces(keep_ref, 0, piece, g_o, ranks_ref)

        @pl.when(odd)
        def _():
            put_pieces(send_ref, 0, 0, g_q, ranks_ref)
            put_pieces(send_ref, 0, piece, g_o, ranks_ref)

    def last(g):
        normed = n_ref[...]
        vg_ref[0:1] = rows_sum(g * normed)
        vg_ref[1:2] = rows_sum(g)
        dz1 = norm_back(g, vrow(vec_ref, 0), normed, r_ref[:, 0:1])
        vg_ref[2:3] = rows_sum(dz1)
        vg_ref[3:8] = jnp.zeros_like(vg_ref[3:8])
        out_ref[...] = dz1

    w = [pick(wa_ref, wb_ref, i, odd) for i in (0, 3)]
    attn_bwd(False, first, w, saved, store, last, keep_ref.shape[3] // 2,
             own_ref, peer_ref, qg_ref, *scratch)


def attn_bwd(causal, first, w, saved, store, last, piece, own_ref, peer_ref, qg_ref,
             dy, dy_t, act_t, acc, dk_ref, dv_ref):
    s = pl.program_id(0)
    q_ref, k_ref, v_ref, p0, p1, p2, p3, ot_ref, o_ref, il_ref = saved
    p_refs = (p0, p1, p2, p3)
    blocks = len(p_refs)
    wq, wo = w

    @pl.when(s == 0)
    def _():
        act_t[...], dz, acc[...] = first()
        low = dz.astype(BF)
        dy[...] = low
        dy_t[...] = low.T

    q = q_ref[0]
    k = k_ref[0]
    v = v_ref[0]
    keys = k.shape[0]
    rows = q.shape[0] // blocks
    do = nn(dy[...], wo).astype(BF)
    g_o = nn(dy_t[...], o_ref[0]).astype(BF)
    do_t = do.T.astype(F32)
    prod = do_t * ot_ref[0].astype(F32)
    inv_a, inv_b = il_ref[0, 0:1], il_ref[0, 1:2]
    inner_a = jnp.sum(prod[:HD], axis=0, keepdims=True) * inv_a
    inner_b = jnp.sum(prod[HD:], axis=0, keepdims=True) * inv_b
    row = lax.broadcasted_iota(jnp.int32, do_t.shape, 0)
    dos = (do_t * jnp.where(row < HD, inv_a, inv_b)).astype(BF).T
    kt = k.T
    dqs = [None] * blocks
    for b in reversed(range(blocks)):
        n = keys // blocks * (b + 1) if causal else keys
        span = slice(b * rows, (b + 1) * rows)
        dob = split_pair(dos[span])
        qb = split_pair(q[span])
        pb = p_refs[b][0]
        dp = nt(v[:n], dob)
        inner = jnp.concatenate([inner_a[:, span], inner_b[:, span]], axis=1)
        ds = (pb.astype(F32) * (dp - inner)).astype(BF)
        dv = nn(pb, dob)
        dk = nn(ds, qb)
        if b == blocks - 1:
            dv_ref[...] = dv
            dk_ref[...] = dk
        else:
            dv_ref[:n] += dv
            dk_ref[:n] += dk
        dqs[b] = (join_pair(nn(kt[:, :n], ds)) * HD ** (-0.5)).T.astype(BF)
    dq = jnp.concatenate(dqs, axis=0)
    g_q = nn(act_t[...], dq).astype(BF)
    store(g_q, g_o, piece)
    qg_ref[0] = rows_sum(dq.astype(F32))
    acc[...] += nt(dq, wq)
    for i, ref in enumerate((dk_ref, dv_ref)):
        if causal:
            for b in range(blocks):
                at = 2 * b * rows
                own_ref[i, 0, b * rows : (b + 1) * rows] = ref[at : at + rows]
                peer_ref[i, 0, b * rows : (b + 1) * rows] = ref[at + rows : at + 2 * rows].astype(BF)
        else:
            own_ref[i, 0] = ref[: keys // 2]
            peer_ref[i, 0] = ref[keys // 2 :].astype(BF)

    @pl.when(s == pl.num_programs(0) - 1)
    def _():
        last(acc[...])


def kv_back(final, lanes, blen, ranks_ref, act_ref, wa_ref, wb_ref, *rest):
    if final:
        (own_ref, got_ref, own_hi, got_hi, base_ref, vgc_ref, vgf_ref, bg_ref, qgs_ref, qgs_hi,
         qgc_ref, vg_mem_ref,
         h0, h1, h2, h3, keep_ref, send_ref, act_t, acc, vg_self, tiles) = rest
    else:
        own_ref, got_ref, h0, h1, h2, h3, keep_ref, send_ref, vgrad_ref, act_t, acc = rest
    s = pl.program_id(0)
    odd = s >= 2
    wk = pick(wa_ref, wb_ref, 1, odd)
    wv = pick(wa_ref, wb_ref, 2, odd)

    @pl.when(s == 0)
    def _():
        act_t[...] = act_ref[...].T
        if final:
            acc[...] = base_ref[...]
        else:
            acc[...] = jnp.zeros_like(acc)

    dk, dv = (own_ref[i, 0] + got_ref[i, 0].astype(F32) for i in range(2))
    if final:
        dk = jnp.where(odd, own_hi[0, 0] + got_hi[0, 0].astype(F32), dk)
        dv = jnp.where(odd, own_hi[1, 0] + got_hi[1, 0].astype(F32), dv)
    dk, dv = dk.astype(BF), dv.astype(BF)
    dkv = jnp.concatenate([dk, dv], axis=1)
    gkv = nn(act_t[...], dkv).astype(BF)
    piece = gkv.shape[0] // (keep_ref.shape[1] * keep_ref.shape[2])
    at = s % 2 if final else 0

    @pl.when(jnp.logical_not(odd))
    def _():
        put_pieces(keep_ref, at, 0, gkv[:, :PAIR], ranks_ref)
        put_pieces(keep_ref, at, piece, gkv[:, PAIR:], ranks_ref)

    @pl.when(odd)
    def _():
        put_pieces(send_ref, at, 0, gkv[:, :PAIR], ranks_ref)
        put_pieces(send_ref, at, piece, gkv[:, PAIR:], ranks_ref)

    sums = rows_sum(dv.astype(F32))
    acc[...] += nt(dkv, jnp.concatenate([wk, wv], axis=1))
    if not final:
        vgrad_ref[0] = sums
    else:
        vg_self[s] = sums
        pairs = vg_self.shape[0]

        @pl.when(s == 0)
        def _():
            for j in range(pairs):
                at = slice(j * PAIR, (j + 1) * PAIR)
                rel = swap(j ^ ranks_ref[4])
                tiles[j, 0:1] = vgc_ref[0:1, at]
                tiles[j, 1:2] = vgf_ref[3:4, at]
                tiles[j, 2:3] = vgf_ref[0:1, at]
                tiles[j, 3:4] = jnp.where(rel < 2, qgs_ref[rel % 2], qgs_hi[rel % 2])
                tiles[j, 5:6] = vgc_ref[2:3, at]
                tiles[j, 6:7] = vgc_ref[1:2, at]
                tiles[j, 7:8] = qgc_ref[rel]
                tiles[j, 8:9] = vg_mem_ref[rel]
                tiles[j, 9:10] = vgf_ref[5:6, at]
                tiles[j, 10:11] = vgf_ref[4:5, at]
                tiles[j, 11:12] = vgf_ref[2:3, at]
                tiles[j, 12:13] = vgf_ref[1:2, at]
                tiles[j, 13:16] = jnp.zeros((3, PAIR), F32)

        tiles[swap(s) ^ ranks_ref[4], 4:5] = sums
        rows_at = lax.broadcasted_iota(jnp.int32, (16, PAIR), 0)
        n_x, n_z = keep_ref.shape[1], keep_ref.shape[2]

        @pl.when(s == pairs - 1)
        def _():
            for ry in range(2):
                for rc, ref in enumerate((keep_ref, send_ref)):
                    for i in range(n_x):
                        for k in range(n_z):
                            dc = (i ^ ranks_ref[0]) * n_z + (k ^ ranks_ref[1])
                            p = dc * pairs + ((2 * ry + rc) ^ ranks_ref[4])
                            tile = tiles[lax.div(p * lanes, PAIR)]
                            bias = bg_ref[pl.ds(lax.div(p * blen, PAIR), 1), :]
                            both = jnp.where(rows_at == 13, bias, tile).astype(BF)
                            ref[ry, i, k, 2 * piece : 2 * piece + 16] = both

    @pl.when(s == pl.num_programs(0) - 1)
    def _():
        put_home(acc, (h0, h1, h2, h3), ranks_ref)


def pack_rows(*refs):
    ins, outs = refs[1 : 1 + len(refs) // 2], refs[1 + len(refs) // 2 :]
    for ref, out in zip(ins, outs):
        out[...] = ref[0]


def pack_rest(*refs):
    ins, (win, wout), outs, f_ref = refs[1:9], refs[9:11], refs[11:19], refs[19]
    for ref, out in zip(ins, outs):
        out[...] = ref[0]
    f_ref[0] = win[...]
    f_ref[1] = wout[...]


def pack_weights(lanes, blen, ranks_ref, wqs, wks, wvs, wos, wqc, wkc, wvc, woc,
                 gains, shifts, bias, s_ref, c_ref, va, vb):
    n = wqs.shape[0]
    for i, ref in enumerate((wqc, wkc, wvc, woc)):
        c_ref[i * n : (i + 1) * n] = ref[...]
    for i, ref in enumerate((wqs, wks, wvs, wos)):
        s_ref[i * n : (i + 1) * n] = ref[...]
    p = (ranks_ref[0] * 4 + ranks_ref[1]) * 4 + ranks_ref[4]
    at = 4 * n
    va[...] = jnp.zeros_like(va)
    va[0:3, 0:lanes] = gains[...].astype(F32)
    va[3:13, 0:lanes] = shifts[...].astype(F32)
    s_ref[at : at + 16] = pltpu.roll(va[...], lax.rem(p * lanes, PAIR), 1).astype(BF)
    vb[...] = jnp.zeros_like(vb)
    vb[pl.ds(lax.div(p * blen, PAIR), 1), 0:blen] = bias[...].astype(F32)
    s_ref[at + 16 : at + 32] = pltpu.roll(vb[...], lax.rem(p * blen, PAIR), 1).astype(BF)


def whole(a):
    return pl.BlockSpec(a.shape, lambda *_: (0,) * len(a.shape))


def without(body, at, count):
    return lambda *refs: body(*refs[:at], *refs[at + count :])


def launch(body, name, grid, ranks, ins, outs, scratch=(), deps=(), limit=VMEM_LIMIT, cost=SMALL_COST):
    first = 0 if ranks is None else 1
    deps = list(deps)
    n_in, n_out = first + len(ins), len(outs)

    def with_token(*refs):
        kept = refs[:n_in] + refs[n_in + len(deps) :]
        kept[n_in + n_out][...] = jnp.zeros((8, PAIR), F32)
        body(*kept[: n_in + n_out], *kept[n_in + n_out + 1 :])

    token = struct((8, PAIR), F32)
    call = pl.pallas_call(
        with_token,
        grid_spec=pltpu.PrefetchScalarGridSpec(
            num_scalar_prefetch=first,
            grid=grid,
            in_specs=[i[1] for i in ins] + [pl.BlockSpec(memory_space=pl.ANY)] * len(deps),
            out_specs=tuple(o[1] for o in outs) + (whole(token),),
            scratch_shapes=list(scratch),
        ),
        out_shape=tuple(
            pltpu.HBM(o[0].shape, o[0].dtype) if len(o) > 2 else o[0] for o in outs
        ) + (token,),
        compiler_params=pltpu.CompilerParams(
            vmem_limit_bytes=limit, dimension_semantics=("arbitrary",) * len(grid)
        ),
        cost_estimate=pl.CostEstimate(flops=cost, bytes_accessed=1, transcendentals=0),
        name=name,
    )
    args = [
        pltpu.with_memory_space_constraint(i[0], pltpu.HBM) if len(i) > 2 else i[0] for i in ins
    ] + deps
    return call(*args) if ranks is None else call(ranks, *args)


def local(body, name, outs, *ins, ranks=None, scratch=(), deps=(), pinned=(), limit=SMALL_LIMIT,
          cost=SMALL_COST):
    return launch(
        body, name, (1,), ranks, [(a, whole(a)) for a in ins],
        [(o, whole(o), True) if i in pinned else (o, whole(o)) for i, o in enumerate(outs)],
        scratch, deps, limit, cost,
    )


def struct(shape, dtype):
    return jax.ShapeDtypeStruct(shape, dtype)


def restack(ins, outs, cuts):
    for out, (lo, hi) in zip(outs, cuts):
        for r, ref in enumerate(ins):
            out[0, 0, r] = ref[lo:hi]


def double(own, got, out, axis):
    m = own.shape[axis]
    if axis == 0:
        out[:m] = own[...]
        out[m:] = got[...]
    else:
        out[:, :m] = own[...]
        out[:, m:] = got[...]


def order(ranks_ref, parts, outs):
    for r, ref in enumerate(parts):
        rows = ref.shape[-2]
        at = pl.multiple_of((r ^ ranks_ref[1]) * rows, rows)
        for i, out in enumerate(outs):
            out[pl.ds(at, rows), :] = ref[...] if len(outs) == 1 else ref[i]


def assemble(lanes, ranks_ref, a0, a1, b0, b1, w_ref, v_ref=None, scr=None):
    pairs = 4
    n_x, n_z = a0.shape[1], a0.shape[2]
    prows = w_ref.shape[3]
    if v_ref is not None:
        scr[...] = jnp.zeros_like(scr)
    for ry in range(2):
        a_ref = (a0, a1)[ry]
        for i in range(n_x):
            for k in range(n_z):
                dc = (i ^ ranks_ref[0]) * n_z + (k ^ ranks_ref[1])
                b_ref, bi = (b0, i) if i < n_x // 2 else (b1, i - n_x // 2)
                for m in range(2):
                    span = slice(m * prows, (m + 1) * prows)
                    w_ref[ry, m, dc] = a_ref[0, i, k, span]
                    w_ref[ry, 2 + m, dc] = b_ref[ry, bi, k, span]
                if v_ref is not None:
                    at = 2 * prows
                    p = dc * pairs + ((2 * ry) ^ ranks_ref[4])
                    tile = lax.div(p * lanes, PAIR)
                    scr[tile] += b_ref[ry, bi, k, at : at + 16].astype(F32)
                    scr[pairs] += b_ref[ry, bi, k, at + 16 : at + 32].astype(F32)
    if v_ref is not None:
        v_ref[...] = scr[...].astype(BF)


def start_one(cuts, ranks_ref, *refs):
    restack(refs[0:4], refs[8:10], cuts)
    order(ranks_ref, refs[4:8], refs[10:11])


def start_two(axes, cuts, a, ga, b, gb, *refs):
    double(a, ga, refs[4], axes[0])
    double(b, gb, refs[5], axes[1])
    restack(refs[0:4], refs[6:8], cuts)


def start_five(lanes, ranks_ref, *refs):
    assemble(lanes, ranks_ref, *refs[0:4], refs[8])
    order(ranks_ref, refs[4:8], refs[9:10])


def double_both(axes, a, ga, b, gb, out_a, out_b):
    double(a, ga, out_a, axes[0])
    double(b, gb, out_b, axes[1])


def order_home(ranks_ref, *refs):
    order(ranks_ref, refs[:4], refs[4:])


def halve_body(axis_a, axis_b, cuts, *refs):
    ins, (sa, ka, sb, kb) = refs[: len(refs) - 4], refs[len(refs) - 4 :]

    def place(axis, send, keep, at, value):
        rows = value.shape[3]
        m = value.shape[axis] // 2
        lo = value[:m] if axis == 0 else value[:, :m]
        hi = value[m:] if axis == 0 else value[:, m:]
        keep[:, :, :, at : at + rows] = lo
        send[:, :, :, at : at + rows] = hi.astype(BF)

    at_a = at_b = 0
    for cut in cuts:
        if cut is None:
            keep_a, got_a, keep_b, got_b, *ins = ins
            parts = (keep_a[...] + got_a[...].astype(F32), keep_b[...] + got_b[...].astype(F32))
        else:
            keep, got, *ins = ins
            total = keep[...].astype(F32) + got[...].astype(F32)
            parts = (total[:, :, :, :cut], total[:, :, :, cut:])
        place(axis_a, sa, ka, at_a, parts[0])
        place(axis_b, sb, kb, at_b, parts[1])
        at_a += parts[0].shape[3]
        at_b += parts[1].shape[3]


def spread_body(*refs):
    ins, (s1, s2, s3, keep) = refs[:-4], refs[-4:]
    at = 0
    for own, got in zip(ins[::2], ins[1::2]):
        rows = own.shape[3]
        for r, ref in enumerate((keep, s1, s2, s3)):
            total = own[0, 0, r] + got[0, 0, r].astype(F32)
            ref[at : at + rows] = total.astype(ref.dtype)
        at += rows


def finish_body(plan, lanes, blen, ranks_ref, keep, r1, r2, r3, *outs):
    total = keep[...] + r1[...].astype(F32) + r2[...].astype(F32) + r3[...].astype(F32)
    at = 0
    outs = list(outs)
    for turn, rows in plan:
        part = total[at : at + rows]
        at += rows
        if turn == 2:
            p = (ranks_ref[0] * 4 + ranks_ref[1]) * 4 + ranks_ref[4]
            vec = pltpu.roll(part, lax.rem(PAIR - lax.rem(p * lanes, PAIR), PAIR), 1)
            outs.pop(0)[...] = vec[0:3, :lanes]
            outs.pop(0)[...] = vec[3:13, :lanes]
            own = pltpu.roll(part, lax.rem(PAIR - lax.rem(p * blen, PAIR), PAIR), 1)
            outs.pop(0)[...] = own[13:14, :blen]
        else:
            outs.pop(0)[...] = part


def home_body(every, out_ref):
    n_c, n_z, rows, _ = every.shape
    for c in range(n_c):
        for z in range(n_z):
            out_ref[z, c * rows : (c + 1) * rows, :] = every[c, z].astype(out_ref.dtype)


def half_spec(w, other):
    if other:
        return pl.BlockSpec((1,) + w.shape[1:], lambda s, _: (jnp.maximum(s - 2, 0), 0, 0, 0, 0))
    return pl.BlockSpec((1,) + w.shape[1:], lambda s, _: (jnp.minimum(s, 1), 0, 0, 0, 0))


def slot_outs(n_x, n_z, rows):
    shape = struct((2, n_x, n_z, rows, PAIR), BF)
    block = (1, n_x, n_z, rows, PAIR)
    return [
        (shape, pl.BlockSpec(block, lambda s, _: (jnp.minimum(s, 1), 0, 0, 0, 0))),
        (shape, pl.BlockSpec(block, lambda s, _: (jnp.maximum(s - 2, 0), 0, 0, 0, 0))),
    ]


def full(shape):
    return pl.BlockSpec(shape, lambda *_: (0,) * len(shape))


def run_attn_fwd(causal, ranks, rows_in, w_own, w_peer, vecs, pairs, deps):
    own, d = rows_in[0].shape
    keys = 2 * own
    blocks = 4
    ns = [keys // blocks * (b + 1) if causal else keys for b in range(blocks)]
    qn = 2 * own // blocks

    def saved(shape, dtype):
        return (struct((pairs,) + shape, dtype),
                pl.BlockSpec((1,) + shape, lambda s, _: (s, 0, 0)), True)

    outs = [
        saved((own, PAIR), BF), saved((keys, PAIR), BF), saved((keys, PAIR), BF),
        *[saved((n, qn), BF) for n in ns],
        saved((PAIR, own), BF), saved((own, PAIR), BF), saved((8, own), F32),
        (struct((own, d), F32), full((own, d))),
        (struct((own, PAIR), F32), full((own, PAIR))),
    ]
    if causal:
        outs.append((struct((pairs, 16, PAIR), F32), full((pairs, 16, PAIR))))
        outs.append((struct((16, PAIR), F32), full((16, PAIR))))
    ins = [(a, whole(a)) for a in rows_in]
    ins += [(w_own, half_spec(w_own, False), True), (w_peer, half_spec(w_peer, True), True)]
    ins += [(a, whole(a)) for a in vecs]
    scratch = [pltpu.VMEM((keys, d), BF)] + ([] if causal else [pltpu.VMEM((own, d), BF)])
    scratch.append(pltpu.VMEM((own, d), F32))

    return launch(
        self_fwd if causal else cross_fwd, "self_fwd" if causal else "cross_fwd",
        (pairs,), ranks, ins, outs, scratch, deps,
        cost=COSTS["self_fwd" if causal else "cross_fwd"],
    )


def run_ffn(ranks, n2, r2, cots, w, bias, vec, n_x, n_z):
    own, d = n2.shape
    dc, parts, _, prows, hid = w.shape
    half = own // 4
    back = lambda p, t, ref: ((p * (t // 2)) ^ ref[2], 0, 0, 0, 0)
    slots = struct((2, n_x, n_z, 2 * prows, hid), BF)
    slot_block = pl.BlockSpec((1, n_x, n_z, 2 * prows, hid), back)
    outs = [(struct((half, d), BF), full((half, d)))] * 4 + [
        (slots, slot_block),
        (slots, slot_block),
        (struct((own, d), F32), full((own, d))),
        (struct((8, d), F32), full((8, d))),
        (struct((16, PAIR), F32), full((16, PAIR))),
    ]
    ins = [(n2, whole(n2)), (r2, whole(r2))] + [(c, whole(c)) for c in cots] + [
        (w, pl.BlockSpec((dc, 1, 2, prows, hid), lambda p, t, _: (0, t, 0, 0, 0)), True),
        (bias, whole(bias)),
        (vec, whole(vec)),
    ]
    scratch = [
        pltpu.VMEM((own, d), BF),
        pltpu.VMEM((d, own), BF),
        pltpu.VMEM((parts, own, hid), BF),
        pltpu.VMEM((parts, own, hid), F32),
        pltpu.VMEM((own, d), F32),
        pltpu.VMEM((own, d), BF),
        pltpu.VMEM((d, own), BF),
        pltpu.VMEM((own, d), F32),
    ]
    return launch(
        ffn_both, "ffn_both", (2, parts), ranks, ins, outs, scratch,
        cost=COSTS["ffn_both"],
    )


def bwd_scratch(own, keys, d):
    return [
        pltpu.VMEM((own, d), BF),
        pltpu.VMEM((d, own), BF),
        pltpu.VMEM((d, own), BF),
        pltpu.VMEM((own, d), F32),
        pltpu.VMEM((keys, PAIR), F32),
        pltpu.VMEM((keys, PAIR), F32),
    ]


def per_pair(a, first=0):
    return (a, pl.BlockSpec((1,) + a.shape[1:], lambda s, _: (s + first, 0, 0)), True)


def run_cross_bwd(ranks, dz, w_own, w_peer, vec, saved, n, r, n_x, n_z, deps):
    pairs, own, _ = saved[0].shape
    keys = saved[1].shape[1]
    d = dz.shape[1]
    prows = w_own.shape[3]
    kv_spec = pl.BlockSpec((2, 1, own, PAIR), lambda s, _: (0, s, 0, 0))
    outs = slot_outs(n_x, n_z, 2 * prows) + [
        (struct((2, pairs, own, PAIR), F32), kv_spec, True),
        (struct((2, pairs, own, PAIR), BF), kv_spec, True),
        (struct((own, d), F32), full((own, d))),
        (struct((8, d), F32), full((8, d))),
        (struct((pairs, 1, PAIR), F32), pl.BlockSpec((1, 1, PAIR), lambda s, _: (s, 0, 0))),
    ]
    ins = [
        (n, whole(n)),
        (r, whole(r)),
        (dz, whole(dz)),
        (w_own, half_spec(w_own, False), True),
        (w_peer, half_spec(w_peer, True), True),
        (vec, whole(vec)),
        *[per_pair(a) for a in saved],
    ]
    return launch(
        cross_bwd, "cross_bwd", (pairs,), ranks, ins, outs, bwd_scratch(own, keys, d), deps,
        cost=COSTS["cross_bwd"],
    )


def run_self_bwd(first, ranks, act, dz, part, w, saved, n_x, n_z, deps):
    _, own, _ = saved[0].shape
    keys = saved[1].shape[1]
    d = dz.shape[1]
    prows = w.shape[3]
    pairs = 2
    kv_spec = pl.BlockSpec((2, 1, own, PAIR), lambda s, _: (0, s, 0, 0))
    slots = (1, n_x, n_z, 2 * prows, PAIR)
    outs = [
        (struct((2,) + slots[1:], BF), pl.BlockSpec(slots, lambda s, _: (s, 0, 0, 0, 0))),
        (struct((2, pairs, own, PAIR), F32), kv_spec, True),
        (struct((2, pairs, own, PAIR), BF), kv_spec, True),
        (struct((own, d), F32), full((own, d))),
        (struct((pairs, 1, PAIR), F32), pl.BlockSpec((1, 1, PAIR), lambda s, _: (s, 0, 0))),
    ]
    ins = [
        (act, whole(act)),
        (dz, whole(dz)),
        (part, whole(part)),
        (w, pl.BlockSpec((1,) + w.shape[1:], lambda s, _: (s, 0, 0, 0, 0)), True),
        *[per_pair(a, first) for a in saved],
    ]
    return launch(
        self_bwd, "self_bwd", (pairs,), ranks, ins, outs, bwd_scratch(own, keys, d), deps,
        cost=COSTS["self_bwd"],
    )


def run_kv_back(name, ranks, act, parts, w_own, w_peer, extra, lanes, blen, n_x, n_z, deps):
    own, d = act.shape
    pairs = 2 * w_own.shape[0]
    prows = w_own.shape[3]
    final = bool(extra)
    rows = 2 * prows + (16 if final else 0)
    half = own // 4
    outs = [(struct((half, d), BF), full((half, d)))] * 4
    scratch = [pltpu.VMEM((d, own), BF), pltpu.VMEM((own, d), F32)]
    block = (2, 1, own, PAIR)
    if final:
        slots = struct((2, n_x, n_z, rows, PAIR), BF)
        outs += [(slots, whole(slots))] * 2
        scratch += [pltpu.VMEM((pairs, 1, PAIR), F32), pltpu.VMEM((pairs, 16, PAIR), F32)]
        low = pl.BlockSpec(block, lambda s, _: (0, jnp.minimum(s, 1), 0, 0))
        high = pl.BlockSpec(block, lambda s, _: (0, jnp.maximum(s - 2, 0), 0, 0))
        specs = [low, low, high, high]
    else:
        outs += slot_outs(n_x, n_z, rows)
        outs.append(
            (struct((pairs, 1, PAIR), F32), pl.BlockSpec((1, 1, PAIR), lambda s, _: (s, 0, 0)))
        )
        specs = [pl.BlockSpec(block, lambda s, _: (0, s, 0, 0)),
                 pl.BlockSpec(block, lambda s, _: (0, s ^ 2, 0, 0))]
    ins = [
        (act, whole(act)),
        (w_own, half_spec(w_own, False), True),
        (w_peer, half_spec(w_peer, True), True),
        *[(a, spec, True) for a, spec in zip(parts, specs)],
        *[(a, whole(a)) for a in extra],
    ]
    return launch(
        functools.partial(kv_back, final, lanes, blen), name, (pairs,), ranks, ins, outs,
        scratch, deps, cost=COSTS[name],
    )


ALL = ("dp", "ctx", "ty", "tc")


def shards(
    inputs, memory, cotangent, wq_self, wk_self, wv_self, wo_self, wq_cross, wk_cross, wv_cross,
    wo_cross, w_in, w_out, gains, shifts, ffn_bias,
):
    seqs, block, d = inputs.shape
    n_x, n_z, n_y, n_c = (lax.axis_size(a) for a in ALL)
    pairs = n_y * n_c
    half = block // n_c
    own = n_z * half
    x_rank, z_rank, y_rank, c_rank = (lax.axis_index(a) for a in ALL)
    ranks = jnp.stack([x_rank, z_rank, y_rank, c_rank, y_rank * n_c + c_rank]).astype(jnp.int32)
    prows, lanes, blen = wq_self.shape[0], gains.shape[1], ffn_bias.shape[0]
    hid = w_in.shape[1]
    x_bits = [1 << i for i in range((n_x - 1).bit_length())]

    def send(array, axis, bit):
        return lax.ppermute(array, axis, [(i, i ^ bit) for i in range(lax.axis_size(axis))])

    def rows_of(r):
        return pl.BlockSpec((1, half, d), lambda i, ref: (ref[2] * 4 + (ref[1] ^ r), ref[3], 0))

    def packed_rows(array):
        return [(array, rows_of(r), True) for r in range(n_z)]

    def around_z(parts):
        return [parts[0]] + [send(parts[r], "ctx", r) for r in range(1, n_z)]

    row_part = struct((half, d), BF)

    def sent_rows(array, name, deps):
        *parts, token = launch(
            pack_rows, name, (1,), ranks, packed_rows(array), [(row_part, whole(row_part))] * n_z,
            deps=deps, limit=SMALL_LIMIT,
        )
        return around_z(parts), token

    x_got, token = sent_rows(inputs, "pack_x", [])
    s_pack, c_pack, token = local(
        functools.partial(pack_weights, lanes, blen), "pack_weights",
        [struct((4 * prows + 32, PAIR), BF), struct((4 * prows, PAIR), BF)],
        wq_self, wk_self, wv_self, wo_self.T, wq_cross, wk_cross, wv_cross, wo_cross.T,
        gains, shifts, ffn_bias.reshape(1, -1), ranks=ranks, deps=[token],
        scratch=[pltpu.VMEM((16, PAIR), F32), pltpu.VMEM((16, PAIR), F32)],
    )
    s_got = around_z([s_pack] * n_z)
    cuts_s = ((0, 2 * prows), (2 * prows, 4 * prows + 32))
    cuts_c = ((0, 2 * prows), (2 * prows, 4 * prows))

    def z_slots(cuts):
        return [struct((1, 1, n_z, hi - lo, PAIR), BF) for lo, hi in cuts]

    def doubled(array, axis):
        shape = list(array.shape)
        shape[axis] *= 2
        return struct(tuple(shape), BF)

    steps_a = [("dp", bit) for bit in x_bits] + [("ty", 1)]
    steps_b = [("ty", 1)] + [("dp", bit) for bit in x_bits]
    axis_of = {"ty": 0, "dp": 1}
    axes_at = [(axis_of[sa[0]], axis_of[sb[0]]) for sa, sb in zip(steps_a, steps_b)]

    def step(i, a, b):
        return [a, send(a, *steps_a[i]), b, send(b, *steps_b[i])]

    def more(ins, deps):
        for i in range(len(steps_a) - 1):
            a, b, token = local(
                functools.partial(double_both, axes_at[i]), "double",
                [doubled(ins[0], axes_at[i][0]), doubled(ins[2], axes_at[i][1])], *ins, deps=deps,
            )
            ins, deps = step(i + 1, a, b), [token]
        return ins, token

    sa, sb, xo, token = local(
        functools.partial(start_one, cuts_s), "start_one",
        z_slots(cuts_s) + [struct((own, d), BF)], *s_got, *x_got, ranks=ranks,
    )
    xp = send(xo, "tc", 1)
    c_got = around_z([c_pack] * n_z)
    sa, sb, ca, cb, token = local(
        functools.partial(start_two, axes_at[0], cuts_c), "start_two",
        [doubled(sa, axes_at[0][0]), doubled(sb, axes_at[0][1])] + z_slots(cuts_c),
        *step(0, sa, sb), *c_got, deps=[token],
    )
    s_last = step(1, sa, sb)
    c_last = step(0, ca, cb)
    for i in range(1, len(steps_a) - 1):
        sa, sb, token = local(
            functools.partial(double_both, axes_at[i]), "double",
            [doubled(s_last[0], axes_at[i][0]), doubled(s_last[2], axes_at[i][1])],
            *s_last, deps=[token],
        )
        s_last = step(i + 1, sa, sb)
    f_shape = struct((2, prows, hid), BF)
    *packed, f_pack, token = launch(
        pack_rest, "pack_rest", (1,), ranks,
        packed_rows(memory) + packed_rows(cotangent) + [(a, whole(a)) for a in (w_in, w_out.T)],
        [(row_part, whole(row_part))] * (2 * n_z) + [(f_shape, whole(f_shape), True)],
        deps=[token], limit=SMALL_LIMIT,
    )
    w_ffn = lax.all_gather(f_pack, ALL, axis=0, tiled=False).reshape(
        n_x * n_z, pairs, 2, prows, hid
    )
    m_got, cots = around_z(packed[:n_z]), around_z(packed[n_z:])
    w_shape = struct((2, 4, n_x * n_z, prows, PAIR), BF)
    ws_own, v_own, token = local(
        functools.partial(assemble, lanes), "assemble",
        [w_shape, struct((pairs + 1, 16, PAIR), BF)], *s_last, ranks=ranks,
        scratch=[pltpu.VMEM((pairs + 1, 16, PAIR), F32)], deps=[token], pinned=(0,),
    )
    v_peer, ws_peer = send(v_own, "tc", 1), send(ws_own, "tc", 1)
    c_last, token = more(c_last, [token])
    *saved_self, n1, r1, vec, bias, token = run_attn_fwd(
        True, ranks, (xo, xp), ws_own, ws_peer, (v_own, v_peer), pairs, [token]
    )
    wc_own, mo, token = local(
        functools.partial(start_five, lanes), "start_five", [w_shape, struct((own, d), BF)],
        *c_last, *m_got, ranks=ranks, deps=[token], pinned=(0,),
    )
    wc_peer, mp = send(wc_own, "tc", 1), send(mo, "tc", 1)
    *saved_cross, n2, r2, token = run_attn_fwd(
        False, ranks, (n1, mo, mp), wc_own, wc_peer, (vec,), pairs, [token]
    )
    *out_rows, f_keep, f_send, dz2, vg_ffn, bg, token = run_ffn(
        ranks, n2, r2, cots, w_ffn, bias, vec, n_x, n_z
    )

    def home_rows(got, deps, cost=SMALL_COST):
        here, token = local(
            order_home, "order_home", [struct((own, d), BF)], *got, ranks=ranks, deps=deps,
            cost=cost,
        )
        return here.reshape(n_z, half, d), token

    def home_all(here):
        return lax.all_gather(here, ("ty", "tc"), axis=0, tiled=False)

    def home_last(every, dtype, deps):
        return launch(
            home_body, "home", (n_y,), None,
            [(every, pl.BlockSpec((n_c, n_z, half, d), lambda y: (y, 0, 0, 0)), True)],
            [(struct((seqs, block, d), dtype),
              pl.BlockSpec((n_z, block, d), lambda y: (y, 0, 0)), True)],
            deps=deps, limit=2 * SMALL_LIMIT,
        )

    def to_core(*arrays):
        return [send(a, "tc", 1) for a in arrays]

    back_a = [("ty", 1)] + [("dp", bit) for bit in reversed(x_bits)]
    back_b = [("dp", bit) for bit in reversed(x_bits)] + [("ty", 1)]
    rounds = len(back_a)

    def shape_at(i, rows, lanes_in, steps):
        shape = [2, n_x, n_z, rows, lanes_in]
        for axis, _ in steps[: i + 1]:
            shape[axis_of[axis]] //= 2
        return tuple(shape)

    def halve(i, ins, cuts, rows, deps, cost=SMALL_COST):
        width = ins[0].shape[4]
        shape_a = shape_at(i, rows[0], width, back_a)
        shape_b = shape_at(i, rows[1], width, back_b)
        to_a, keep_a, to_b, keep_b, token = local(
            functools.partial(
                halve_body, axis_of[back_a[i][0]], axis_of[back_b[i][0]], cuts
            ),
            "halve",
            [struct(shape_a, BF), struct(shape_a, F32), struct(shape_b, BF), struct(shape_b, F32)],
            *ins, deps=deps, limit=2 * SMALL_LIMIT, cost=cost,
        )
        return [keep_a, send(to_a, *back_a[i]), keep_b, send(to_b, *back_b[i])], token

    def halve_more(groups, rows, deps, cost=SMALL_COST):
        ins, cuts = sum(groups, []), (None,) * len(groups)
        for i in range(1, rounds):
            ins, token = halve(i, ins, cuts, rows, deps, cost)
            cuts, deps = (None,), [token]
        return ins, token

    def spread(ins, deps):
        rows, width = sum(a.shape[3] for a in ins[::2]), ins[0].shape[4]
        *sends, keep, token = local(
            spread_body, "spread",
            [struct((rows, width), BF)] * 3 + [struct((rows, width), F32)], *ins, deps=deps,
        )
        return [keep] + [send(sends[r - 1], "ctx", r) for r in range(1, n_z)], token

    def finish(ins, plan, extra, deps):
        width = ins[0].shape[1]
        outs = [struct((size, width), F32) for turn, size in plan if turn != 2] + extra
        return local(
            functools.partial(finish_body, plan, lanes, blen), "finish", outs, *ins,
            ranks=ranks, deps=deps,
        )

    out_got = around_z(out_rows)
    rows_f = (prows, prows)
    ffn, token = halve(0, [f_keep, to_core(f_send)[0]], (prows,), rows_f, [token])
    c_keep, c_send, c_own, c_peer, dz1, vg_cross, qgc, token = run_cross_bwd(
        ranks, dz2, wc_own, wc_peer, vec, saved_cross, n1, r1, n_x, n_z, [token]
    )
    c_got, c_add = to_core(c_peer, c_send)
    ffn, token = halve_more([ffn], rows_f, [token])
    s_send, own_hi, peer_hi, base, qgs_hi, token = run_self_bwd(
        2, ranks, xo, dz1, dz1, ws_peer, saved_self, n_x, n_z, [token]
    )
    ffn, token = spread(ffn, [token])
    *mem_rows, m_keep, m_send, vgc, token = run_kv_back(
        "mem_back", ranks, mo, (c_own, c_got), wc_own, wc_peer, (), lanes, blen, n_x, n_z, [token]
    )
    mem_got = around_z(mem_rows)
    out_here, token = home_rows(out_got, [token])
    out_every = home_all(out_here)
    got_low, s_add = to_core(peer_hi, s_send)
    s_keep, own_low, peer_low, base, qgs, token = run_self_bwd(
        0, ranks, xo, dz1, base, ws_own, saved_self, n_x, n_z, [token]
    )
    (m_add,) = to_core(m_send)
    rows_one = (3 * prows, 3 * prows)
    one, token = halve(
        0, [c_keep, c_add, m_keep, m_add, s_keep, s_add], (prows,) * 3, rows_one, [token]
    )
    mem_here, token = home_rows(mem_got, [token], COVER)
    mem_every = home_all(mem_here)
    (got_hi,) = to_core(peer_low)
    *in_rows, i_keep, i_send, token = run_kv_back(
        "in_back", ranks, xo, (own_low, got_low, own_hi, got_hi), ws_own, ws_peer,
        (base, vg_cross, vg_ffn, bg, qgs, qgs_hi, qgc, vgc), lanes, blen, n_x, n_z, [token],
    )
    in_got = around_z(in_rows)
    one, token = halve_more([one], rows_one, [token], COVER)
    rows_two = (prows, prows + 16)
    two, token = halve(0, [i_keep, to_core(i_send)[0]], (prows,), rows_two, [token])
    in_here, token = home_rows(in_got, [token], COVER)
    in_every = home_all(in_here)
    two, token = halve_more([two], rows_two, [token])
    out, token = home_last(out_every, BF, [token])
    g_in, g_out, token = finish(ffn, ((0, prows),) * 2, [], [token])
    sums, token = spread(one + two, [token])
    grad_memory, token = home_last(mem_every, F32, [token])
    grad_inputs, token = home_last(in_every, F32, [token])
    gqc, gkc, gqs, goc, gvc, gos, gks, gvs, g_gains, g_shifts, g_bias, _ = finish(
        sums, ((0, prows),) * 8 + ((2, 16),),
        [struct(gains.shape, F32), struct(shifts.shape, F32), struct((1, blen), F32)], [token],
    )
    return (
        out, grad_inputs, grad_memory, gqs, gks, gvs, gos.T, gqc, gkc, gvc, goc.T,
        g_in, g_out.T, g_gains, g_shifts, g_bias.reshape(-1),
    )


def solution(mesh):
    sizes = mesh.devices.shape
    inner = jax.sharding.Mesh(
        mesh.devices.reshape(sizes[0], sizes[1], sizes[2] // 2, 2), ALL
    )
    rows = P("dp", "ctx", None)
    tp = ("ty", "tc")
    col = P(("dp", "ctx"), tp)
    row = P(tp, ("dp", "ctx"))
    small = P(None, ALL)
    weights = (col, col, col, row, col, col, col, row, col, row)
    tail = (small, small, P(ALL))
    return jax.shard_map(
        shards,
        mesh=inner,
        in_specs=(rows, rows, rows) + weights + tail,
        out_specs=(rows, rows, rows) + weights + tail,
        check_vma=False,
    )
```

```python
import functools

import jax
import jax.numpy as jnp
from jax import lax
from jax.experimental import pallas as pl
from jax.experimental.pallas import tpu as pltpu
from jax.sharding import PartitionSpec as P

HD = 64
EPS = 1e-05
BF = jnp.bfloat16
F32 = jnp.float32
PAIR = 2 * HD
VMEM_LIMIT = 40 << 20
SMALL_LIMIT = 16 << 20
SMALL_COST = 1_000_000_000
COVER = 10 * SMALL_COST
COSTS = dict(
    self_fwd=24_000_000_000, cross_fwd=28_000_000_000, ffn_both=25_000_000_000,
    cross_bwd=30_000_000_000, self_bwd=16_000_000_000, mem_back=9_000_000_000,
    in_back=9_000_000_000,
)
GELU_C = 0.7978845608028654
GELU_A = 0.044715


def nn(left, right):
    return lax.dot_general(left, right, (((1,), (0,)), ((), ())), preferred_element_type=F32)


def nt(left, right):
    return lax.dot_general(left, right, (((1,), (1,)), ((), ())), preferred_element_type=F32)


def norm_stats(z):
    mean = jnp.mean(z, axis=-1, keepdims=True)
    cent = z - mean
    var = jnp.mean(cent * cent, axis=-1, keepdims=True)
    inv = lax.rsqrt(var + EPS)
    return cent * inv, inv


def norm_back(grad, gain, normed, inv):
    e = grad * gain
    me = jnp.mean(e, axis=-1, keepdims=True)
    men = jnp.mean(e * normed, axis=-1, keepdims=True)
    return inv * (e - me - normed * men)


def rows_sum(a):
    return jnp.sum(a, axis=0, keepdims=True)


def split_pair(block):
    lane = lax.broadcasted_iota(jnp.int32, block.shape, 1)
    zero = jnp.zeros_like(block)
    return jnp.concatenate(
        [jnp.where(lane < HD, block, zero), jnp.where(lane < HD, zero, block)], axis=0
    )


def join_pair(both):
    q = both.shape[1] // 2
    row = lax.broadcasted_iota(jnp.int32, (both.shape[0], q), 0)
    return jnp.where(row < HD, both[:, :q], both[:, q:])


def vrow(vec_ref, row):
    return jnp.concatenate([vec_ref[j, row : row + 1] for j in range(vec_ref.shape[0])], axis=1)


def swap(pair):
    return (pair % 2) * 2 + pair // 2


def pick(own_ref, peer_ref, mat, other_half):
    shape = own_ref.shape
    own = own_ref[0, mat].reshape(shape[2] * shape[3], shape[4])
    other = peer_ref[0, mat].reshape(shape[2] * shape[3], shape[4])
    return jnp.where(other_half, other, own)


def put_pieces(ref, at, first, value, ranks_ref):
    n_x, n_z = ref.shape[1], ref.shape[2]
    rows = value.shape[0] // (n_x * n_z)
    for d in range(n_x):
        for z in range(n_z):
            i = d * n_z + z
            ref[at, d ^ ranks_ref[0], z ^ ranks_ref[1], first : first + rows] = value[
                i * rows : (i + 1) * rows
            ]


def attn_fwd_body(
    causal, q_rows, kv_parts, w, biases,
    q_ref, k_ref, v_ref, p_refs, ot_ref, o_ref, il_ref, o_all, wo_all,
):
    wq, wk, wv, wo = w
    kv = nn(kv_parts, jnp.concatenate([wk, wv], axis=1))
    k = kv[:, :PAIR].astype(BF)
    v = (kv[:, PAIR:] + biases[1]).astype(BF)
    q = (nn(q_rows, wq) + biases[0]).astype(BF) * HD ** (-0.5)
    q_ref[0] = q
    k_ref[0] = k
    v_ref[0] = v
    vt = v.T
    blocks = len(p_refs)
    rows = q.shape[0] // blocks
    keys = k.shape[0]
    for b in range(blocks):
        n = keys // blocks * (b + 1) if causal else keys
        scores = nt(k[:n], split_pair(q[b * rows : (b + 1) * rows]))
        if causal:
            last = rows
            lane = lax.broadcasted_iota(jnp.int32, (last, 2 * rows), 1)
            hidden = lane % rows < rows // 2
            scores = jnp.concatenate(
                [scores[: n - last], jnp.where(hidden, -1e30, scores[n - last :])], axis=0
            )
        top = jnp.max(scores, axis=0, keepdims=True)
        p = jnp.exp(scores - top)
        inv = 1.0 / jnp.sum(p, axis=0, keepdims=True)
        pb = p.astype(BF)
        p_refs[b][0] = pb
        ot = join_pair(nn(vt[:, :n], pb) * inv)
        span = slice(b * rows, (b + 1) * rows)
        ot_ref[0, :, span] = ot.astype(BF)
        o_ref[0, span, :] = ot.T.astype(BF)
        il_ref[0, 0:1, span] = inv[:, :rows]
        il_ref[0, 1:2, span] = inv[:, rows:]
    s = pl.program_id(0)
    o_all[s] = o_ref[0]
    wo_all[s] = wo


def wide(ref):
    return jnp.concatenate([ref[i] for i in range(ref.shape[0])], axis=1)


def finish_norm(z, n_ref, r_ref):
    normed, inv = norm_stats(z)
    n_ref[...] = normed
    r_ref[...] = jnp.broadcast_to(inv, r_ref.shape)


def self_fwd(ranks_ref, xo_ref, xp_ref, wa_ref, wb_ref, va_ref, vb_ref, *refs):
    saved, (n_ref, r_ref, vec_ref, bias_ref, x_all, acc_ref, o_all, wo_all) = refs[:8], refs[8:]
    q_ref, k_ref, v_ref, *p_refs, ot_ref, o_ref, il_ref = saved
    s = pl.program_id(0)
    blocks = 4
    half = xo_ref.shape[0] // blocks
    tiles = vec_ref.shape[0]

    @pl.when(s == 0)
    def _():
        for b in range(blocks):
            x_all[2 * b * half : (2 * b + 1) * half] = xo_ref[b * half : (b + 1) * half]
            x_all[(2 * b + 1) * half : (2 * b + 2) * half] = xp_ref[b * half : (b + 1) * half]
        both = va_ref[...].astype(F32) + vb_ref[...].astype(F32)
        vec_ref[...] = both[:tiles]
        bias_ref[...] = both[tiles]
        acc_ref[...] = xo_ref[...].astype(F32) + vrow(vec_ref, 5)

    w = [pick(wa_ref, wb_ref, i, s >= 2) for i in range(4)]
    t = swap(s) ^ ranks_ref[4]
    attn_fwd_body(True, xo_ref[...], x_all[...], w, (vec_ref[t, 3:4], vec_ref[t, 4:5]),
                  q_ref, k_ref, v_ref, p_refs, ot_ref, o_ref, il_ref, o_all, wo_all)

    @pl.when(s == pl.num_programs(0) - 1)
    def _():
        finish_norm(acc_ref[...] + nt(wide(o_all), wide(wo_all)), n_ref, r_ref)


def cross_fwd(ranks_ref, n1_ref, mo_ref, mp_ref, wa_ref, wb_ref, vec_ref, *refs):
    saved, (n_ref, r_ref, m_all, h_low, acc_ref, o_all, wo_all) = refs[:7], refs[7:]
    q_ref, k_ref, v_ref, *p_refs, ot_ref, o_ref, il_ref = saved
    s = pl.program_id(0)
    half = mo_ref.shape[0]

    @pl.when(s == 0)
    def _():
        m_all[:half] = mo_ref[...]
        m_all[half:] = mp_ref[...]
        h1 = n1_ref[...] * vrow(vec_ref, 0) + vrow(vec_ref, 6)
        h_low[...] = h1.astype(BF)
        acc_ref[...] = h1 + vrow(vec_ref, 9)

    w = [pick(wa_ref, wb_ref, i, s >= 2) for i in range(4)]
    t = swap(s) ^ ranks_ref[4]
    attn_fwd_body(False, h_low[...], m_all[...], w, (vec_ref[t, 7:8], vec_ref[t, 8:9]),
                  q_ref, k_ref, v_ref, p_refs, ot_ref, o_ref, il_ref, o_all, wo_all)

    @pl.when(s == pl.num_programs(0) - 1)
    def _():
        finish_norm(acc_ref[...] + nt(wide(o_all), wide(wo_all)), n_ref, r_ref)


def ffn_both(ranks_ref, n2_ref, r2_ref, c0, c1, c2, c3, w_ref, bias_ref, vec_ref,
             h0, h1, h2, h3, keep_ref, send_ref, dz2_ref, vg_ref, bg_ref,
             h_low, h_t, act, slope, acc, dz3_low, dz3_t, dh2):
    phase = pl.program_id(0)
    t = pl.program_id(1)
    d = n2_ref.shape[1]
    last = pl.num_programs(1) - 1
    w_in = w_ref[:, 0, 0].reshape(d, -1)
    w_out = w_ref[:, 0, 1].reshape(d, -1)
    hid = w_in.shape[1]
    strips = hid // PAIR

    @pl.when((phase == 0) & (t == 0))
    def _():
        h = n2_ref[...] * vrow(vec_ref, 1) + vrow(vec_ref, 10)
        h_low[...] = h.astype(BF)
        h_t[...] = h.astype(BF).T
        acc[...] = h + vrow(vec_ref, 11)

    @pl.when(phase == 0)
    def _():
        bias = jnp.concatenate(
            [bias_ref[pl.ds(t * strips + j, 1), :] for j in range(strips)], axis=1
        )
        u = nn(h_low[...], w_in) + bias
        cube = GELU_A * u * u
        th = jnp.tanh(GELU_C * u * (1.0 + cube))
        low = 0.5 * (1.0 + th)
        f = (u * low).astype(BF)
        act[t] = f
        slope[t] = low + 0.5 * u * (1.0 - th * th) * (GELU_C * (1.0 + 3.0 * cube))
        acc[...] += nt(f, w_out)

    @pl.when((phase == 0) & (t == last))
    def _():
        n3, r3 = norm_stats(acc[...])
        acc[...] = n3 * vrow(vec_ref, 2) + vrow(vec_ref, 12)
        put_home(acc, (h0, h1, h2, h3), ranks_ref)
        for r, ref in enumerate((c0, c1, c2, c3)):
            rows = ref.shape[0]
            at = pl.multiple_of((r ^ ranks_ref[1]) * rows, rows)
            dh2[pl.ds(at, rows), :] = ref[...].astype(F32)
        g = dh2[...]
        vg_ref[0:1] = rows_sum(g * n3)
        vg_ref[1:2] = rows_sum(g)
        dz3 = norm_back(g, vrow(vec_ref, 2), n3, r3)
        vg_ref[2:3] = rows_sum(dz3)
        low = dz3.astype(BF)
        dz3_low[...] = low
        dz3_t[...] = low.T
        dh2[...] = dz3

    @pl.when(phase == 1)
    def _():
        f = act[t]
        df = nn(dz3_low[...], w_out).astype(BF).astype(F32)
        du = (df * slope[t]).astype(BF)
        g_out = nn(dz3_t[...], f).astype(BF)
        g_in = nn(h_t[...], du).astype(BF)
        sums = rows_sum(du.astype(F32))
        for j in range(strips):
            bg_ref[pl.ds(t * strips + j, 1), :] = sums[:, j * PAIR : (j + 1) * PAIR]
        dh2[...] += nt(du, w_in)
        mine = t % 2 == ranks_ref[3]
        piece = keep_ref.shape[3] // 2

        @pl.when(mine)
        def _():
            put_pieces(keep_ref, 0, 0, g_in, ranks_ref)
            put_pieces(keep_ref, 0, piece, g_out, ranks_ref)

        @pl.when(jnp.logical_not(mine))
        def _():
            put_pieces(send_ref, 0, 0, g_in, ranks_ref)
            put_pieces(send_ref, 0, piece, g_out, ranks_ref)

    @pl.when((phase == 1) & (t == last))
    def _():
        g = dh2[...]
        n2 = n2_ref[...]
        vg_ref[3:4] = rows_sum(g * n2)
        vg_ref[4:5] = rows_sum(g)
        dz2 = norm_back(g, vrow(vec_ref, 1), n2, r2_ref[:, 0:1])
        vg_ref[5:6] = rows_sum(dz2)
        vg_ref[6:8] = jnp.zeros_like(vg_ref[6:8])
        dz2_ref[...] = dz2


def put_home(acc, refs, ranks_ref):
    rows = refs[0].shape[0]
    for r, ref in enumerate(refs):
        at = pl.multiple_of((r ^ ranks_ref[1]) * rows, rows)
        ref[...] = acc[pl.ds(at, rows), :].astype(BF)


def self_bwd(ranks_ref, act_ref, dz_ref, part_ref, w_ref, *refs):
    saved, (slot_ref, own_ref, peer_ref, out_ref, qg_ref, *scratch) = refs[:8], refs[8:]
    shape = w_ref.shape
    w = [w_ref[0, i].reshape(shape[2] * shape[3], shape[4]) for i in (0, 3)]

    def first():
        dz = dz_ref[...]
        return act_ref[...].T, dz, part_ref[...]

    def store(g_q, g_o, piece):
        put_pieces(slot_ref, 0, 0, g_q, ranks_ref)
        put_pieces(slot_ref, 0, piece, g_o, ranks_ref)

    def last(total):
        out_ref[...] = total

    attn_bwd(True, first, w, saved, store, last, slot_ref.shape[3] // 2,
             own_ref, peer_ref, qg_ref, *scratch)


def cross_bwd(ranks_ref, n_ref, r_ref, dz_ref, wa_ref, wb_ref, vec_ref, *refs):
    saved = refs[:7]
    keep_ref, send_ref, own_ref, peer_ref, out_ref, vg_ref, qg_ref, *scratch = refs[7:]
    s = pl.program_id(0)
    odd = s >= 2

    def first():
        h = n_ref[...] * vrow(vec_ref, 0) + vrow(vec_ref, 6)
        dz = dz_ref[...]
        return h.astype(BF).T, dz, dz

    def store(g_q, g_o, piece):
        @pl.when(jnp.logical_not(odd))
        def _():
            put_pieces(keep_ref, 0, 0, g_q, ranks_ref)
            put_pieces(keep_ref, 0, piece, g_o, ranks_ref)

        @pl.when(odd)
        def _():
            put_pieces(send_ref, 0, 0, g_q, ranks_ref)
            put_pieces(send_ref, 0, piece, g_o, ranks_ref)

    def last(g):
        normed = n_ref[...]
        vg_ref[0:1] = rows_sum(g * normed)
        vg_ref[1:2] = rows_sum(g)
        dz1 = norm_back(g, vrow(vec_ref, 0), normed, r_ref[:, 0:1])
        vg_ref[2:3] = rows_sum(dz1)
        vg_ref[3:8] = jnp.zeros_like(vg_ref[3:8])
        out_ref[...] = dz1

    w = [pick(wa_ref, wb_ref, i, odd) for i in (0, 3)]
    attn_bwd(False, first, w, saved, store, last, keep_ref.shape[3] // 2,
             own_ref, peer_ref, qg_ref, *scratch)


def attn_bwd(causal, first, w, saved, store, last, piece, own_ref, peer_ref, qg_ref,
             dy, dy_t, act_t, acc, dk_ref, dv_ref, dq_all, wq_all):
    s = pl.program_id(0)
    q_ref, k_ref, v_ref, *p_refs, ot_ref, o_ref, il_ref = saved
    blocks = len(p_refs)
    wq, wo = w

    @pl.when(s == 0)
    def _():
        act_t[...], dz, acc[...] = first()
        low = dz.astype(BF)
        dy[...] = low
        dy_t[...] = low.T

    q = q_ref[0]
    k = k_ref[0]
    v = v_ref[0]
    keys = k.shape[0]
    rows = q.shape[0] // blocks
    do = nn(dy[...], wo).astype(BF)
    g_o = nn(dy_t[...], o_ref[0]).astype(BF)
    do_t = do.T.astype(F32)
    prod = do_t * ot_ref[0].astype(F32)
    inv_a, inv_b = il_ref[0, 0:1], il_ref[0, 1:2]
    inner_a = jnp.sum(prod[:HD], axis=0, keepdims=True) * inv_a
    inner_b = jnp.sum(prod[HD:], axis=0, keepdims=True) * inv_b
    row = lax.broadcasted_iota(jnp.int32, do_t.shape, 0)
    dos = (do_t * jnp.where(row < HD, inv_a, inv_b)).astype(BF).T
    kt = k.T
    dqs = [None] * blocks
    for b in reversed(range(blocks)):
        n = keys // blocks * (b + 1) if causal else keys
        span = slice(b * rows, (b + 1) * rows)
        dob = split_pair(dos[span])
        qb = split_pair(q[span])
        pb = p_refs[b][0]
        dp = nt(v[:n], dob)
        inner = jnp.concatenate([inner_a[:, span], inner_b[:, span]], axis=1)
        ds = (pb.astype(F32) * (dp - inner)).astype(BF)
        dv = nn(pb, dob)
        dk = nn(ds, qb)
        if b == blocks - 1:
            dv_ref[...] = dv
            dk_ref[...] = dk
        else:
            dv_ref[:n] += dv
            dk_ref[:n] += dk
        dqs[b] = (join_pair(nn(kt[:, :n], ds)) * HD ** (-0.5)).T.astype(BF)
    dq = jnp.concatenate(dqs, axis=0)
    g_q = nn(act_t[...], dq).astype(BF)
    store(g_q, g_o, piece)
    qg_ref[0] = rows_sum(dq.astype(F32))
    dq_all[s] = dq
    wq_all[s] = wq
    for i, ref in enumerate((dk_ref, dv_ref)):
        if causal:
            part = keys // 8
            for b in range(4):
                at, to = 2 * b * part, slice(b * part, (b + 1) * part)
                own_ref[i, 0, to] = ref[at : at + part].astype(BF)
                peer_ref[i, 0, to] = ref[at + part : at + 2 * part].astype(BF)
        else:
            own_ref[i, 0] = ref[: keys // 2].astype(BF)
            peer_ref[i, 0] = ref[keys // 2 :].astype(BF)

    @pl.when(s == pl.num_programs(0) - 1)
    def _():
        last(acc[...] + nt(wide(dq_all), wide(wq_all)))


def kv_back(final, lanes, blen, ranks_ref, act_ref, *refs):
    (wk_own, wv_own, wk_peer, wv_peer), rest = refs[:4], refs[4:]
    if final:
        (own_low, got_low, own_hi, got_hi, base_ref, vgc_ref, vgf_ref, bg_ref, qgs_ref, qgs_hi,
         qgc_ref, vg_mem_ref, h0, h1, h2, h3, keep_ref, send_ref, acc, tiles) = rest
        parts = [(own_low, 0, got_low, 0), (own_low, 1, got_low, 1),
                 (own_hi, 0, got_hi, 0), (own_hi, 1, got_hi, 1)]
    else:
        own_ref, got_ref, h0, h1, h2, h3, keep_ref, send_ref, vgrad_ref, acc = rest
        parts = [(own_ref, s, got_ref, s ^ 2) for s in range(4)]
    pairs = len(parts)
    d = act_ref.shape[1]

    def gathered(own, i, got, j, kind):
        return (own[kind, i].astype(F32) + got[kind, j].astype(F32)).astype(BF)

    def weight(ref, ry):
        return ref[ry, 0].reshape(d, PAIR)

    dkv = [gathered(*part, kind) for part in parts for kind in range(2)]
    wkv = [weight(ref, ry) for refs in ((wk_own, wv_own), (wk_peer, wv_peer))
           for ry in range(2) for ref in refs]
    dkv_all = jnp.concatenate(dkv, axis=1)
    gkv = nn(act_ref[...].T, dkv_all).astype(BF)
    total = nt(dkv_all, jnp.concatenate(wkv, axis=1))
    acc[...] = total + base_ref[...] if final else total
    put_home(acc, (h0, h1, h2, h3), ranks_ref)
    n_x, n_z = keep_ref.shape[1], keep_ref.shape[2]
    piece = d // (n_x * n_z)
    for s in range(pairs):
        ref = keep_ref if s < 2 else send_ref
        for kind in range(2):
            at = (2 * s + kind) * PAIR
            put_pieces(ref, s % 2, kind * piece, gkv[:, at : at + PAIR], ranks_ref)
    sums = [rows_sum(dkv[2 * s + 1].astype(F32)) for s in range(pairs)]
    if not final:
        for s in range(pairs):
            vgrad_ref[s] = sums[s]
        return
    for j in range(pairs):
        at = slice(j * PAIR, (j + 1) * PAIR)
        rel = swap(j ^ ranks_ref[4])
        tiles[j, 0:1] = vgc_ref[0:1, at]
        tiles[j, 1:2] = vgf_ref[3:4, at]
        tiles[j, 2:3] = vgf_ref[0:1, at]
        tiles[j, 3:4] = jnp.where(rel < 2, qgs_ref[rel % 2], qgs_hi[rel % 2])
        tiles[j, 5:6] = vgc_ref[2:3, at]
        tiles[j, 6:7] = vgc_ref[1:2, at]
        tiles[j, 7:8] = qgc_ref[rel]
        tiles[j, 8:9] = vg_mem_ref[rel]
        tiles[j, 9:10] = vgf_ref[5:6, at]
        tiles[j, 10:11] = vgf_ref[4:5, at]
        tiles[j, 11:12] = vgf_ref[2:3, at]
        tiles[j, 12:13] = vgf_ref[1:2, at]
        tiles[j, 13:16] = jnp.zeros((3, PAIR), F32)
    for s in range(pairs):
        tiles[swap(s) ^ ranks_ref[4], 4:5] = sums[s]
    rows_at = lax.broadcasted_iota(jnp.int32, (16, PAIR), 0)
    for ry in range(2):
        for rc, ref in enumerate((keep_ref, send_ref)):
            for i in range(n_x):
                for k in range(n_z):
                    dc = (i ^ ranks_ref[0]) * n_z + (k ^ ranks_ref[1])
                    p = dc * pairs + ((2 * ry + rc) ^ ranks_ref[4])
                    tile = tiles[lax.div(p * lanes, PAIR)]
                    bias = bg_ref[pl.ds(lax.div(p * blen, PAIR), 1), :]
                    both = jnp.where(rows_at == 13, bias, tile).astype(BF)
                    ref[ry, i, k, 2 * piece : 2 * piece + 16] = both


def pack_rows(*refs):
    ins, outs = refs[1 : 1 + len(refs) // 2], refs[1 + len(refs) // 2 :]
    for ref, out in zip(ins, outs):
        out[...] = ref[0]


def pack_rest(*refs):
    for ref, out in zip(refs[1:9], refs[9:17]):
        out[...] = ref[0]


def pack_weights(lanes, blen, ranks_ref, wqs, wks, wvs, wos, wqc, wkc, wvc, woc, win, wout,
                 gains, shifts, bias, s_ref, c_ref, f_ref, va, vb):
    f_ref[0] = win[...]
    f_ref[1] = wout[...]
    n = wqs.shape[0]
    for i, ref in enumerate((wqc, wkc, wvc, woc)):
        c_ref[i * n : (i + 1) * n] = ref[...]
    for i, ref in enumerate((wqs, wks, wvs, wos)):
        s_ref[i * n : (i + 1) * n] = ref[...]
    p = (ranks_ref[0] * 4 + ranks_ref[1]) * 4 + ranks_ref[4]
    at = 4 * n
    va[...] = jnp.zeros_like(va)
    va[0:3, 0:lanes] = gains[...].astype(F32)
    va[3:13, 0:lanes] = shifts[...].astype(F32)
    s_ref[at : at + 16] = pltpu.roll(va[...], lax.rem(p * lanes, PAIR), 1).astype(BF)
    vb[...] = jnp.zeros_like(vb)
    vb[pl.ds(lax.div(p * blen, PAIR), 1), 0:blen] = bias[...].astype(F32)
    s_ref[at + 16 : at + 32] = pltpu.roll(vb[...], lax.rem(p * blen, PAIR), 1).astype(BF)


def whole(a):
    return pl.BlockSpec(a.shape, lambda *_: (0,) * len(a.shape))


def without(body, at, count):
    return lambda *refs: body(*refs[:at], *refs[at + count :])


def launch(body, name, grid, ranks, ins, outs, scratch=(), deps=(), limit=VMEM_LIMIT, cost=SMALL_COST):
    first = 0 if ranks is None else 1
    deps = list(deps)
    n_in, n_out = first + len(ins), len(outs)

    def with_token(*refs):
        kept = refs[:n_in] + refs[n_in + len(deps) :]
        kept[n_in + n_out][...] = jnp.zeros((8, PAIR), F32)
        body(*kept[: n_in + n_out], *kept[n_in + n_out + 1 :])

    token = struct((8, PAIR), F32)
    call = pl.pallas_call(
        with_token,
        grid_spec=pltpu.PrefetchScalarGridSpec(
            num_scalar_prefetch=first,
            grid=grid,
            in_specs=[i[1] for i in ins] + [pl.BlockSpec(memory_space=pl.ANY)] * len(deps),
            out_specs=tuple(o[1] for o in outs) + (whole(token),),
            scratch_shapes=list(scratch),
        ),
        out_shape=tuple(
            pltpu.HBM(o[0].shape, o[0].dtype) if len(o) > 2 else o[0] for o in outs
        ) + (token,),
        compiler_params=pltpu.CompilerParams(
            vmem_limit_bytes=limit, dimension_semantics=("arbitrary",) * len(grid)
        ),
        cost_estimate=pl.CostEstimate(flops=cost, bytes_accessed=1, transcendentals=0),
        name=name,
    )
    args = [
        pltpu.with_memory_space_constraint(i[0], pltpu.HBM) if len(i) > 2 else i[0] for i in ins
    ] + deps
    return call(*args) if ranks is None else call(ranks, *args)


def local(body, name, outs, *ins, ranks=None, scratch=(), deps=(), pinned=(), limit=SMALL_LIMIT,
          cost=SMALL_COST):
    return launch(
        body, name, (1,), ranks, [(a, whole(a)) for a in ins],
        [(o, whole(o), True) if i in pinned else (o, whole(o)) for i, o in enumerate(outs)],
        scratch, deps, limit, cost,
    )


def struct(shape, dtype):
    return jax.ShapeDtypeStruct(shape, dtype)


def restack(ins, outs, cuts):
    for out, (lo, hi) in zip(outs, cuts):
        for r, ref in enumerate(ins):
            out[0, 0, r] = ref[lo:hi]


def double(own, got, out, axis):
    m = own.shape[axis]
    if axis == 0:
        out[:m] = own[...]
        out[m:] = got[...]
    else:
        out[:, :m] = own[...]
        out[:, m:] = got[...]


def order(ranks_ref, parts, outs):
    for r, ref in enumerate(parts):
        rows = ref.shape[-2]
        at = pl.multiple_of((r ^ ranks_ref[1]) * rows, rows)
        for i, out in enumerate(outs):
            out[pl.ds(at, rows), :] = ref[...] if len(outs) == 1 else ref[i]


def assemble(lanes, ranks_ref, a0, a1, b0, b1, w_ref, v_ref=None, scr=None):
    pairs = 4
    n_x, n_z = a0.shape[1], a0.shape[2]
    prows = w_ref.shape[3]
    if v_ref is not None:
        scr[...] = jnp.zeros_like(scr)
    for ry in range(2):
        a_ref = (a0, a1)[ry]
        for i in range(n_x):
            for k in range(n_z):
                dc = (i ^ ranks_ref[0]) * n_z + (k ^ ranks_ref[1])
                b_ref, bi = (b0, i) if i < n_x // 2 else (b1, i - n_x // 2)
                for m in range(2):
                    span = slice(m * prows, (m + 1) * prows)
                    w_ref[ry, m, dc] = a_ref[0, i, k, span]
                    w_ref[ry, 2 + m, dc] = b_ref[ry, bi, k, span]
                if v_ref is not None:
                    at = 2 * prows
                    p = dc * pairs + ((2 * ry) ^ ranks_ref[4])
                    tile = lax.div(p * lanes, PAIR)
                    scr[tile] += b_ref[ry, bi, k, at : at + 16].astype(F32)
                    scr[pairs] += b_ref[ry, bi, k, at + 16 : at + 32].astype(F32)
    if v_ref is not None:
        v_ref[...] = scr[...].astype(BF)


def start_one(cuts, ranks_ref, *refs):
    restack(refs[0:4], refs[8:10], cuts)
    order(ranks_ref, refs[4:8], refs[10:11])


def start_two(axes, cuts, a, ga, b, gb, *refs):
    double(a, ga, refs[4], axes[0])
    double(b, gb, refs[5], axes[1])
    restack(refs[0:4], refs[6:8], cuts)


def start_five(lanes, ranks_ref, *refs):
    assemble(lanes, ranks_ref, *refs[0:4], refs[8])
    order(ranks_ref, refs[4:8], refs[9:10])


def double_both(axes, a, ga, b, gb, out_a, out_b):
    double(a, ga, out_a, axes[0])
    double(b, gb, out_b, axes[1])


def order_home(ranks_ref, *refs):
    order(ranks_ref, refs[:4], refs[4:])


def halve_body(axis_a, axis_b, cuts, *refs):
    ins, (sa, ka, sb, kb) = refs[: len(refs) - 4], refs[len(refs) - 4 :]

    def place(axis, send, keep, at, value):
        rows = value.shape[3]
        m = value.shape[axis] // 2
        lo = value[:m] if axis == 0 else value[:, :m]
        hi = value[m:] if axis == 0 else value[:, m:]
        keep[:, :, :, at : at + rows] = lo
        send[:, :, :, at : at + rows] = hi.astype(BF)

    at_a = at_b = 0
    for cut in cuts:
        if cut is None:
            keep_a, got_a, keep_b, got_b, *ins = ins
            parts = (keep_a[...] + got_a[...].astype(F32), keep_b[...] + got_b[...].astype(F32))
        else:
            keep, got, *ins = ins
            total = keep[...].astype(F32) + got[...].astype(F32)
            parts = (total[:, :, :, :cut], total[:, :, :, cut:])
        place(axis_a, sa, ka, at_a, parts[0])
        place(axis_b, sb, kb, at_b, parts[1])
        at_a += parts[0].shape[3]
        at_b += parts[1].shape[3]


def spread_body(*refs):
    ins, (s1, s2, s3, keep) = refs[:-4], refs[-4:]
    at = 0
    for own, got in zip(ins[::2], ins[1::2]):
        rows = own.shape[3]
        for r, ref in enumerate((keep, s1, s2, s3)):
            total = own[0, 0, r] + got[0, 0, r].astype(F32)
            ref[at : at + rows] = total.astype(ref.dtype)
        at += rows


def finish_body(plan, lanes, blen, ranks_ref, keep, r1, r2, r3, *outs):
    total = keep[...] + r1[...].astype(F32) + r2[...].astype(F32) + r3[...].astype(F32)
    at = 0
    outs = list(outs)
    for turn, rows in plan:
        part = total[at : at + rows]
        at += rows
        if turn == 2:
            p = (ranks_ref[0] * 4 + ranks_ref[1]) * 4 + ranks_ref[4]
            vec = pltpu.roll(part, lax.rem(PAIR - lax.rem(p * lanes, PAIR), PAIR), 1)
            outs.pop(0)[...] = vec[0:3, :lanes]
            outs.pop(0)[...] = vec[3:13, :lanes]
            own = pltpu.roll(part, lax.rem(PAIR - lax.rem(p * blen, PAIR), PAIR), 1)
            outs.pop(0)[...] = own[13:14, :blen]
        else:
            outs.pop(0)[...] = part


def home_body(every, out_ref):
    n_c, n_z, rows, _ = every.shape
    for c in range(n_c):
        for z in range(n_z):
            out_ref[z, c * rows : (c + 1) * rows, :] = every[c, z].astype(out_ref.dtype)


def half_spec(w, other):
    if other:
        return pl.BlockSpec((1,) + w.shape[1:], lambda s, _: (jnp.maximum(s - 2, 0), 0, 0, 0, 0))
    return pl.BlockSpec((1,) + w.shape[1:], lambda s, _: (jnp.minimum(s, 1), 0, 0, 0, 0))


def slot_outs(n_x, n_z, rows):
    shape = struct((2, n_x, n_z, rows, PAIR), BF)
    block = (1, n_x, n_z, rows, PAIR)
    return [
        (shape, pl.BlockSpec(block, lambda s, _: (jnp.minimum(s, 1), 0, 0, 0, 0))),
        (shape, pl.BlockSpec(block, lambda s, _: (jnp.maximum(s - 2, 0), 0, 0, 0, 0))),
    ]


def full(shape):
    return pl.BlockSpec(shape, lambda *_: (0,) * len(shape))


def run_attn_fwd(causal, ranks, rows_in, w_own, w_peer, vecs, pairs, deps):
    own, d = rows_in[0].shape
    keys = 2 * own
    blocks = 2 if causal else 1
    ns = [keys // blocks * (b + 1) if causal else keys for b in range(blocks)]
    qn = 2 * own // blocks

    def saved(shape, dtype):
        return (struct((pairs,) + shape, dtype),
                pl.BlockSpec((1,) + shape, lambda s, _: (s, 0, 0)), True)

    outs = [
        saved((own, PAIR), BF), saved((keys, PAIR), BF), saved((keys, PAIR), BF),
        *[saved((n, qn), BF) for n in ns],
        saved((PAIR, own), BF), saved((own, PAIR), BF), saved((8, own), F32),
        (struct((own, d), F32), full((own, d))),
        (struct((own, PAIR), F32), full((own, PAIR))),
    ]
    if causal:
        outs.append((struct((pairs, 16, PAIR), F32), full((pairs, 16, PAIR))))
        outs.append((struct((16, PAIR), F32), full((16, PAIR))))
    ins = [(a, whole(a)) for a in rows_in]
    ins += [(w_own, half_spec(w_own, False), True), (w_peer, half_spec(w_peer, True), True)]
    ins += [(a, whole(a)) for a in vecs]
    scratch = [pltpu.VMEM((keys, d), BF)] + ([] if causal else [pltpu.VMEM((own, d), BF)])
    scratch.append(pltpu.VMEM((own, d), F32))
    scratch += [pltpu.VMEM((pairs, own, PAIR), BF), pltpu.VMEM((pairs, d, PAIR), BF)]

    return launch(
        self_fwd if causal else cross_fwd, "self_fwd" if causal else "cross_fwd",
        (pairs,), ranks, ins, outs, scratch, deps,
        cost=COSTS["self_fwd" if causal else "cross_fwd"],
    )


def run_ffn(ranks, n2, r2, cots, w, bias, vec, n_x, n_z):
    own, d = n2.shape
    dc, parts, _, prows, hid = w.shape
    half = own // 4
    back = lambda p, t, ref: ((p * (t // 2)) ^ ref[2], 0, 0, 0, 0)
    slots = struct((2, n_x, n_z, 2 * prows, hid), BF)
    slot_block = pl.BlockSpec((1, n_x, n_z, 2 * prows, hid), back)
    outs = [(struct((half, d), BF), full((half, d)))] * 4 + [
        (slots, slot_block),
        (slots, slot_block),
        (struct((own, d), F32), full((own, d))),
        (struct((8, d), F32), full((8, d))),
        (struct((16, PAIR), F32), full((16, PAIR))),
    ]
    ins = [(n2, whole(n2)), (r2, whole(r2))] + [(c, whole(c)) for c in cots] + [
        (w, pl.BlockSpec((dc, 1, 2, prows, hid), lambda p, t, _: (0, t, 0, 0, 0)), True),
        (bias, whole(bias)),
        (vec, whole(vec)),
    ]
    scratch = [
        pltpu.VMEM((own, d), BF),
        pltpu.VMEM((d, own), BF),
        pltpu.VMEM((parts, own, hid), BF),
        pltpu.VMEM((parts, own, hid), F32),
        pltpu.VMEM((own, d), F32),
        pltpu.VMEM((own, d), BF),
        pltpu.VMEM((d, own), BF),
        pltpu.VMEM((own, d), F32),
    ]
    return launch(
        ffn_both, "ffn_both", (2, parts), ranks, ins, outs, scratch,
        cost=COSTS["ffn_both"],
    )


def bwd_scratch(own, keys, d, pairs):
    return [
        pltpu.VMEM((own, d), BF),
        pltpu.VMEM((d, own), BF),
        pltpu.VMEM((d, own), BF),
        pltpu.VMEM((own, d), F32),
        pltpu.VMEM((keys, PAIR), F32),
        pltpu.VMEM((keys, PAIR), F32),
        pltpu.VMEM((pairs, own, PAIR), BF),
        pltpu.VMEM((pairs, d, PAIR), BF),
    ]


def per_pair(a, first=0):
    return (a, pl.BlockSpec((1,) + a.shape[1:], lambda s, _: (s + first, 0, 0)), True)


def run_cross_bwd(ranks, dz, w_own, w_peer, vec, saved, n, r, n_x, n_z, deps):
    pairs, own, _ = saved[0].shape
    keys = saved[1].shape[1]
    d = dz.shape[1]
    prows = w_own.shape[3]
    kv_spec = pl.BlockSpec((2, 1, own, PAIR), lambda s, _: (0, s, 0, 0))
    outs = slot_outs(n_x, n_z, 2 * prows) + [
        (struct((2, pairs, own, PAIR), BF), kv_spec, True),
        (struct((2, pairs, own, PAIR), BF), kv_spec, True),
        (struct((own, d), F32), full((own, d))),
        (struct((8, d), F32), full((8, d))),
        (struct((pairs, 1, PAIR), F32), pl.BlockSpec((1, 1, PAIR), lambda s, _: (s, 0, 0))),
    ]
    ins = [
        (n, whole(n)),
        (r, whole(r)),
        (dz, whole(dz)),
        (w_own, half_spec(w_own, False), True),
        (w_peer, half_spec(w_peer, True), True),
        (vec, whole(vec)),
        *[per_pair(a) for a in saved],
    ]
    return launch(
        cross_bwd, "cross_bwd", (pairs,), ranks, ins, outs, bwd_scratch(own, keys, d, pairs), deps,
        cost=COSTS["cross_bwd"],
    )


def run_self_bwd(first, ranks, act, dz, part, w, saved, n_x, n_z, deps):
    _, own, _ = saved[0].shape
    keys = saved[1].shape[1]
    d = dz.shape[1]
    prows = w.shape[3]
    pairs = 2
    kv_spec = pl.BlockSpec((2, 1, own, PAIR), lambda s, _: (0, s, 0, 0))
    slots = (1, n_x, n_z, 2 * prows, PAIR)
    outs = [
        (struct((2,) + slots[1:], BF), pl.BlockSpec(slots, lambda s, _: (s, 0, 0, 0, 0))),
        (struct((2, pairs, own, PAIR), BF), kv_spec, True),
        (struct((2, pairs, own, PAIR), BF), kv_spec, True),
        (struct((own, d), F32), full((own, d))),
        (struct((pairs, 1, PAIR), F32), pl.BlockSpec((1, 1, PAIR), lambda s, _: (s, 0, 0))),
    ]
    ins = [
        (act, whole(act)),
        (dz, whole(dz)),
        (part, whole(part)),
        (w, pl.BlockSpec((1,) + w.shape[1:], lambda s, _: (s, 0, 0, 0, 0)), True),
        *[per_pair(a, first) for a in saved],
    ]
    return launch(
        self_bwd, "self_bwd", (pairs,), ranks, ins, outs, bwd_scratch(own, keys, d, pairs), deps,
        cost=COSTS["self_bwd"],
    )


def run_kv_back(name, ranks, act, parts, w_own, w_peer, extra, lanes, blen, n_x, n_z, deps):
    own, d = act.shape
    pairs = 2 * w_own.shape[0]
    prows = w_own.shape[3]
    final = bool(extra)
    rows = 2 * prows + (16 if final else 0)
    half = own // 4
    slots = struct((2, n_x, n_z, rows, PAIR), BF)
    outs = [(struct((half, d), BF), full((half, d)))] * 4 + [(slots, whole(slots))] * 2
    scratch = [pltpu.VMEM((own, d), F32)]
    if final:
        scratch.append(pltpu.VMEM((pairs, 16, PAIR), F32))
    else:
        outs.append((struct((pairs, 1, PAIR), F32), full((pairs, 1, PAIR))))

    def mat(w, i):
        block = (w.shape[0], 1) + w.shape[2:]
        return (w, pl.BlockSpec(block, lambda *_: (0, i, 0, 0, 0)), True)

    ins = [
        (act, whole(act)),
        mat(w_own, 1), mat(w_own, 2), mat(w_peer, 1), mat(w_peer, 2),
        *[(a, whole(a), True) for a in parts],
        *[(a, whole(a)) for a in extra],
    ]
    return launch(
        functools.partial(kv_back, final, lanes, blen), name, (1,), ranks, ins, outs,
        scratch, deps, cost=COSTS[name],
    )


ALL = ("dp", "ctx", "ty", "tc")


def shards(
    inputs, memory, cotangent, wq_self, wk_self, wv_self, wo_self, wq_cross, wk_cross, wv_cross,
    wo_cross, w_in, w_out, gains, shifts, ffn_bias,
):
    seqs, block, d = inputs.shape
    n_x, n_z, n_y, n_c = (lax.axis_size(a) for a in ALL)
    pairs = n_y * n_c
    half = block // n_c
    own = n_z * half
    x_rank, z_rank, y_rank, c_rank = (lax.axis_index(a) for a in ALL)
    ranks = jnp.stack([x_rank, z_rank, y_rank, c_rank, y_rank * n_c + c_rank]).astype(jnp.int32)
    prows, lanes, blen = wq_self.shape[0], gains.shape[1], ffn_bias.shape[0]
    hid = w_in.shape[1]
    x_bits = [1 << i for i in range((n_x - 1).bit_length())]

    def send(array, axis, bit):
        return lax.ppermute(array, axis, [(i, i ^ bit) for i in range(lax.axis_size(axis))])

    def rows_of(r):
        return pl.BlockSpec((1, half, d), lambda i, ref: (ref[2] * 4 + (ref[1] ^ r), ref[3], 0))

    def packed_rows(array):
        return [(array, rows_of(r), True) for r in range(n_z)]

    def around_z(parts):
        return [parts[0]] + [send(parts[r], "ctx", r) for r in range(1, n_z)]

    row_part = struct((half, d), BF)

    def sent_rows(array, name, deps):
        *parts, token = launch(
            pack_rows, name, (1,), ranks, packed_rows(array), [(row_part, whole(row_part))] * n_z,
            deps=deps, limit=SMALL_LIMIT,
        )
        return around_z(parts), token

    x_got, token = sent_rows(inputs, "pack_x", [])
    f_shape = struct((2, prows, hid), BF)
    s_pack, c_pack, f_pack, token = local(
        functools.partial(pack_weights, lanes, blen), "pack_weights",
        [struct((4 * prows + 32, PAIR), BF), struct((4 * prows, PAIR), BF), f_shape],
        wq_self, wk_self, wv_self, wo_self.T, wq_cross, wk_cross, wv_cross, wo_cross.T,
        w_in, w_out.T, gains, shifts, ffn_bias.reshape(1, -1), ranks=ranks, deps=[token],
        pinned=(2,),
        scratch=[pltpu.VMEM((16, PAIR), F32), pltpu.VMEM((16, PAIR), F32)],
    )
    s_got = around_z([s_pack] * n_z)
    w_ffn = lax.all_gather(f_pack, ALL, axis=0, tiled=False).reshape(
        n_x * n_z, pairs, 2, prows, hid
    )
    cuts_s = ((0, 2 * prows), (2 * prows, 4 * prows + 32))
    cuts_c = ((0, 2 * prows), (2 * prows, 4 * prows))

    def z_slots(cuts):
        return [struct((1, 1, n_z, hi - lo, PAIR), BF) for lo, hi in cuts]

    def doubled(array, axis):
        shape = list(array.shape)
        shape[axis] *= 2
        return struct(tuple(shape), BF)

    steps_a = [("dp", bit) for bit in x_bits] + [("ty", 1)]
    steps_b = [("ty", 1)] + [("dp", bit) for bit in x_bits]
    axis_of = {"ty": 0, "dp": 1}
    axes_at = [(axis_of[sa[0]], axis_of[sb[0]]) for sa, sb in zip(steps_a, steps_b)]

    def step(i, a, b):
        return [a, send(a, *steps_a[i]), b, send(b, *steps_b[i])]

    def more(ins, deps):
        for i in range(len(steps_a) - 1):
            a, b, token = local(
                functools.partial(double_both, axes_at[i]), "double",
                [doubled(ins[0], axes_at[i][0]), doubled(ins[2], axes_at[i][1])], *ins, deps=deps,
            )
            ins, deps = step(i + 1, a, b), [token]
        return ins, token

    sa, sb, xo, token = local(
        functools.partial(start_one, cuts_s), "start_one",
        z_slots(cuts_s) + [struct((own, d), BF)], *s_got, *x_got, ranks=ranks,
    )
    xp = send(xo, "tc", 1)
    c_got = around_z([c_pack] * n_z)
    sa, sb, ca, cb, token = local(
        functools.partial(start_two, axes_at[0], cuts_c), "start_two",
        [doubled(sa, axes_at[0][0]), doubled(sb, axes_at[0][1])] + z_slots(cuts_c),
        *step(0, sa, sb), *c_got, deps=[token],
    )
    s_last = step(1, sa, sb)
    c_last = step(0, ca, cb)
    for i in range(1, len(steps_a) - 1):
        sa, sb, token = local(
            functools.partial(double_both, axes_at[i]), "double",
            [doubled(s_last[0], axes_at[i][0]), doubled(s_last[2], axes_at[i][1])],
            *s_last, deps=[token],
        )
        s_last = step(i + 1, sa, sb)
    *packed, token = launch(
        pack_rest, "pack_rest", (1,), ranks, packed_rows(memory) + packed_rows(cotangent),
        [(row_part, whole(row_part))] * (2 * n_z), deps=[token], limit=SMALL_LIMIT,
    )
    m_got, cots = around_z(packed[:n_z]), around_z(packed[n_z:])
    w_shape = struct((2, 4, n_x * n_z, prows, PAIR), BF)
    ws_own, v_own, token = local(
        functools.partial(assemble, lanes), "assemble",
        [w_shape, struct((pairs + 1, 16, PAIR), BF)], *s_last, ranks=ranks,
        scratch=[pltpu.VMEM((pairs + 1, 16, PAIR), F32)], deps=[token], pinned=(0,),
    )
    v_peer, ws_peer = send(v_own, "tc", 1), send(ws_own, "tc", 1)
    c_last, token = more(c_last, [token])
    *saved_self, n1, r1, vec, bias, token = run_attn_fwd(
        True, ranks, (xo, xp), ws_own, ws_peer, (v_own, v_peer), pairs, [token]
    )
    wc_own, mo, token = local(
        functools.partial(start_five, lanes), "start_five", [w_shape, struct((own, d), BF)],
        *c_last, *m_got, ranks=ranks, deps=[token], pinned=(0,),
    )
    wc_peer, mp = send(wc_own, "tc", 1), send(mo, "tc", 1)
    *saved_cross, n2, r2, token = run_attn_fwd(
        False, ranks, (n1, mo, mp), wc_own, wc_peer, (vec,), pairs, [token]
    )
    *out_rows, f_keep, f_send, dz2, vg_ffn, bg, token = run_ffn(
        ranks, n2, r2, cots, w_ffn, bias, vec, n_x, n_z
    )

    def home_rows(got, deps, cost=SMALL_COST):
        here, token = local(
            order_home, "order_home", [struct((own, d), BF)], *got, ranks=ranks, deps=deps,
            cost=cost,
        )
        return here.reshape(n_z, half, d), token

    def home_all(here):
        return lax.all_gather(here, ("ty", "tc"), axis=0, tiled=False)

    def home_last(every, dtype, deps):
        return launch(
            home_body, "home", (n_y,), None,
            [(every, pl.BlockSpec((n_c, n_z, half, d), lambda y: (y, 0, 0, 0)), True)],
            [(struct((seqs, block, d), dtype),
              pl.BlockSpec((n_z, block, d), lambda y: (y, 0, 0)), True)],
            deps=deps, limit=2 * SMALL_LIMIT,
        )

    def to_core(*arrays):
        return [send(a, "tc", 1) for a in arrays]

    back_a = [("ty", 1)] + [("dp", bit) for bit in reversed(x_bits)]
    back_b = [("dp", bit) for bit in reversed(x_bits)] + [("ty", 1)]
    rounds = len(back_a)

    def shape_at(i, rows, lanes_in, steps):
        shape = [2, n_x, n_z, rows, lanes_in]
        for axis, _ in steps[: i + 1]:
            shape[axis_of[axis]] //= 2
        return tuple(shape)

    def halve(i, ins, cuts, rows, deps, cost=SMALL_COST):
        width = ins[0].shape[4]
        shape_a = shape_at(i, rows[0], width, back_a)
        shape_b = shape_at(i, rows[1], width, back_b)
        to_a, keep_a, to_b, keep_b, token = local(
            functools.partial(
                halve_body, axis_of[back_a[i][0]], axis_of[back_b[i][0]], cuts
            ),
            "halve",
            [struct(shape_a, BF), struct(shape_a, F32), struct(shape_b, BF), struct(shape_b, F32)],
            *ins, deps=deps, limit=2 * SMALL_LIMIT, cost=cost,
        )
        return [keep_a, send(to_a, *back_a[i]), keep_b, send(to_b, *back_b[i])], token

    def halve_more(groups, rows, deps, cost=SMALL_COST):
        ins, cuts = sum(groups, []), (None,) * len(groups)
        for i in range(1, rounds):
            ins, token = halve(i, ins, cuts, rows, deps, cost)
            cuts, deps = (None,), [token]
        return ins, token

    def spread(ins, deps):
        rows, width = sum(a.shape[3] for a in ins[::2]), ins[0].shape[4]
        *sends, keep, token = local(
            spread_body, "spread",
            [struct((rows, width), BF)] * 3 + [struct((rows, width), F32)], *ins, deps=deps,
        )
        return [keep] + [send(sends[r - 1], "ctx", r) for r in range(1, n_z)], token

    def finish(ins, plan, extra, deps):
        width = ins[0].shape[1]
        outs = [struct((size, width), F32) for turn, size in plan if turn != 2] + extra
        return local(
            functools.partial(finish_body, plan, lanes, blen), "finish", outs, *ins,
            ranks=ranks, deps=deps,
        )

    out_got = around_z(out_rows)
    rows_f = (prows, prows)
    ffn, token = halve(0, [f_keep, to_core(f_send)[0]], (prows,), rows_f, [token])
    c_keep, c_send, c_own, c_peer, dz1, vg_cross, qgc, token = run_cross_bwd(
        ranks, dz2, wc_own, wc_peer, vec, saved_cross, n1, r1, n_x, n_z, [token]
    )
    c_got, c_add = to_core(c_peer, c_send)
    ffn, token = halve_more([ffn], rows_f, [token])
    s_send, own_hi, peer_hi, base, qgs_hi, token = run_self_bwd(
        2, ranks, xo, dz1, dz1, ws_peer, saved_self, n_x, n_z, [token]
    )
    ffn, token = spread(ffn, [token])
    *mem_rows, m_keep, m_send, vgc, token = run_kv_back(
        "mem_back", ranks, mo, (c_own, c_got), wc_own, wc_peer, (), lanes, blen, n_x, n_z, [token]
    )
    mem_got = around_z(mem_rows)
    out_here, token = home_rows(out_got, [token])
    out_every = home_all(out_here)
    got_low, s_add = to_core(peer_hi, s_send)
    s_keep, own_low, peer_low, base, qgs, token = run_self_bwd(
        0, ranks, xo, dz1, base, ws_own, saved_self, n_x, n_z, [token]
    )
    (m_add,) = to_core(m_send)
    rows_one = (3 * prows, 3 * prows)
    one, token = halve(
        0, [c_keep, c_add, m_keep, m_add, s_keep, s_add], (prows,) * 3, rows_one, [token]
    )
    mem_here, token = home_rows(mem_got, [token], COVER)
    mem_every = home_all(mem_here)
    (got_hi,) = to_core(peer_low)
    *in_rows, i_keep, i_send, token = run_kv_back(
        "in_back", ranks, xo, (own_low, got_low, own_hi, got_hi), ws_own, ws_peer,
        (base, vg_cross, vg_ffn, bg, qgs, qgs_hi, qgc, vgc), lanes, blen, n_x, n_z, [token],
    )
    in_got = around_z(in_rows)
    one, token = halve_more([one], rows_one, [token], COVER)
    rows_two = (prows, prows + 16)
    two, token = halve(0, [i_keep, to_core(i_send)[0]], (prows,), rows_two, [token])
    in_here, token = home_rows(in_got, [token], COVER)
    in_every = home_all(in_here)
    two, token = halve_more([two], rows_two, [token])
    out, token = home_last(out_every, BF, [token])
    g_in, g_out, token = finish(ffn, ((0, prows),) * 2, [], [token])
    sums, token = spread(one + two, [token])
    grad_memory, token = home_last(mem_every, F32, [token])
    grad_inputs, token = home_last(in_every, F32, [token])
    gqc, gkc, gqs, goc, gvc, gos, gks, gvs, g_gains, g_shifts, g_bias, _ = finish(
        sums, ((0, prows),) * 8 + ((2, 16),),
        [struct(gains.shape, F32), struct(shifts.shape, F32), struct((1, blen), F32)], [token],
    )
    return (
        out, grad_inputs, grad_memory, gqs, gks, gvs, gos.T, gqc, gkc, gvc, goc.T,
        g_in, g_out.T, g_gains, g_shifts, g_bias.reshape(-1),
    )


def solution(mesh):
    sizes = mesh.devices.shape
    inner = jax.sharding.Mesh(
        mesh.devices.reshape(sizes[0], sizes[1], sizes[2] // 2, 2), ALL
    )
    rows = P("dp", "ctx", None)
    tp = ("ty", "tc")
    col = P(("dp", "ctx"), tp)
    row = P(tp, ("dp", "ctx"))
    small = P(None, ALL)
    weights = (col, col, col, row, col, col, col, row, col, row)
    tail = (small, small, P(ALL))
    return jax.shard_map(
        shards,
        mesh=inner,
        in_specs=(rows, rows, rows) + weights + tail,
        out_specs=(rows, rows, rows) + weights + tail,
        check_vma=False,
    )
```

```python
import functools

import jax
import jax.numpy as jnp
from jax import lax
from jax.experimental import pallas as pl
from jax.experimental.pallas import tpu as pltpu
from jax.sharding import PartitionSpec as P

HD = 64
EPS = 1e-05
BF = jnp.bfloat16
F32 = jnp.float32
PAIR = 2 * HD
VMEM_LIMIT = 40 << 20
SMALL_LIMIT = 16 << 20
SMALL_COST = 1_000_000_000
COVER = 10 * SMALL_COST
COSTS = dict(
    self_fwd=24_000_000_000, cross_fwd=28_000_000_000, ffn_both=25_000_000_000,
    cross_bwd=30_000_000_000, self_bwd=16_000_000_000, mem_back=9_000_000_000,
    in_back=9_000_000_000,
)
GELU_C = 0.7978845608028654
GELU_A = 0.044715


def nn(left, right):
    return lax.dot_general(left, right, (((1,), (0,)), ((), ())), preferred_element_type=F32)


def nt(left, right):
    return lax.dot_general(left, right, (((1,), (1,)), ((), ())), preferred_element_type=F32)


def norm_stats(z):
    mean = jnp.mean(z, axis=-1, keepdims=True)
    cent = z - mean
    var = jnp.mean(cent * cent, axis=-1, keepdims=True)
    inv = lax.rsqrt(var + EPS)
    return cent * inv, inv


def norm_back(grad, gain, normed, inv):
    e = grad * gain
    me = jnp.mean(e, axis=-1, keepdims=True)
    men = jnp.mean(e * normed, axis=-1, keepdims=True)
    return inv * (e - me - normed * men)


def rows_sum(a):
    return jnp.sum(a, axis=0, keepdims=True)


def split_pair(block):
    lane = lax.broadcasted_iota(jnp.int32, block.shape, 1)
    zero = jnp.zeros_like(block)
    return jnp.concatenate(
        [jnp.where(lane < HD, block, zero), jnp.where(lane < HD, zero, block)], axis=0
    )


def join_pair(both):
    q = both.shape[1] // 2
    row = lax.broadcasted_iota(jnp.int32, (both.shape[0], q), 0)
    return jnp.where(row < HD, both[:, :q], both[:, q:])


def vrow(vec_ref, row):
    return jnp.concatenate([vec_ref[j, row : row + 1] for j in range(vec_ref.shape[0])], axis=1)


def swap(pair):
    return (pair % 2) * 2 + pair // 2


def pick(own_ref, peer_ref, mat, other_half):
    shape = own_ref.shape
    own = own_ref[0, mat].reshape(shape[2] * shape[3], shape[4])
    other = peer_ref[0, mat].reshape(shape[2] * shape[3], shape[4])
    return jnp.where(other_half, other, own)


def put_pieces(ref, at, first, value, ranks_ref):
    n_x, n_z = ref.shape[1], ref.shape[2]
    rows = value.shape[0] // (n_x * n_z)
    for d in range(n_x):
        for z in range(n_z):
            i = d * n_z + z
            ref[at, d ^ ranks_ref[0], z ^ ranks_ref[1], first : first + rows] = value[
                i * rows : (i + 1) * rows
            ]


def attn_fwd_body(
    causal, q_rows, kv_parts, w, biases,
    q_ref, k_ref, v_ref, p_refs, ot_ref, o_ref, il_ref, o_all, wo_all,
):
    wq, wk, wv, wo = w
    kv = nn(kv_parts, jnp.concatenate([wk, wv], axis=1))
    k = kv[:, :PAIR].astype(BF)
    v = (kv[:, PAIR:] + biases[1]).astype(BF)
    q = (nn(q_rows, wq) + biases[0]).astype(BF) * HD ** (-0.5)
    q_ref[0] = q
    k_ref[0] = k
    v_ref[0] = v
    vt = v.T
    blocks = len(p_refs)
    rows = q.shape[0] // blocks
    keys = k.shape[0]
    for b in range(blocks):
        n = keys // blocks * (b + 1) if causal else keys
        scores = nt(k[:n], split_pair(q[b * rows : (b + 1) * rows]))
        if causal:
            last = rows
            lane = lax.broadcasted_iota(jnp.int32, (last, 2 * rows), 1)
            hidden = lane % rows < rows // 2
            scores = jnp.concatenate(
                [scores[: n - last], jnp.where(hidden, -1e30, scores[n - last :])], axis=0
            )
        top = jnp.max(scores, axis=0, keepdims=True)
        p = jnp.exp(scores - top)
        inv = 1.0 / jnp.sum(p, axis=0, keepdims=True)
        pb = p.astype(BF)
        p_refs[b][0] = pb
        ot = join_pair(nn(vt[:, :n], pb) * inv)
        span = slice(b * rows, (b + 1) * rows)
        ot_ref[0, :, span] = ot.astype(BF)
        o_ref[0, span, :] = ot.T.astype(BF)
        il_ref[0, 0:1, span] = inv[:, :rows]
        il_ref[0, 1:2, span] = inv[:, rows:]
    s = pl.program_id(0)
    o_all[s] = o_ref[0]
    wo_all[s] = wo


def wide(ref):
    return jnp.concatenate([ref[i] for i in range(ref.shape[0])], axis=1)


def finish_norm(z, n_ref, r_ref):
    normed, inv = norm_stats(z)
    n_ref[...] = normed
    r_ref[...] = jnp.broadcast_to(inv, r_ref.shape)


def self_fwd(ranks_ref, xo_ref, xp_ref, wa_ref, wb_ref, va_ref, vb_ref, *refs):
    saved, (n_ref, r_ref, vec_ref, bias_ref, x_all, acc_ref, o_all, wo_all) = refs[:8], refs[8:]
    q_ref, k_ref, v_ref, *p_refs, ot_ref, o_ref, il_ref = saved
    s = pl.program_id(0)
    blocks = 4
    half = xo_ref.shape[0] // blocks
    tiles = vec_ref.shape[0]

    @pl.when(s == 0)
    def _():
        for b in range(blocks):
            x_all[2 * b * half : (2 * b + 1) * half] = xo_ref[b * half : (b + 1) * half]
            x_all[(2 * b + 1) * half : (2 * b + 2) * half] = xp_ref[b * half : (b + 1) * half]
        both = va_ref[...].astype(F32) + vb_ref[...].astype(F32)
        vec_ref[...] = both[:tiles]
        bias_ref[...] = both[tiles]
        acc_ref[...] = xo_ref[...].astype(F32) + vrow(vec_ref, 5)

    w = [pick(wa_ref, wb_ref, i, s >= 2) for i in range(4)]
    t = swap(s) ^ ranks_ref[4]
    attn_fwd_body(True, xo_ref[...], x_all[...], w, (vec_ref[t, 3:4], vec_ref[t, 4:5]),
                  q_ref, k_ref, v_ref, p_refs, ot_ref, o_ref, il_ref, o_all, wo_all)

    @pl.when(s == pl.num_programs(0) - 1)
    def _():
        finish_norm(acc_ref[...] + nt(wide(o_all), wide(wo_all)), n_ref, r_ref)


def cross_fwd(ranks_ref, n1_ref, mo_ref, mp_ref, wa_ref, wb_ref, vec_ref, *refs):
    saved, (n_ref, r_ref, m_all, h_low, acc_ref, o_all, wo_all) = refs[:7], refs[7:]
    q_ref, k_ref, v_ref, *p_refs, ot_ref, o_ref, il_ref = saved
    s = pl.program_id(0)
    half = mo_ref.shape[0]

    @pl.when(s == 0)
    def _():
        m_all[:half] = mo_ref[...]
        m_all[half:] = mp_ref[...]
        h1 = n1_ref[...] * vrow(vec_ref, 0) + vrow(vec_ref, 6)
        h_low[...] = h1.astype(BF)
        acc_ref[...] = h1 + vrow(vec_ref, 9)

    w = [pick(wa_ref, wb_ref, i, s >= 2) for i in range(4)]
    t = swap(s) ^ ranks_ref[4]
    attn_fwd_body(False, h_low[...], m_all[...], w, (vec_ref[t, 7:8], vec_ref[t, 8:9]),
                  q_ref, k_ref, v_ref, p_refs, ot_ref, o_ref, il_ref, o_all, wo_all)

    @pl.when(s == pl.num_programs(0) - 1)
    def _():
        finish_norm(acc_ref[...] + nt(wide(o_all), wide(wo_all)), n_ref, r_ref)


def ffn_both(ranks_ref, n2_ref, r2_ref, c0, c1, c2, c3, w_ref, bias_ref, vec_ref,
             h0, h1, h2, h3, keep_ref, send_ref, dz2_ref, vg_ref, bg_ref,
             h_low, h_t, act, slope, acc, dz3_low, dz3_t, dh2):
    phase = pl.program_id(0)
    t = pl.program_id(1)
    d = n2_ref.shape[1]
    last = pl.num_programs(1) - 1
    w_in = w_ref[:, 0, 0].reshape(d, -1)
    w_out = w_ref[:, 0, 1].reshape(d, -1)
    hid = w_in.shape[1]
    strips = hid // PAIR

    @pl.when((phase == 0) & (t == 0))
    def _():
        h = n2_ref[...] * vrow(vec_ref, 1) + vrow(vec_ref, 10)
        h_low[...] = h.astype(BF)
        h_t[...] = h.astype(BF).T
        acc[...] = h + vrow(vec_ref, 11)

    @pl.when(phase == 0)
    def _():
        bias = jnp.concatenate(
            [bias_ref[pl.ds(t * strips + j, 1), :] for j in range(strips)], axis=1
        )
        u = nn(h_low[...], w_in) + bias
        cube = GELU_A * u * u
        th = jnp.tanh(GELU_C * u * (1.0 + cube))
        low = 0.5 * (1.0 + th)
        f = (u * low).astype(BF)
        act[t] = f
        slope[t] = low + 0.5 * u * (1.0 - th * th) * (GELU_C * (1.0 + 3.0 * cube))
        acc[...] += nt(f, w_out)

    @pl.when((phase == 0) & (t == last))
    def _():
        n3, r3 = norm_stats(acc[...])
        acc[...] = n3 * vrow(vec_ref, 2) + vrow(vec_ref, 12)
        put_home(acc, (h0, h1, h2, h3), ranks_ref)
        for r, ref in enumerate((c0, c1, c2, c3)):
            rows = ref.shape[0]
            at = pl.multiple_of((r ^ ranks_ref[1]) * rows, rows)
            dh2[pl.ds(at, rows), :] = ref[...].astype(F32)
        g = dh2[...]
        vg_ref[0:1] = rows_sum(g * n3)
        vg_ref[1:2] = rows_sum(g)
        dz3 = norm_back(g, vrow(vec_ref, 2), n3, r3)
        vg_ref[2:3] = rows_sum(dz3)
        low = dz3.astype(BF)
        dz3_low[...] = low
        dz3_t[...] = low.T
        dh2[...] = dz3

    @pl.when(phase == 1)
    def _():
        f = act[t]
        df = nn(dz3_low[...], w_out).astype(BF).astype(F32)
        du = (df * slope[t]).astype(BF)
        g_out = nn(dz3_t[...], f).astype(BF)
        g_in = nn(h_t[...], du).astype(BF)
        sums = rows_sum(du.astype(F32))
        for j in range(strips):
            bg_ref[pl.ds(t * strips + j, 1), :] = sums[:, j * PAIR : (j + 1) * PAIR]
        dh2[...] += nt(du, w_in)
        mine = t % 2 == ranks_ref[3]
        piece = keep_ref.shape[3] // 2

        @pl.when(mine)
        def _():
            put_pieces(keep_ref, 0, 0, g_in, ranks_ref)
            put_pieces(keep_ref, 0, piece, g_out, ranks_ref)

        @pl.when(jnp.logical_not(mine))
        def _():
            put_pieces(send_ref, 0, 0, g_in, ranks_ref)
            put_pieces(send_ref, 0, piece, g_out, ranks_ref)

    @pl.when((phase == 1) & (t == last))
    def _():
        g = dh2[...]
        n2 = n2_ref[...]
        vg_ref[3:4] = rows_sum(g * n2)
        vg_ref[4:5] = rows_sum(g)
        dz2 = norm_back(g, vrow(vec_ref, 1), n2, r2_ref[:, 0:1])
        vg_ref[5:6] = rows_sum(dz2)
        vg_ref[6:8] = jnp.zeros_like(vg_ref[6:8])
        dz2_ref[...] = dz2


def put_home(acc, refs, ranks_ref):
    rows = refs[0].shape[0]
    for r, ref in enumerate(refs):
        at = pl.multiple_of((r ^ ranks_ref[1]) * rows, rows)
        ref[...] = acc[pl.ds(at, rows), :].astype(BF)


def self_bwd(ranks_ref, act_ref, dz_ref, part_ref, w_ref, *refs):
    saved, (slot_ref, own_ref, peer_ref, out_ref, qg_ref, *scratch) = refs[:8], refs[8:]
    shape = w_ref.shape
    w = [w_ref[0, i].reshape(shape[2] * shape[3], shape[4]) for i in (0, 3)]

    def first():
        dz = dz_ref[...]
        return act_ref[...].T, dz, part_ref[...]

    def store(g_q, g_o, piece):
        put_pieces(slot_ref, 0, 0, g_q, ranks_ref)
        put_pieces(slot_ref, 0, piece, g_o, ranks_ref)

    def last(total):
        out_ref[...] = total

    attn_bwd(True, first, w, saved, store, last, slot_ref.shape[3] // 2,
             own_ref, peer_ref, qg_ref, *scratch)


def cross_bwd(ranks_ref, n_ref, r_ref, dz_ref, wa_ref, wb_ref, vec_ref, *refs):
    saved = refs[:7]
    keep_ref, send_ref, own_ref, peer_ref, out_ref, vg_ref, qg_ref, *scratch = refs[7:]
    s = pl.program_id(0)
    odd = s >= 2

    def first():
        h = n_ref[...] * vrow(vec_ref, 0) + vrow(vec_ref, 6)
        dz = dz_ref[...]
        return h.astype(BF).T, dz, dz

    def store(g_q, g_o, piece):
        @pl.when(jnp.logical_not(odd))
        def _():
            put_pieces(keep_ref, 0, 0, g_q, ranks_ref)
            put_pieces(keep_ref, 0, piece, g_o, ranks_ref)

        @pl.when(odd)
        def _():
            put_pieces(send_ref, 0, 0, g_q, ranks_ref)
            put_pieces(send_ref, 0, piece, g_o, ranks_ref)

    def last(g):
        normed = n_ref[...]
        vg_ref[0:1] = rows_sum(g * normed)
        vg_ref[1:2] = rows_sum(g)
        dz1 = norm_back(g, vrow(vec_ref, 0), normed, r_ref[:, 0:1])
        vg_ref[2:3] = rows_sum(dz1)
        vg_ref[3:8] = jnp.zeros_like(vg_ref[3:8])
        out_ref[...] = dz1

    w = [pick(wa_ref, wb_ref, i, odd) for i in (0, 3)]
    attn_bwd(False, first, w, saved, store, last, keep_ref.shape[3] // 2,
             own_ref, peer_ref, qg_ref, *scratch)


def attn_bwd(causal, first, w, saved, store, last, piece, own_ref, peer_ref, qg_ref,
             dy, dy_t, act_t, acc, dk_ref, dv_ref, dq_all, wq_all):
    s = pl.program_id(0)
    q_ref, k_ref, v_ref, *p_refs, ot_ref, o_ref, il_ref = saved
    blocks = len(p_refs)
    wq, wo = w

    @pl.when(s == 0)
    def _():
        act_t[...], dz, acc[...] = first()
        low = dz.astype(BF)
        dy[...] = low
        dy_t[...] = low.T

    q = q_ref[0]
    k = k_ref[0]
    v = v_ref[0]
    keys = k.shape[0]
    rows = q.shape[0] // blocks
    do = nn(dy[...], wo).astype(BF)
    g_o = nn(dy_t[...], o_ref[0]).astype(BF)
    do_t = do.T.astype(F32)
    prod = do_t * ot_ref[0].astype(F32)
    inv_a, inv_b = il_ref[0, 0:1], il_ref[0, 1:2]
    inner_a = jnp.sum(prod[:HD], axis=0, keepdims=True) * inv_a
    inner_b = jnp.sum(prod[HD:], axis=0, keepdims=True) * inv_b
    row = lax.broadcasted_iota(jnp.int32, do_t.shape, 0)
    dos = (do_t * jnp.where(row < HD, inv_a, inv_b)).astype(BF).T
    kt = k.T
    dqs = [None] * blocks
    for b in reversed(range(blocks)):
        n = keys // blocks * (b + 1) if causal else keys
        span = slice(b * rows, (b + 1) * rows)
        dob = split_pair(dos[span])
        qb = split_pair(q[span])
        pb = p_refs[b][0]
        dp = nt(v[:n], dob)
        inner = jnp.concatenate([inner_a[:, span], inner_b[:, span]], axis=1)
        ds = (pb.astype(F32) * (dp - inner)).astype(BF)
        dv = nn(pb, dob)
        dk = nn(ds, qb)
        if b == blocks - 1:
            dv_ref[...] = dv
            dk_ref[...] = dk
        else:
            dv_ref[:n] += dv
            dk_ref[:n] += dk
        dqs[b] = (join_pair(nn(kt[:, :n], ds)) * HD ** (-0.5)).T.astype(BF)
    dq = jnp.concatenate(dqs, axis=0)
    g_q = nn(act_t[...], dq).astype(BF)
    store(g_q, g_o, piece)
    qg_ref[0] = rows_sum(dq.astype(F32))
    dq_all[s] = dq
    wq_all[s] = wq
    for i, ref in enumerate((dk_ref, dv_ref)):
        if causal:
            part = keys // 8
            for b in range(4):
                at, to = 2 * b * part, slice(b * part, (b + 1) * part)
                own_ref[i, 0, to] = ref[at : at + part].astype(BF)
                peer_ref[i, 0, to] = ref[at + part : at + 2 * part].astype(BF)
        else:
            own_ref[i, 0] = ref[: keys // 2].astype(BF)
            peer_ref[i, 0] = ref[keys // 2 :].astype(BF)

    @pl.when(s == pl.num_programs(0) - 1)
    def _():
        last(acc[...] + nt(wide(dq_all), wide(wq_all)))


def kv_back(final, lanes, blen, ranks_ref, act_ref, *refs):
    (wk_own, wv_own, wk_peer, wv_peer), rest = refs[:4], refs[4:]
    if final:
        (own_low, got_low, own_hi, got_hi, base_ref, vgc_ref, vgf_ref, bg_ref, qgs_ref, qgs_hi,
         qgc_ref, vg_mem_ref, h0, h1, h2, h3, keep_ref, send_ref, acc, tiles) = rest
        parts = [(own_low, 0, got_low, 0), (own_low, 1, got_low, 1),
                 (own_hi, 0, got_hi, 0), (own_hi, 1, got_hi, 1)]
    else:
        own_ref, got_ref, h0, h1, h2, h3, keep_ref, send_ref, vgrad_ref, acc = rest
        parts = [(own_ref, s, got_ref, s ^ 2) for s in range(4)]
    pairs = len(parts)
    d = act_ref.shape[1]

    def gathered(own, i, got, j, kind):
        return (own[kind, i].astype(F32) + got[kind, j].astype(F32)).astype(BF)

    def weight(ref, ry):
        return ref[ry, 0].reshape(d, PAIR)

    dkv = [gathered(*part, kind) for part in parts for kind in range(2)]
    wkv = [weight(ref, ry) for refs in ((wk_own, wv_own), (wk_peer, wv_peer))
           for ry in range(2) for ref in refs]
    dkv_all = jnp.concatenate(dkv, axis=1)
    gkv = nn(act_ref[...].T, dkv_all).astype(BF)
    total = nt(dkv_all, jnp.concatenate(wkv, axis=1))
    acc[...] = total + base_ref[...] if final else total
    put_home(acc, (h0, h1, h2, h3), ranks_ref)
    n_x, n_z = keep_ref.shape[1], keep_ref.shape[2]
    piece = d // (n_x * n_z)
    for s in range(pairs):
        ref = keep_ref if s < 2 else send_ref
        for kind in range(2):
            at = (2 * s + kind) * PAIR
            put_pieces(ref, s % 2, kind * piece, gkv[:, at : at + PAIR], ranks_ref)
    sums = [rows_sum(dkv[2 * s + 1].astype(F32)) for s in range(pairs)]
    if not final:
        for s in range(pairs):
            vgrad_ref[s] = sums[s]
        return
    for j in range(pairs):
        at = slice(j * PAIR, (j + 1) * PAIR)
        rel = swap(j ^ ranks_ref[4])
        tiles[j, 0:1] = vgc_ref[0:1, at]
        tiles[j, 1:2] = vgf_ref[3:4, at]
        tiles[j, 2:3] = vgf_ref[0:1, at]
        tiles[j, 3:4] = jnp.where(rel < 2, qgs_ref[rel % 2], qgs_hi[rel % 2])
        tiles[j, 5:6] = vgc_ref[2:3, at]
        tiles[j, 6:7] = vgc_ref[1:2, at]
        tiles[j, 7:8] = qgc_ref[rel]
        tiles[j, 8:9] = vg_mem_ref[rel]
        tiles[j, 9:10] = vgf_ref[5:6, at]
        tiles[j, 10:11] = vgf_ref[4:5, at]
        tiles[j, 11:12] = vgf_ref[2:3, at]
        tiles[j, 12:13] = vgf_ref[1:2, at]
        tiles[j, 13:16] = jnp.zeros((3, PAIR), F32)
    for s in range(pairs):
        tiles[swap(s) ^ ranks_ref[4], 4:5] = sums[s]
    rows_at = lax.broadcasted_iota(jnp.int32, (16, PAIR), 0)
    for ry in range(2):
        for rc, ref in enumerate((keep_ref, send_ref)):
            for i in range(n_x):
                for k in range(n_z):
                    dc = (i ^ ranks_ref[0]) * n_z + (k ^ ranks_ref[1])
                    p = dc * pairs + ((2 * ry + rc) ^ ranks_ref[4])
                    tile = tiles[lax.div(p * lanes, PAIR)]
                    bias = bg_ref[pl.ds(lax.div(p * blen, PAIR), 1), :]
                    both = jnp.where(rows_at == 13, bias, tile).astype(BF)
                    ref[ry, i, k, 2 * piece : 2 * piece + 16] = both


def pack_rows(*refs):
    ins, outs = refs[1 : 1 + len(refs) // 2], refs[1 + len(refs) // 2 :]
    for ref, out in zip(ins, outs):
        out[...] = ref[0]


def pack_rest(*refs):
    for ref, out in zip(refs[1:9], refs[9:17]):
        out[...] = ref[0]


def pack_weights(lanes, blen, ranks_ref, wqs, wks, wvs, wos, wqc, wkc, wvc, woc, win, wout,
                 gains, shifts, bias, s_ref, c_ref, f_ref, va, vb):
    f_ref[0] = win[...]
    f_ref[1] = wout[...]
    n = wqs.shape[0]
    for i, ref in enumerate((wqc, wkc, wvc, woc)):
        c_ref[i * n : (i + 1) * n] = ref[...]
    for i, ref in enumerate((wqs, wks, wvs, wos)):
        s_ref[i * n : (i + 1) * n] = ref[...]
    p = (ranks_ref[0] * 4 + ranks_ref[1]) * 4 + ranks_ref[4]
    at = 4 * n
    va[...] = jnp.zeros_like(va)
    va[0:3, 0:lanes] = gains[...].astype(F32)
    va[3:13, 0:lanes] = shifts[...].astype(F32)
    s_ref[at : at + 16] = pltpu.roll(va[...], lax.rem(p * lanes, PAIR), 1).astype(BF)
    vb[...] = jnp.zeros_like(vb)
    vb[pl.ds(lax.div(p * blen, PAIR), 1), 0:blen] = bias[...].astype(F32)
    s_ref[at + 16 : at + 32] = pltpu.roll(vb[...], lax.rem(p * blen, PAIR), 1).astype(BF)


def whole(a):
    return pl.BlockSpec(a.shape, lambda *_: (0,) * len(a.shape))


def without(body, at, count):
    return lambda *refs: body(*refs[:at], *refs[at + count :])


def launch(body, name, grid, ranks, ins, outs, scratch=(), deps=(), limit=VMEM_LIMIT, cost=SMALL_COST):
    first = 0 if ranks is None else 1
    deps = list(deps)
    n_in, n_out = first + len(ins), len(outs)

    def with_token(*refs):
        kept = refs[:n_in] + refs[n_in + len(deps) :]
        kept[n_in + n_out][...] = jnp.zeros((8, PAIR), F32)
        body(*kept[: n_in + n_out], *kept[n_in + n_out + 1 :])

    token = struct((8, PAIR), F32)
    call = pl.pallas_call(
        with_token,
        grid_spec=pltpu.PrefetchScalarGridSpec(
            num_scalar_prefetch=first,
            grid=grid,
            in_specs=[i[1] for i in ins] + [pl.BlockSpec(memory_space=pl.ANY)] * len(deps),
            out_specs=tuple(o[1] for o in outs) + (whole(token),),
            scratch_shapes=list(scratch),
        ),
        out_shape=tuple(
            pltpu.HBM(o[0].shape, o[0].dtype) if len(o) > 2 else o[0] for o in outs
        ) + (token,),
        compiler_params=pltpu.CompilerParams(
            vmem_limit_bytes=limit, dimension_semantics=("arbitrary",) * len(grid)
        ),
        cost_estimate=pl.CostEstimate(flops=cost, bytes_accessed=1, transcendentals=0),
        name=name,
    )
    args = [
        pltpu.with_memory_space_constraint(i[0], pltpu.HBM) if len(i) > 2 else i[0] for i in ins
    ] + deps
    return call(*args) if ranks is None else call(ranks, *args)


def local(body, name, outs, *ins, ranks=None, scratch=(), deps=(), pinned=(), limit=SMALL_LIMIT,
          cost=SMALL_COST):
    return launch(
        body, name, (1,), ranks, [(a, whole(a)) for a in ins],
        [(o, whole(o), True) if i in pinned else (o, whole(o)) for i, o in enumerate(outs)],
        scratch, deps, limit, cost,
    )


def struct(shape, dtype):
    return jax.ShapeDtypeStruct(shape, dtype)


def restack(ins, outs, cuts):
    for out, (lo, hi) in zip(outs, cuts):
        for r, ref in enumerate(ins):
            out[0, 0, r] = ref[lo:hi]


def double(own, got, out, axis):
    m = own.shape[axis]
    if axis == 0:
        out[:m] = own[...]
        out[m:] = got[...]
    else:
        out[:, :m] = own[...]
        out[:, m:] = got[...]


def order(ranks_ref, parts, outs):
    for r, ref in enumerate(parts):
        rows = ref.shape[-2]
        at = pl.multiple_of((r ^ ranks_ref[1]) * rows, rows)
        for i, out in enumerate(outs):
            out[pl.ds(at, rows), :] = ref[...] if len(outs) == 1 else ref[i]


def assemble(lanes, ranks_ref, a0, a1, b0, b1, w_ref, v_ref=None, scr=None):
    pairs = 4
    n_x, n_z = a0.shape[1], a0.shape[2]
    prows = w_ref.shape[3]
    if v_ref is not None:
        scr[...] = jnp.zeros_like(scr)
    for ry in range(2):
        a_ref = (a0, a1)[ry]
        for i in range(n_x):
            for k in range(n_z):
                dc = (i ^ ranks_ref[0]) * n_z + (k ^ ranks_ref[1])
                b_ref, bi = (b0, i) if i < n_x // 2 else (b1, i - n_x // 2)
                for m in range(2):
                    span = slice(m * prows, (m + 1) * prows)
                    w_ref[ry, m, dc] = a_ref[0, i, k, span]
                    w_ref[ry, 2 + m, dc] = b_ref[ry, bi, k, span]
                if v_ref is not None:
                    at = 2 * prows
                    p = dc * pairs + ((2 * ry) ^ ranks_ref[4])
                    tile = lax.div(p * lanes, PAIR)
                    scr[tile] += b_ref[ry, bi, k, at : at + 16].astype(F32)
                    scr[pairs] += b_ref[ry, bi, k, at + 16 : at + 32].astype(F32)
    if v_ref is not None:
        v_ref[...] = scr[...].astype(BF)


def start_one(cuts, ranks_ref, *refs):
    restack(refs[0:4], refs[8:10], cuts)
    order(ranks_ref, refs[4:8], refs[10:11])


def start_two(axes, cuts, a, ga, b, gb, *refs):
    double(a, ga, refs[4], axes[0])
    double(b, gb, refs[5], axes[1])
    restack(refs[0:4], refs[6:8], cuts)


def start_five(lanes, ranks_ref, *refs):
    assemble(lanes, ranks_ref, *refs[0:4], refs[8])
    order(ranks_ref, refs[4:8], refs[9:10])


def double_both(axes, a, ga, b, gb, out_a, out_b):
    double(a, ga, out_a, axes[0])
    double(b, gb, out_b, axes[1])


def order_home(ranks_ref, *refs):
    order(ranks_ref, refs[:4], refs[4:])


def halve_body(axis_a, axis_b, cuts, *refs):
    ins, (sa, ka, sb, kb) = refs[: len(refs) - 4], refs[len(refs) - 4 :]

    def place(axis, send, keep, at, value):
        rows = value.shape[3]
        m = value.shape[axis] // 2
        lo = value[:m] if axis == 0 else value[:, :m]
        hi = value[m:] if axis == 0 else value[:, m:]
        keep[:, :, :, at : at + rows] = lo
        send[:, :, :, at : at + rows] = hi.astype(BF)

    at_a = at_b = 0
    for cut in cuts:
        if cut is None:
            keep_a, got_a, keep_b, got_b, *ins = ins
            parts = (keep_a[...] + got_a[...].astype(F32), keep_b[...] + got_b[...].astype(F32))
        else:
            keep, got, *ins = ins
            total = keep[...].astype(F32) + got[...].astype(F32)
            parts = (total[:, :, :, :cut], total[:, :, :, cut:])
        place(axis_a, sa, ka, at_a, parts[0])
        place(axis_b, sb, kb, at_b, parts[1])
        at_a += parts[0].shape[3]
        at_b += parts[1].shape[3]


def spread_body(*refs):
    ins, (s1, s2, s3, keep) = refs[:-4], refs[-4:]
    at = 0
    for own, got in zip(ins[::2], ins[1::2]):
        rows = own.shape[3]
        for r, ref in enumerate((keep, s1, s2, s3)):
            total = own[0, 0, r] + got[0, 0, r].astype(F32)
            ref[at : at + rows] = total.astype(ref.dtype)
        at += rows


def finish_body(plan, lanes, blen, ranks_ref, keep, r1, r2, r3, *outs):
    total = keep[...] + r1[...].astype(F32) + r2[...].astype(F32) + r3[...].astype(F32)
    at = 0
    outs = list(outs)
    for turn, rows in plan:
        part = total[at : at + rows]
        at += rows
        if turn == 2:
            p = (ranks_ref[0] * 4 + ranks_ref[1]) * 4 + ranks_ref[4]
            vec = pltpu.roll(part, lax.rem(PAIR - lax.rem(p * lanes, PAIR), PAIR), 1)
            outs.pop(0)[...] = vec[0:3, :lanes]
            outs.pop(0)[...] = vec[3:13, :lanes]
            own = pltpu.roll(part, lax.rem(PAIR - lax.rem(p * blen, PAIR), PAIR), 1)
            outs.pop(0)[...] = own[13:14, :blen]
        else:
            outs.pop(0)[...] = part


def home_body(every, out_ref):
    n_c, n_z, rows, _ = every.shape
    for c in range(n_c):
        for z in range(n_z):
            out_ref[z, c * rows : (c + 1) * rows, :] = every[c, z].astype(out_ref.dtype)


def half_spec(w, other):
    if other:
        return pl.BlockSpec((1,) + w.shape[1:], lambda s, _: (jnp.maximum(s - 2, 0), 0, 0, 0, 0))
    return pl.BlockSpec((1,) + w.shape[1:], lambda s, _: (jnp.minimum(s, 1), 0, 0, 0, 0))


def slot_outs(n_x, n_z, rows):
    shape = struct((2, n_x, n_z, rows, PAIR), BF)
    block = (1, n_x, n_z, rows, PAIR)
    return [
        (shape, pl.BlockSpec(block, lambda s, _: (jnp.minimum(s, 1), 0, 0, 0, 0))),
        (shape, pl.BlockSpec(block, lambda s, _: (jnp.maximum(s - 2, 0), 0, 0, 0, 0))),
    ]


def full(shape):
    return pl.BlockSpec(shape, lambda *_: (0,) * len(shape))


def run_attn_fwd(causal, ranks, rows_in, w_own, w_peer, vecs, pairs, deps):
    own, d = rows_in[0].shape
    keys = 2 * own
    blocks = 2 if causal else 1
    ns = [keys // blocks * (b + 1) if causal else keys for b in range(blocks)]
    qn = 2 * own // blocks

    def saved(shape, dtype):
        return (struct((pairs,) + shape, dtype),
                pl.BlockSpec((1,) + shape, lambda s, _: (s, 0, 0)), True)

    outs = [
        saved((own, PAIR), BF), saved((keys, PAIR), BF), saved((keys, PAIR), BF),
        *[saved((n, qn), BF) for n in ns],
        saved((PAIR, own), BF), saved((own, PAIR), BF), saved((8, own), F32),
        (struct((own, d), F32), full((own, d))) + (() if causal else (True,)),
        (struct((own, PAIR), F32), full((own, PAIR))),
    ]
    if causal:
        outs.append((struct((pairs, 16, PAIR), F32), full((pairs, 16, PAIR))))
        outs.append((struct((16, PAIR), F32), full((16, PAIR))))
    ins = [(a, whole(a)) for a in rows_in]
    ins += [(w_own, half_spec(w_own, False), True), (w_peer, half_spec(w_peer, True), True)]
    ins += [(a, whole(a)) for a in vecs]
    scratch = [pltpu.VMEM((keys, d), BF)] + ([] if causal else [pltpu.VMEM((own, d), BF)])
    scratch.append(pltpu.VMEM((own, d), F32))
    scratch += [pltpu.VMEM((pairs, own, PAIR), BF), pltpu.VMEM((pairs, d, PAIR), BF)]

    return launch(
        self_fwd if causal else cross_fwd, "self_fwd" if causal else "cross_fwd",
        (pairs,), ranks, ins, outs, scratch, deps,
        cost=COSTS["self_fwd" if causal else "cross_fwd"],
    )


def run_ffn(ranks, n2, r2, cots, w, bias, vec, n_x, n_z):
    own, d = n2.shape
    dc, parts, _, prows, hid = w.shape
    half = own // 4
    back = lambda p, t, ref: ((p * (t // 2)) ^ ref[2], 0, 0, 0, 0)
    slots = struct((2, n_x, n_z, 2 * prows, hid), BF)
    slot_block = pl.BlockSpec((1, n_x, n_z, 2 * prows, hid), back)
    outs = [(struct((half, d), BF), full((half, d)))] * 4 + [
        (slots, slot_block),
        (slots, slot_block),
        (struct((own, d), F32), full((own, d))),
        (struct((8, d), F32), full((8, d))),
        (struct((16, PAIR), F32), full((16, PAIR))),
    ]
    ins = [(n2, whole(n2), True), (r2, whole(r2))] + [(c, whole(c)) for c in cots] + [
        (w, pl.BlockSpec((dc, 1, 2, prows, hid), lambda p, t, _: (0, t, 0, 0, 0)), True),
        (bias, whole(bias)),
        (vec, whole(vec)),
    ]
    scratch = [
        pltpu.VMEM((own, d), BF),
        pltpu.VMEM((d, own), BF),
        pltpu.VMEM((parts, own, hid), BF),
        pltpu.VMEM((parts, own, hid), F32),
        pltpu.VMEM((own, d), F32),
        pltpu.VMEM((own, d), BF),
        pltpu.VMEM((d, own), BF),
        pltpu.VMEM((own, d), F32),
    ]
    return launch(
        ffn_both, "ffn_both", (2, parts), ranks, ins, outs, scratch,
        cost=COSTS["ffn_both"],
    )


def bwd_scratch(own, keys, d, pairs):
    return [
        pltpu.VMEM((own, d), BF),
        pltpu.VMEM((d, own), BF),
        pltpu.VMEM((d, own), BF),
        pltpu.VMEM((own, d), F32),
        pltpu.VMEM((keys, PAIR), F32),
        pltpu.VMEM((keys, PAIR), F32),
        pltpu.VMEM((pairs, own, PAIR), BF),
        pltpu.VMEM((pairs, d, PAIR), BF),
    ]


def per_pair(a, first=0):
    return (a, pl.BlockSpec((1,) + a.shape[1:], lambda s, _: (s + first, 0, 0)), True)


def run_cross_bwd(ranks, dz, w_own, w_peer, vec, saved, n, r, n_x, n_z, deps):
    pairs, own, _ = saved[0].shape
    keys = saved[1].shape[1]
    d = dz.shape[1]
    prows = w_own.shape[3]
    kv_spec = pl.BlockSpec((2, 1, own, PAIR), lambda s, _: (0, s, 0, 0))
    outs = slot_outs(n_x, n_z, 2 * prows) + [
        (struct((2, pairs, own, PAIR), BF), kv_spec, True),
        (struct((2, pairs, own, PAIR), BF), kv_spec, True),
        (struct((own, d), F32), full((own, d))),
        (struct((8, d), F32), full((8, d))),
        (struct((pairs, 1, PAIR), F32), pl.BlockSpec((1, 1, PAIR), lambda s, _: (s, 0, 0))),
    ]
    ins = [
        (n, whole(n)),
        (r, whole(r)),
        (dz, whole(dz)),
        (w_own, half_spec(w_own, False), True),
        (w_peer, half_spec(w_peer, True), True),
        (vec, whole(vec)),
        *[per_pair(a) for a in saved],
    ]
    return launch(
        cross_bwd, "cross_bwd", (pairs,), ranks, ins, outs, bwd_scratch(own, keys, d, pairs), deps,
        cost=COSTS["cross_bwd"],
    )


def run_self_bwd(first, ranks, act, dz, part, w, saved, n_x, n_z, deps):
    _, own, _ = saved[0].shape
    keys = saved[1].shape[1]
    d = dz.shape[1]
    prows = w.shape[3]
    pairs = 2
    kv_spec = pl.BlockSpec((2, 1, own, PAIR), lambda s, _: (0, s, 0, 0))
    slots = (1, n_x, n_z, 2 * prows, PAIR)
    outs = [
        (struct((2,) + slots[1:], BF), pl.BlockSpec(slots, lambda s, _: (s, 0, 0, 0, 0))),
        (struct((2, pairs, own, PAIR), BF), kv_spec, True),
        (struct((2, pairs, own, PAIR), BF), kv_spec, True),
        (struct((own, d), F32), full((own, d)), True),
        (struct((pairs, 1, PAIR), F32), pl.BlockSpec((1, 1, PAIR), lambda s, _: (s, 0, 0))),
    ]
    ins = [
        (act, whole(act)),
        (dz, whole(dz)) if first else (dz, whole(dz), True),
        (part, whole(part)) if first else (part, whole(part), True),
        (w, pl.BlockSpec((1,) + w.shape[1:], lambda s, _: (s, 0, 0, 0, 0)), True),
        *[per_pair(a, first) for a in saved],
    ]
    return launch(
        self_bwd, "self_bwd", (pairs,), ranks, ins, outs, bwd_scratch(own, keys, d, pairs), deps,
        cost=COSTS["self_bwd"],
    )


def run_kv_back(name, ranks, act, parts, w_own, w_peer, extra, lanes, blen, n_x, n_z, deps):
    own, d = act.shape
    pairs = 2 * w_own.shape[0]
    prows = w_own.shape[3]
    final = bool(extra)
    rows = 2 * prows + (16 if final else 0)
    half = own // 4
    slots = struct((2, n_x, n_z, rows, PAIR), BF)
    outs = [(struct((half, d), BF), full((half, d)))] * 4 + [(slots, whole(slots))] * 2
    scratch = [pltpu.VMEM((own, d), F32)]
    if final:
        scratch.append(pltpu.VMEM((pairs, 16, PAIR), F32))
    else:
        outs.append((struct((pairs, 1, PAIR), F32), full((pairs, 1, PAIR))))

    def mat(w, i):
        block = (w.shape[0], 1) + w.shape[2:]
        return (w, pl.BlockSpec(block, lambda *_: (0, i, 0, 0, 0)), True)

    ins = [
        (act, whole(act)),
        mat(w_own, 1), mat(w_own, 2), mat(w_peer, 1), mat(w_peer, 2),
        *[(a, whole(a), True) for a in parts],
        *[(a, whole(a), True) if i == 0 else (a, whole(a)) for i, a in enumerate(extra)],
    ]
    return launch(
        functools.partial(kv_back, final, lanes, blen), name, (1,), ranks, ins, outs,
        scratch, deps, cost=COSTS[name],
    )


ALL = ("dp", "ctx", "ty", "tc")


def shards(
    inputs, memory, cotangent, wq_self, wk_self, wv_self, wo_self, wq_cross, wk_cross, wv_cross,
    wo_cross, w_in, w_out, gains, shifts, ffn_bias,
):
    seqs, block, d = inputs.shape
    n_x, n_z, n_y, n_c = (lax.axis_size(a) for a in ALL)
    pairs = n_y * n_c
    half = block // n_c
    own = n_z * half
    x_rank, z_rank, y_rank, c_rank = (lax.axis_index(a) for a in ALL)
    ranks = jnp.stack([x_rank, z_rank, y_rank, c_rank, y_rank * n_c + c_rank]).astype(jnp.int32)
    prows, lanes, blen = wq_self.shape[0], gains.shape[1], ffn_bias.shape[0]
    hid = w_in.shape[1]
    x_bits = [1 << i for i in range((n_x - 1).bit_length())]

    def send(array, axis, bit):
        return lax.ppermute(array, axis, [(i, i ^ bit) for i in range(lax.axis_size(axis))])

    def rows_of(r):
        return pl.BlockSpec((1, half, d), lambda i, ref: (ref[2] * 4 + (ref[1] ^ r), ref[3], 0))

    def packed_rows(array):
        return [(array, rows_of(r), True) for r in range(n_z)]

    def around_z(parts):
        return [parts[0]] + [send(parts[r], "ctx", r) for r in range(1, n_z)]

    row_part = struct((half, d), BF)

    def sent_rows(array, name, deps):
        *parts, token = launch(
            pack_rows, name, (1,), ranks, packed_rows(array), [(row_part, whole(row_part))] * n_z,
            deps=deps, limit=SMALL_LIMIT,
        )
        return around_z(parts), token

    x_got, token = sent_rows(inputs, "pack_x", [])
    f_shape = struct((2, prows, hid), BF)
    s_pack, c_pack, f_pack, token = local(
        functools.partial(pack_weights, lanes, blen), "pack_weights",
        [struct((4 * prows + 32, PAIR), BF), struct((4 * prows, PAIR), BF), f_shape],
        wq_self, wk_self, wv_self, wo_self.T, wq_cross, wk_cross, wv_cross, wo_cross.T,
        w_in, w_out.T, gains, shifts, ffn_bias.reshape(1, -1), ranks=ranks, deps=[token],
        pinned=(2,),
        scratch=[pltpu.VMEM((16, PAIR), F32), pltpu.VMEM((16, PAIR), F32)],
    )
    s_got = around_z([s_pack] * n_z)
    w_ffn = lax.all_gather(f_pack, ALL, axis=0, tiled=False).reshape(
        n_x * n_z, pairs, 2, prows, hid
    )
    cuts_s = ((0, 2 * prows), (2 * prows, 4 * prows + 32))
    cuts_c = ((0, 2 * prows), (2 * prows, 4 * prows))

    def z_slots(cuts):
        return [struct((1, 1, n_z, hi - lo, PAIR), BF) for lo, hi in cuts]

    def doubled(array, axis):
        shape = list(array.shape)
        shape[axis] *= 2
        return struct(tuple(shape), BF)

    steps_a = [("dp", bit) for bit in x_bits] + [("ty", 1)]
    steps_b = [("ty", 1)] + [("dp", bit) for bit in x_bits]
    axis_of = {"ty": 0, "dp": 1}
    axes_at = [(axis_of[sa[0]], axis_of[sb[0]]) for sa, sb in zip(steps_a, steps_b)]

    def step(i, a, b):
        return [a, send(a, *steps_a[i]), b, send(b, *steps_b[i])]

    def more(ins, deps):
        for i in range(len(steps_a) - 1):
            a, b, token = local(
                functools.partial(double_both, axes_at[i]), "double",
                [doubled(ins[0], axes_at[i][0]), doubled(ins[2], axes_at[i][1])], *ins, deps=deps,
            )
            ins, deps = step(i + 1, a, b), [token]
        return ins, token

    sa, sb, xo, token = local(
        functools.partial(start_one, cuts_s), "start_one",
        z_slots(cuts_s) + [struct((own, d), BF)], *s_got, *x_got, ranks=ranks,
    )
    xp = send(xo, "tc", 1)
    c_got = around_z([c_pack] * n_z)
    sa, sb, ca, cb, token = local(
        functools.partial(start_two, axes_at[0], cuts_c), "start_two",
        [doubled(sa, axes_at[0][0]), doubled(sb, axes_at[0][1])] + z_slots(cuts_c),
        *step(0, sa, sb), *c_got, deps=[token],
    )
    s_last = step(1, sa, sb)
    c_last = step(0, ca, cb)
    for i in range(1, len(steps_a) - 1):
        sa, sb, token = local(
            functools.partial(double_both, axes_at[i]), "double",
            [doubled(s_last[0], axes_at[i][0]), doubled(s_last[2], axes_at[i][1])],
            *s_last, deps=[token],
        )
        s_last = step(i + 1, sa, sb)
    *packed, token = launch(
        pack_rest, "pack_rest", (1,), ranks, packed_rows(memory) + packed_rows(cotangent),
        [(row_part, whole(row_part))] * (2 * n_z), deps=[token], limit=SMALL_LIMIT,
    )
    m_got, cots = around_z(packed[:n_z]), around_z(packed[n_z:])
    c_last, token = more(c_last, [token])
    w_shape = struct((2, 4, n_x * n_z, prows, PAIR), BF)
    ws_own, v_own, token = local(
        functools.partial(assemble, lanes), "assemble",
        [w_shape, struct((pairs + 1, 16, PAIR), BF)], *s_last, ranks=ranks,
        scratch=[pltpu.VMEM((pairs + 1, 16, PAIR), F32)], deps=[token], pinned=(0,),
    )
    v_peer, ws_peer = send(v_own, "tc", 1), send(ws_own, "tc", 1)
    *saved_self, n1, r1, vec, bias, token = run_attn_fwd(
        True, ranks, (xo, xp), ws_own, ws_peer, (v_own, v_peer), pairs, [token]
    )
    wc_own, mo, token = local(
        functools.partial(start_five, lanes), "start_five", [w_shape, struct((own, d), BF)],
        *c_last, *m_got, ranks=ranks, deps=[token], pinned=(0,),
    )
    wc_peer, mp = send(wc_own, "tc", 1), send(mo, "tc", 1)
    *saved_cross, n2, r2, token = run_attn_fwd(
        False, ranks, (n1, mo, mp), wc_own, wc_peer, (vec,), pairs, [token]
    )
    *out_rows, f_keep, f_send, dz2, vg_ffn, bg, token = run_ffn(
        ranks, n2, r2, cots, w_ffn, bias, vec, n_x, n_z
    )

    def home_rows(got, deps, cost=SMALL_COST):
        here, token = local(
            order_home, "order_home", [struct((own, d), BF)], *got, ranks=ranks, deps=deps,
            cost=cost,
        )
        return here.reshape(n_z, half, d), token

    def home_all(here):
        return lax.all_gather(here, ("ty", "tc"), axis=0, tiled=False)

    def home_last(every, dtype, deps):
        return launch(
            home_body, "home", (n_y,), None,
            [(every, pl.BlockSpec((n_c, n_z, half, d), lambda y: (y, 0, 0, 0)), True)],
            [(struct((seqs, block, d), dtype),
              pl.BlockSpec((n_z, block, d), lambda y: (y, 0, 0)), True)],
            deps=deps, limit=2 * SMALL_LIMIT,
        )

    def to_core(*arrays):
        return [send(a, "tc", 1) for a in arrays]

    back_a = [("ty", 1)] + [("dp", bit) for bit in reversed(x_bits)]
    back_b = [("dp", bit) for bit in reversed(x_bits)] + [("ty", 1)]
    rounds = len(back_a)

    def shape_at(i, rows, lanes_in, steps):
        shape = [2, n_x, n_z, rows, lanes_in]
        for axis, _ in steps[: i + 1]:
            shape[axis_of[axis]] //= 2
        return tuple(shape)

    def halve(i, ins, cuts, rows, deps, cost=SMALL_COST):
        width = ins[0].shape[4]
        shape_a = shape_at(i, rows[0], width, back_a)
        shape_b = shape_at(i, rows[1], width, back_b)
        to_a, keep_a, to_b, keep_b, token = local(
            functools.partial(
                halve_body, axis_of[back_a[i][0]], axis_of[back_b[i][0]], cuts
            ),
            "halve",
            [struct(shape_a, BF), struct(shape_a, F32), struct(shape_b, BF), struct(shape_b, F32)],
            *ins, deps=deps, limit=2 * SMALL_LIMIT, cost=cost,
        )
        return [keep_a, send(to_a, *back_a[i]), keep_b, send(to_b, *back_b[i])], token

    def halve_more(groups, rows, deps, cost=SMALL_COST):
        ins, cuts = sum(groups, []), (None,) * len(groups)
        for i in range(1, rounds):
            ins, token = halve(i, ins, cuts, rows, deps, cost)
            cuts, deps = (None,), [token]
        return ins, token

    def spread(ins, deps):
        rows, width = sum(a.shape[3] for a in ins[::2]), ins[0].shape[4]
        *sends, keep, token = local(
            spread_body, "spread",
            [struct((rows, width), BF)] * 3 + [struct((rows, width), F32)], *ins, deps=deps,
        )
        return [keep] + [send(sends[r - 1], "ctx", r) for r in range(1, n_z)], token

    def finish(ins, plan, extra, deps):
        width = ins[0].shape[1]
        outs = [struct((size, width), F32) for turn, size in plan if turn != 2] + extra
        return local(
            functools.partial(finish_body, plan, lanes, blen), "finish", outs, *ins,
            ranks=ranks, deps=deps,
        )

    out_got = around_z(out_rows)
    rows_f = (prows, prows)
    ffn, token = halve(0, [f_keep, to_core(f_send)[0]], (prows,), rows_f, [token])
    c_keep, c_send, c_own, c_peer, dz1, vg_cross, qgc, token = run_cross_bwd(
        ranks, dz2, wc_own, wc_peer, vec, saved_cross, n1, r1, n_x, n_z, [token]
    )
    c_got, c_add = to_core(c_peer, c_send)
    ffn, token = halve_more([ffn], rows_f, [token])
    s_send, own_hi, peer_hi, base, qgs_hi, token = run_self_bwd(
        2, ranks, xo, dz1, dz1, ws_peer, saved_self, n_x, n_z, [token]
    )
    out_here, token = home_rows(out_got, [token])
    out_every = home_all(out_here)
    ffn, token = spread(ffn, [token])
    *mem_rows, m_keep, m_send, vgc, token = run_kv_back(
        "mem_back", ranks, mo, (c_own, c_got), wc_own, wc_peer, (), lanes, blen, n_x, n_z, [token]
    )
    mem_got = around_z(mem_rows)
    got_low, s_add = to_core(peer_hi, s_send)
    s_keep, own_low, peer_low, base, qgs, token = run_self_bwd(
        0, ranks, xo, dz1, base, ws_own, saved_self, n_x, n_z, [token]
    )
    (m_add,) = to_core(m_send)
    rows_one = (3 * prows, 3 * prows)
    one, token = halve(
        0, [c_keep, c_add, m_keep, m_add, s_keep, s_add], (prows,) * 3, rows_one, [token]
    )
    mem_here, token = home_rows(mem_got, [token], COVER)
    mem_every = home_all(mem_here)
    (got_hi,) = to_core(peer_low)
    *in_rows, i_keep, i_send, token = run_kv_back(
        "in_back", ranks, xo, (own_low, got_low, own_hi, got_hi), ws_own, ws_peer,
        (base, vg_cross, vg_ffn, bg, qgs, qgs_hi, qgc, vgc), lanes, blen, n_x, n_z, [token],
    )
    in_got = around_z(in_rows)
    one, token = halve_more([one], rows_one, [token], COVER)
    rows_two = (prows, prows + 16)
    two, token = halve(0, [i_keep, to_core(i_send)[0]], (prows,), rows_two, [token])
    in_here, token = home_rows(in_got, [token], COVER)
    in_every = home_all(in_here)
    two, token = halve_more([two], rows_two, [token])
    out, token = home_last(out_every, BF, [token])
    g_in, g_out, token = finish(ffn, ((0, prows),) * 2, [], [token])
    sums, token = spread(one + two, [token])
    grad_memory, token = home_last(mem_every, F32, [token])
    grad_inputs, token = home_last(in_every, F32, [token])
    gqc, gkc, gqs, goc, gvc, gos, gks, gvs, g_gains, g_shifts, g_bias, _ = finish(
        sums, ((0, prows),) * 8 + ((2, 16),),
        [struct(gains.shape, F32), struct(shifts.shape, F32), struct((1, blen), F32)], [token],
    )
    return (
        out, grad_inputs, grad_memory, gqs, gks, gvs, gos.T, gqc, gkc, gvc, goc.T,
        g_in, g_out.T, g_gains, g_shifts, g_bias.reshape(-1),
    )


def solution(mesh):
    sizes = mesh.devices.shape
    inner = jax.sharding.Mesh(
        mesh.devices.reshape(sizes[0], sizes[1], sizes[2] // 2, 2), ALL
    )
    rows = P("dp", "ctx", None)
    tp = ("ty", "tc")
    col = P(("dp", "ctx"), tp)
    row = P(tp, ("dp", "ctx"))
    small = P(None, ALL)
    weights = (col, col, col, row, col, col, col, row, col, row)
    tail = (small, small, P(ALL))
    return jax.shard_map(
        shards,
        mesh=inner,
        in_specs=(rows, rows, rows) + weights + tail,
        out_specs=(rows, rows, rows) + weights + tail,
        check_vma=False,
    )
```

```python
import functools

import jax
import jax.numpy as jnp
from jax import lax
from jax.experimental import pallas as pl
from jax.experimental.pallas import tpu as pltpu
from jax.sharding import PartitionSpec as P

HD = 64
EPS = 1e-05
BF = jnp.bfloat16
F32 = jnp.float32
PAIR = 2 * HD
VMEM_LIMIT = 40 << 20
SMALL_LIMIT = 16 << 20
SMALL_COST = 1_000_000_000
COVER = 10 * SMALL_COST
COSTS = dict(
    self_fwd=24_000_000_000, cross_fwd=28_000_000_000, ffn_both=25_000_000_000,
    cross_bwd=30_000_000_000, self_bwd=16_000_000_000, mem_back=9_000_000_000,
    in_back=9_000_000_000,
)
GELU_C = 0.7978845608028654
GELU_A = 0.044715


def nn(left, right):
    return lax.dot_general(left, right, (((1,), (0,)), ((), ())), preferred_element_type=F32)


def nt(left, right):
    return lax.dot_general(left, right, (((1,), (1,)), ((), ())), preferred_element_type=F32)


def norm_stats(z):
    mean = jnp.mean(z, axis=-1, keepdims=True)
    cent = z - mean
    var = jnp.mean(cent * cent, axis=-1, keepdims=True)
    inv = lax.rsqrt(var + EPS)
    return cent * inv, inv


def norm_back(grad, gain, normed, inv):
    e = grad * gain
    me = jnp.mean(e, axis=-1, keepdims=True)
    men = jnp.mean(e * normed, axis=-1, keepdims=True)
    return inv * (e - me - normed * men)


def rows_sum(a):
    return jnp.sum(a, axis=0, keepdims=True)


def split_pair(block):
    lane = lax.broadcasted_iota(jnp.int32, block.shape, 1)
    zero = jnp.zeros_like(block)
    return jnp.concatenate(
        [jnp.where(lane < HD, block, zero), jnp.where(lane < HD, zero, block)], axis=0
    )


def join_pair(both):
    q = both.shape[1] // 2
    row = lax.broadcasted_iota(jnp.int32, (both.shape[0], q), 0)
    return jnp.where(row < HD, both[:, :q], both[:, q:])


def vrow(vec_ref, row):
    return jnp.concatenate([vec_ref[j, row : row + 1] for j in range(vec_ref.shape[0])], axis=1)


def swap(pair):
    return (pair % 2) * 2 + pair // 2


def pick(own_ref, peer_ref, mat, other_half):
    shape = own_ref.shape
    own = own_ref[0, mat].reshape(shape[2] * shape[3], shape[4])
    other = peer_ref[0, mat].reshape(shape[2] * shape[3], shape[4])
    return jnp.where(other_half, other, own)


def put_pieces(ref, at, first, value, ranks_ref):
    n_x, n_z = ref.shape[1], ref.shape[2]
    rows = value.shape[0] // (n_x * n_z)
    for d in range(n_x):
        for z in range(n_z):
            i = d * n_z + z
            ref[at, d ^ ranks_ref[0], z ^ ranks_ref[1], first : first + rows] = value[
                i * rows : (i + 1) * rows
            ]


def attn_fwd_body(
    causal, q_rows, kv_parts, w, biases,
    q_ref, k_ref, v_ref, p_refs, ot_ref, o_ref, il_ref, o_all, wo_all,
):
    wq, wk, wv, wo = w
    kv = nn(kv_parts, jnp.concatenate([wk, wv], axis=1))
    k = kv[:, :PAIR].astype(BF)
    v = (kv[:, PAIR:] + biases[1]).astype(BF)
    q = (nn(q_rows, wq) + biases[0]).astype(BF) * HD ** (-0.5)
    q_ref[0] = q
    k_ref[0] = k
    v_ref[0] = v
    vt = v.T
    blocks = len(p_refs)
    rows = q.shape[0] // blocks
    keys = k.shape[0]
    for b in range(blocks):
        n = keys // blocks * (b + 1) if causal else keys
        scores = nt(k[:n], split_pair(q[b * rows : (b + 1) * rows]))
        if causal:
            last = rows
            lane = lax.broadcasted_iota(jnp.int32, (last, 2 * rows), 1)
            hidden = lane % rows < rows // 2
            scores = jnp.concatenate(
                [scores[: n - last], jnp.where(hidden, -1e30, scores[n - last :])], axis=0
            )
        top = jnp.max(scores, axis=0, keepdims=True)
        p = jnp.exp(scores - top)
        inv = 1.0 / jnp.sum(p, axis=0, keepdims=True)
        pb = p.astype(BF)
        p_refs[b][0] = pb
        ot = join_pair(nn(vt[:, :n], pb) * inv)
        span = slice(b * rows, (b + 1) * rows)
        ot_ref[0, :, span] = ot.astype(BF)
        o_ref[0, span, :] = ot.T.astype(BF)
        il_ref[0, 0:1, span] = inv[:, :rows]
        il_ref[0, 1:2, span] = inv[:, rows:]
    s = pl.program_id(0)
    o_all[s] = o_ref[0]
    wo_all[s] = wo


def wide(ref):
    return jnp.concatenate([ref[i] for i in range(ref.shape[0])], axis=1)


def finish_norm(z, n_ref, r_ref):
    normed, inv = norm_stats(z)
    n_ref[...] = normed
    r_ref[...] = jnp.broadcast_to(inv, r_ref.shape)


def self_fwd(ranks_ref, xo_ref, xp_ref, wa_ref, wb_ref, va_ref, vb_ref, *refs):
    saved, (n_ref, r_ref, vec_ref, bias_ref, x_all, acc_ref, o_all, wo_all) = refs[:8], refs[8:]
    q_ref, k_ref, v_ref, *p_refs, ot_ref, o_ref, il_ref = saved
    s = pl.program_id(0)
    blocks = 4
    half = xo_ref.shape[0] // blocks
    tiles = vec_ref.shape[0]

    @pl.when(s == 0)
    def _():
        for b in range(blocks):
            x_all[2 * b * half : (2 * b + 1) * half] = xo_ref[b * half : (b + 1) * half]
            x_all[(2 * b + 1) * half : (2 * b + 2) * half] = xp_ref[b * half : (b + 1) * half]
        both = va_ref[...].astype(F32) + vb_ref[...].astype(F32)
        vec_ref[...] = both[:tiles]
        bias_ref[...] = both[tiles]
        acc_ref[...] = xo_ref[...].astype(F32) + vrow(vec_ref, 5)

    w = [pick(wa_ref, wb_ref, i, s >= 2) for i in range(4)]
    t = swap(s) ^ ranks_ref[4]
    attn_fwd_body(True, xo_ref[...], x_all[...], w, (vec_ref[t, 3:4], vec_ref[t, 4:5]),
                  q_ref, k_ref, v_ref, p_refs, ot_ref, o_ref, il_ref, o_all, wo_all)

    @pl.when(s == pl.num_programs(0) - 1)
    def _():
        finish_norm(acc_ref[...] + nt(wide(o_all), wide(wo_all)), n_ref, r_ref)


def cross_fwd(ranks_ref, n1_ref, mo_ref, mp_ref, wa_ref, wb_ref, vec_ref, *refs):
    saved, (n_ref, r_ref, m_all, h_low, acc_ref, o_all, wo_all) = refs[:7], refs[7:]
    q_ref, k_ref, v_ref, *p_refs, ot_ref, o_ref, il_ref = saved
    s = pl.program_id(0)
    half = mo_ref.shape[0]

    @pl.when(s == 0)
    def _():
        m_all[:half] = mo_ref[...]
        m_all[half:] = mp_ref[...]
        h1 = n1_ref[...] * vrow(vec_ref, 0) + vrow(vec_ref, 6)
        h_low[...] = h1.astype(BF)
        acc_ref[...] = h1 + vrow(vec_ref, 9)

    w = [pick(wa_ref, wb_ref, i, s >= 2) for i in range(4)]
    t = swap(s) ^ ranks_ref[4]
    attn_fwd_body(False, h_low[...], m_all[...], w, (vec_ref[t, 7:8], vec_ref[t, 8:9]),
                  q_ref, k_ref, v_ref, p_refs, ot_ref, o_ref, il_ref, o_all, wo_all)

    @pl.when(s == pl.num_programs(0) - 1)
    def _():
        finish_norm(acc_ref[...] + nt(wide(o_all), wide(wo_all)), n_ref, r_ref)


def ffn_both(ranks_ref, n2_ref, r2_ref, c0, c1, c2, c3, w_ref, bias_ref, vec_ref,
             h0, h1, h2, h3, keep_ref, send_ref, dz2_ref, vg_ref, bg_ref,
             h_low, h_t, act, slope, acc, dz3_low, dz3_t, dh2):
    phase = pl.program_id(0)
    t = pl.program_id(1)
    d = n2_ref.shape[1]
    last = pl.num_programs(1) - 1
    w_in = w_ref[:, 0, 0].reshape(d, -1)
    w_out = w_ref[:, 0, 1].reshape(d, -1)
    hid = w_in.shape[1]
    strips = hid // PAIR

    @pl.when((phase == 0) & (t == 0))
    def _():
        h = n2_ref[...] * vrow(vec_ref, 1) + vrow(vec_ref, 10)
        h_low[...] = h.astype(BF)
        h_t[...] = h.astype(BF).T
        acc[...] = h + vrow(vec_ref, 11)

    @pl.when(phase == 0)
    def _():
        bias = jnp.concatenate(
            [bias_ref[pl.ds(t * strips + j, 1), :] for j in range(strips)], axis=1
        )
        u = nn(h_low[...], w_in) + bias
        cube = GELU_A * u * u
        th = jnp.tanh(GELU_C * u * (1.0 + cube))
        low = 0.5 * (1.0 + th)
        f = (u * low).astype(BF)
        act[t] = f
        slope[t] = low + 0.5 * u * (1.0 - th * th) * (GELU_C * (1.0 + 3.0 * cube))
        acc[...] += nt(f, w_out)

    @pl.when((phase == 0) & (t == last))
    def _():
        n3, r3 = norm_stats(acc[...])
        acc[...] = n3 * vrow(vec_ref, 2) + vrow(vec_ref, 12)
        put_home(acc, (h0, h1, h2, h3), ranks_ref)
        for r, ref in enumerate((c0, c1, c2, c3)):
            rows = ref.shape[0]
            at = pl.multiple_of((r ^ ranks_ref[1]) * rows, rows)
            dh2[pl.ds(at, rows), :] = ref[...].astype(F32)
        g = dh2[...]
        vg_ref[0:1] = rows_sum(g * n3)
        vg_ref[1:2] = rows_sum(g)
        dz3 = norm_back(g, vrow(vec_ref, 2), n3, r3)
        vg_ref[2:3] = rows_sum(dz3)
        low = dz3.astype(BF)
        dz3_low[...] = low
        dz3_t[...] = low.T
        dh2[...] = dz3

    @pl.when(phase == 1)
    def _():
        f = act[t]
        df = nn(dz3_low[...], w_out).astype(BF).astype(F32)
        du = (df * slope[t]).astype(BF)
        g_out = nn(dz3_t[...], f).astype(BF)
        g_in = nn(h_t[...], du).astype(BF)
        sums = rows_sum(du.astype(F32))
        for j in range(strips):
            bg_ref[pl.ds(t * strips + j, 1), :] = sums[:, j * PAIR : (j + 1) * PAIR]
        dh2[...] += nt(du, w_in)
        mine = t % 2 == ranks_ref[3]
        piece = keep_ref.shape[3] // 2

        @pl.when(mine)
        def _():
            put_pieces(keep_ref, 0, 0, g_in, ranks_ref)
            put_pieces(keep_ref, 0, piece, g_out, ranks_ref)

        @pl.when(jnp.logical_not(mine))
        def _():
            put_pieces(send_ref, 0, 0, g_in, ranks_ref)
            put_pieces(send_ref, 0, piece, g_out, ranks_ref)

    @pl.when((phase == 1) & (t == last))
    def _():
        g = dh2[...]
        n2 = n2_ref[...]
        vg_ref[3:4] = rows_sum(g * n2)
        vg_ref[4:5] = rows_sum(g)
        dz2 = norm_back(g, vrow(vec_ref, 1), n2, r2_ref[:, 0:1])
        vg_ref[5:6] = rows_sum(dz2)
        vg_ref[6:8] = jnp.zeros_like(vg_ref[6:8])
        dz2_ref[...] = dz2


def put_home(acc, refs, ranks_ref):
    rows = refs[0].shape[0]
    for r, ref in enumerate(refs):
        at = pl.multiple_of((r ^ ranks_ref[1]) * rows, rows)
        ref[...] = acc[pl.ds(at, rows), :].astype(BF)


def self_bwd(ranks_ref, act_ref, dz_ref, part_ref, w_ref, *refs):
    saved, (slot_ref, own_ref, peer_ref, out_ref, qg_ref, *scratch) = refs[:8], refs[8:]
    shape = w_ref.shape
    w = [w_ref[0, i].reshape(shape[2] * shape[3], shape[4]) for i in (0, 3)]

    def first():
        dz = dz_ref[...]
        return act_ref[...].T, dz, part_ref[...]

    def store(g_q, g_o, piece):
        put_pieces(slot_ref, 0, 0, g_q, ranks_ref)
        put_pieces(slot_ref, 0, piece, g_o, ranks_ref)

    def last(total):
        out_ref[...] = total

    attn_bwd(True, first, w, saved, store, last, slot_ref.shape[3] // 2,
             own_ref, peer_ref, qg_ref, *scratch)


def cross_bwd(ranks_ref, n_ref, r_ref, dz_ref, wa_ref, wb_ref, vec_ref, *refs):
    saved = refs[:7]
    keep_ref, send_ref, own_ref, peer_ref, out_ref, vg_ref, qg_ref, *scratch = refs[7:]
    s = pl.program_id(0)
    odd = s >= 2

    def first():
        h = n_ref[...] * vrow(vec_ref, 0) + vrow(vec_ref, 6)
        dz = dz_ref[...]
        return h.astype(BF).T, dz, dz

    def store(g_q, g_o, piece):
        @pl.when(jnp.logical_not(odd))
        def _():
            put_pieces(keep_ref, 0, 0, g_q, ranks_ref)
            put_pieces(keep_ref, 0, piece, g_o, ranks_ref)

        @pl.when(odd)
        def _():
            put_pieces(send_ref, 0, 0, g_q, ranks_ref)
            put_pieces(send_ref, 0, piece, g_o, ranks_ref)

    def last(g):
        normed = n_ref[...]
        vg_ref[0:1] = rows_sum(g * normed)
        vg_ref[1:2] = rows_sum(g)
        dz1 = norm_back(g, vrow(vec_ref, 0), normed, r_ref[:, 0:1])
        vg_ref[2:3] = rows_sum(dz1)
        vg_ref[3:8] = jnp.zeros_like(vg_ref[3:8])
        out_ref[...] = dz1

    w = [pick(wa_ref, wb_ref, i, odd) for i in (0, 3)]
    attn_bwd(False, first, w, saved, store, last, keep_ref.shape[3] // 2,
             own_ref, peer_ref, qg_ref, *scratch)


def attn_bwd(causal, first, w, saved, store, last, piece, own_ref, peer_ref, qg_ref,
             dy, dy_t, act_t, acc, dk_ref, dv_ref, dq_all, wq_all):
    s = pl.program_id(0)
    q_ref, k_ref, v_ref, *p_refs, ot_ref, o_ref, il_ref = saved
    blocks = len(p_refs)
    wq, wo = w

    @pl.when(s == 0)
    def _():
        act_t[...], dz, acc[...] = first()
        low = dz.astype(BF)
        dy[...] = low
        dy_t[...] = low.T

    q = q_ref[0]
    k = k_ref[0]
    v = v_ref[0]
    keys = k.shape[0]
    rows = q.shape[0] // blocks
    do = nn(dy[...], wo).astype(BF)
    g_o = nn(dy_t[...], o_ref[0]).astype(BF)
    do_t = do.T.astype(F32)
    prod = do_t * ot_ref[0].astype(F32)
    inv_a, inv_b = il_ref[0, 0:1], il_ref[0, 1:2]
    inner_a = jnp.sum(prod[:HD], axis=0, keepdims=True) * inv_a
    inner_b = jnp.sum(prod[HD:], axis=0, keepdims=True) * inv_b
    row = lax.broadcasted_iota(jnp.int32, do_t.shape, 0)
    dos = (do_t * jnp.where(row < HD, inv_a, inv_b)).astype(BF).T
    kt = k.T
    dqs = [None] * blocks
    for b in reversed(range(blocks)):
        n = keys // blocks * (b + 1) if causal else keys
        span = slice(b * rows, (b + 1) * rows)
        dob = split_pair(dos[span])
        qb = split_pair(q[span])
        pb = p_refs[b][0]
        dp = nt(v[:n], dob)
        inner = jnp.concatenate([inner_a[:, span], inner_b[:, span]], axis=1)
        ds = (pb.astype(F32) * (dp - inner)).astype(BF)
        dv = nn(pb, dob)
        dk = nn(ds, qb)
        if b == blocks - 1:
            dv_ref[...] = dv
            dk_ref[...] = dk
        else:
            dv_ref[:n] += dv
            dk_ref[:n] += dk
        dqs[b] = (join_pair(nn(kt[:, :n], ds)) * HD ** (-0.5)).T.astype(BF)
    dq = jnp.concatenate(dqs, axis=0)
    g_q = nn(act_t[...], dq).astype(BF)
    store(g_q, g_o, piece)
    qg_ref[0] = rows_sum(dq.astype(F32))
    dq_all[s] = dq
    wq_all[s] = wq
    for i, ref in enumerate((dk_ref, dv_ref)):
        if causal:
            part = keys // 8
            for b in range(4):
                at, to = 2 * b * part, slice(b * part, (b + 1) * part)
                own_ref[i, 0, to] = ref[at : at + part].astype(BF)
                peer_ref[i, 0, to] = ref[at + part : at + 2 * part].astype(BF)
        else:
            own_ref[i, 0] = ref[: keys // 2].astype(BF)
            peer_ref[i, 0] = ref[keys // 2 :].astype(BF)

    @pl.when(s == pl.num_programs(0) - 1)
    def _():
        last(acc[...] + nt(wide(dq_all), wide(wq_all)))


def kv_back(final, lanes, blen, ranks_ref, act_ref, *refs):
    (wk_own, wv_own, wk_peer, wv_peer), rest = refs[:4], refs[4:]
    if final:
        (own_low, got_low, own_hi, got_hi, base_ref, vgc_ref, vgf_ref, bg_ref, qgs_ref, qgs_hi,
         qgc_ref, vg_mem_ref, h0, h1, h2, h3, keep_ref, send_ref, acc, tiles) = rest
        parts = [(own_low, 0, got_low, 0), (own_low, 1, got_low, 1),
                 (own_hi, 0, got_hi, 0), (own_hi, 1, got_hi, 1)]
    else:
        own_ref, got_ref, h0, h1, h2, h3, keep_ref, send_ref, vgrad_ref, acc = rest
        parts = [(own_ref, s, got_ref, s ^ 2) for s in range(4)]
    pairs = len(parts)
    d = act_ref.shape[1]

    def gathered(own, i, got, j, kind):
        return (own[kind, i].astype(F32) + got[kind, j].astype(F32)).astype(BF)

    def weight(ref, ry):
        return ref[ry, 0].reshape(d, PAIR)

    dkv = [gathered(*part, kind) for part in parts for kind in range(2)]
    wkv = [weight(ref, ry) for refs in ((wk_own, wv_own), (wk_peer, wv_peer))
           for ry in range(2) for ref in refs]
    dkv_all = jnp.concatenate(dkv, axis=1)
    gkv = nn(act_ref[...].T, dkv_all).astype(BF)
    total = nt(dkv_all, jnp.concatenate(wkv, axis=1))
    acc[...] = total + base_ref[...] if final else total
    put_home(acc, (h0, h1, h2, h3), ranks_ref)
    n_x, n_z = keep_ref.shape[1], keep_ref.shape[2]
    piece = d // (n_x * n_z)
    for s in range(pairs):
        ref = keep_ref if s < 2 else send_ref
        for kind in range(2):
            at = (2 * s + kind) * PAIR
            put_pieces(ref, s % 2, kind * piece, gkv[:, at : at + PAIR], ranks_ref)
    sums = [rows_sum(dkv[2 * s + 1].astype(F32)) for s in range(pairs)]
    if not final:
        for s in range(pairs):
            vgrad_ref[s] = sums[s]
        return
    for j in range(pairs):
        at = slice(j * PAIR, (j + 1) * PAIR)
        rel = swap(j ^ ranks_ref[4])
        tiles[j, 0:1] = vgc_ref[0:1, at]
        tiles[j, 1:2] = vgf_ref[3:4, at]
        tiles[j, 2:3] = vgf_ref[0:1, at]
        tiles[j, 3:4] = jnp.where(rel < 2, qgs_ref[rel % 2], qgs_hi[rel % 2])
        tiles[j, 5:6] = vgc_ref[2:3, at]
        tiles[j, 6:7] = vgc_ref[1:2, at]
        tiles[j, 7:8] = qgc_ref[rel]
        tiles[j, 8:9] = vg_mem_ref[rel]
        tiles[j, 9:10] = vgf_ref[5:6, at]
        tiles[j, 10:11] = vgf_ref[4:5, at]
        tiles[j, 11:12] = vgf_ref[2:3, at]
        tiles[j, 12:13] = vgf_ref[1:2, at]
        tiles[j, 13:16] = jnp.zeros((3, PAIR), F32)
    for s in range(pairs):
        tiles[swap(s) ^ ranks_ref[4], 4:5] = sums[s]
    rows_at = lax.broadcasted_iota(jnp.int32, (16, PAIR), 0)
    for ry in range(2):
        for rc, ref in enumerate((keep_ref, send_ref)):
            for i in range(n_x):
                for k in range(n_z):
                    dc = (i ^ ranks_ref[0]) * n_z + (k ^ ranks_ref[1])
                    p = dc * pairs + ((2 * ry + rc) ^ ranks_ref[4])
                    tile = tiles[lax.div(p * lanes, PAIR)]
                    bias = bg_ref[pl.ds(lax.div(p * blen, PAIR), 1), :]
                    both = jnp.where(rows_at == 13, bias, tile).astype(BF)
                    ref[ry, i, k, 2 * piece : 2 * piece + 16] = both


def pack_rows(*refs):
    ins, outs = refs[1 : 1 + len(refs) // 2], refs[1 + len(refs) // 2 :]
    for ref, out in zip(ins, outs):
        out[...] = ref[0]


def pack_rest(*refs):
    for ref, out in zip(refs[1:9], refs[9:17]):
        out[...] = ref[0]


def pack_weights(lanes, blen, ranks_ref, wqs, wks, wvs, wos, wqc, wkc, wvc, woc, win, wout,
                 gains, shifts, bias, s_ref, c_ref, f_ref, va, vb):
    f_ref[0] = win[...]
    f_ref[1] = wout[...]
    n = wqs.shape[0]
    for i, ref in enumerate((wqc, wkc, wvc, woc)):
        c_ref[i * n : (i + 1) * n] = ref[...]
    for i, ref in enumerate((wqs, wks, wvs, wos)):
        s_ref[i * n : (i + 1) * n] = ref[...]
    p = (ranks_ref[0] * 4 + ranks_ref[1]) * 4 + ranks_ref[4]
    at = 4 * n
    va[...] = jnp.zeros_like(va)
    va[0:3, 0:lanes] = gains[...].astype(F32)
    va[3:13, 0:lanes] = shifts[...].astype(F32)
    s_ref[at : at + 16] = pltpu.roll(va[...], lax.rem(p * lanes, PAIR), 1).astype(BF)
    vb[...] = jnp.zeros_like(vb)
    vb[pl.ds(lax.div(p * blen, PAIR), 1), 0:blen] = bias[...].astype(F32)
    s_ref[at + 16 : at + 32] = pltpu.roll(vb[...], lax.rem(p * blen, PAIR), 1).astype(BF)


def whole(a):
    return pl.BlockSpec(a.shape, lambda *_: (0,) * len(a.shape))


def without(body, at, count):
    return lambda *refs: body(*refs[:at], *refs[at + count :])


def launch(body, name, grid, ranks, ins, outs, scratch=(), deps=(), limit=VMEM_LIMIT, cost=SMALL_COST):
    first = 0 if ranks is None else 1
    deps = list(deps)
    n_in, n_out = first + len(ins), len(outs)

    def with_token(*refs):
        kept = refs[:n_in] + refs[n_in + len(deps) :]
        kept[n_in + n_out][...] = jnp.zeros((8, PAIR), F32)
        body(*kept[: n_in + n_out], *kept[n_in + n_out + 1 :])

    token = struct((8, PAIR), F32)
    call = pl.pallas_call(
        with_token,
        grid_spec=pltpu.PrefetchScalarGridSpec(
            num_scalar_prefetch=first,
            grid=grid,
            in_specs=[i[1] for i in ins] + [pl.BlockSpec(memory_space=pl.ANY)] * len(deps),
            out_specs=tuple(o[1] for o in outs) + (whole(token),),
            scratch_shapes=list(scratch),
        ),
        out_shape=tuple(
            pltpu.HBM(o[0].shape, o[0].dtype) if len(o) > 2 else o[0] for o in outs
        ) + (token,),
        compiler_params=pltpu.CompilerParams(
            vmem_limit_bytes=limit, dimension_semantics=("arbitrary",) * len(grid)
        ),
        cost_estimate=pl.CostEstimate(flops=cost, bytes_accessed=1, transcendentals=0),
        name=name,
    )
    args = [
        pltpu.with_memory_space_constraint(i[0], pltpu.HBM) if len(i) > 2 else i[0] for i in ins
    ] + deps
    return call(*args) if ranks is None else call(ranks, *args)


def local(body, name, outs, *ins, ranks=None, scratch=(), deps=(), pinned=(), limit=SMALL_LIMIT,
          cost=SMALL_COST):
    return launch(
        body, name, (1,), ranks, [(a, whole(a)) for a in ins],
        [(o, whole(o), True) if i in pinned else (o, whole(o)) for i, o in enumerate(outs)],
        scratch, deps, limit, cost,
    )


def struct(shape, dtype):
    return jax.ShapeDtypeStruct(shape, dtype)


def restack(ins, outs, cuts):
    for out, (lo, hi) in zip(outs, cuts):
        for r, ref in enumerate(ins):
            out[0, 0, r] = ref[lo:hi]


def double(own, got, out, axis):
    m = own.shape[axis]
    if axis == 0:
        out[:m] = own[...]
        out[m:] = got[...]
    else:
        out[:, :m] = own[...]
        out[:, m:] = got[...]


def order(ranks_ref, parts, outs):
    for r, ref in enumerate(parts):
        rows = ref.shape[-2]
        at = pl.multiple_of((r ^ ranks_ref[1]) * rows, rows)
        for i, out in enumerate(outs):
            out[pl.ds(at, rows), :] = ref[...] if len(outs) == 1 else ref[i]


def assemble(lanes, ranks_ref, a0, a1, b0, b1, w_ref, v_ref=None, scr=None):
    pairs = 4
    n_x, n_z = a0.shape[1], a0.shape[2]
    prows = w_ref.shape[3]
    if v_ref is not None:
        scr[...] = jnp.zeros_like(scr)
    for ry in range(2):
        a_ref = (a0, a1)[ry]
        for i in range(n_x):
            for k in range(n_z):
                dc = (i ^ ranks_ref[0]) * n_z + (k ^ ranks_ref[1])
                b_ref, bi = (b0, i) if i < n_x // 2 else (b1, i - n_x // 2)
                for m in range(2):
                    span = slice(m * prows, (m + 1) * prows)
                    w_ref[ry, m, dc] = a_ref[0, i, k, span]
                    w_ref[ry, 2 + m, dc] = b_ref[ry, bi, k, span]
                if v_ref is not None:
                    at = 2 * prows
                    p = dc * pairs + ((2 * ry) ^ ranks_ref[4])
                    tile = lax.div(p * lanes, PAIR)
                    scr[tile] += b_ref[ry, bi, k, at : at + 16].astype(F32)
                    scr[pairs] += b_ref[ry, bi, k, at + 16 : at + 32].astype(F32)
    if v_ref is not None:
        v_ref[...] = scr[...].astype(BF)


def start_one(cuts, ranks_ref, *refs):
    restack(refs[0:4], refs[8:10], cuts)
    order(ranks_ref, refs[4:8], refs[10:11])


def start_two(axes, cuts, a, ga, b, gb, *refs):
    double(a, ga, refs[4], axes[0])
    double(b, gb, refs[5], axes[1])
    restack(refs[0:4], refs[6:8], cuts)


def start_five(lanes, ranks_ref, *refs):
    assemble(lanes, ranks_ref, *refs[0:4], refs[8])
    order(ranks_ref, refs[4:8], refs[9:10])


def double_both(axes, a, ga, b, gb, out_a, out_b):
    double(a, ga, out_a, axes[0])
    double(b, gb, out_b, axes[1])


def order_home(ranks_ref, *refs):
    order(ranks_ref, refs[:4], refs[4:])


def halve_body(axis_a, axis_b, cuts, *refs):
    ins, (sa, ka, sb, kb) = refs[: len(refs) - 4], refs[len(refs) - 4 :]

    def place(axis, send, keep, at, value):
        rows = value.shape[3]
        m = value.shape[axis] // 2
        lo = value[:m] if axis == 0 else value[:, :m]
        hi = value[m:] if axis == 0 else value[:, m:]
        keep[:, :, :, at : at + rows] = lo
        send[:, :, :, at : at + rows] = hi.astype(BF)

    at_a = at_b = 0
    for cut in cuts:
        if cut is None:
            keep_a, got_a, keep_b, got_b, *ins = ins
            parts = (keep_a[...] + got_a[...].astype(F32), keep_b[...] + got_b[...].astype(F32))
        else:
            keep, got, *ins = ins
            total = keep[...].astype(F32) + got[...].astype(F32)
            parts = (total[:, :, :, :cut], total[:, :, :, cut:])
        place(axis_a, sa, ka, at_a, parts[0])
        place(axis_b, sb, kb, at_b, parts[1])
        at_a += parts[0].shape[3]
        at_b += parts[1].shape[3]


def spread_body(*refs):
    ins, (s1, s2, s3, keep) = refs[:-4], refs[-4:]
    at = 0
    for own, got in zip(ins[::2], ins[1::2]):
        rows = own.shape[3]
        for r, ref in enumerate((keep, s1, s2, s3)):
            total = own[0, 0, r] + got[0, 0, r].astype(F32)
            ref[at : at + rows] = total.astype(ref.dtype)
        at += rows


def finish_body(plan, lanes, blen, ranks_ref, keep, r1, r2, r3, *outs):
    total = keep[...] + r1[...].astype(F32) + r2[...].astype(F32) + r3[...].astype(F32)
    at = 0
    outs = list(outs)
    for turn, rows in plan:
        part = total[at : at + rows]
        at += rows
        if turn == 2:
            p = (ranks_ref[0] * 4 + ranks_ref[1]) * 4 + ranks_ref[4]
            vec = pltpu.roll(part, lax.rem(PAIR - lax.rem(p * lanes, PAIR), PAIR), 1)
            outs.pop(0)[...] = vec[0:3, :lanes]
            outs.pop(0)[...] = vec[3:13, :lanes]
            own = pltpu.roll(part, lax.rem(PAIR - lax.rem(p * blen, PAIR), PAIR), 1)
            outs.pop(0)[...] = own[13:14, :blen]
        else:
            outs.pop(0)[...] = part


def home_body(every, out_ref):
    n_c, n_z, rows, _ = every.shape
    for c in range(n_c):
        for z in range(n_z):
            out_ref[z, c * rows : (c + 1) * rows, :] = every[c, z].astype(out_ref.dtype)


def half_spec(w, other):
    if other:
        return pl.BlockSpec((1,) + w.shape[1:], lambda s, _: (jnp.maximum(s - 2, 0), 0, 0, 0, 0))
    return pl.BlockSpec((1,) + w.shape[1:], lambda s, _: (jnp.minimum(s, 1), 0, 0, 0, 0))


def slot_outs(n_x, n_z, rows):
    shape = struct((2, n_x, n_z, rows, PAIR), BF)
    block = (1, n_x, n_z, rows, PAIR)
    return [
        (shape, pl.BlockSpec(block, lambda s, _: (jnp.minimum(s, 1), 0, 0, 0, 0))),
        (shape, pl.BlockSpec(block, lambda s, _: (jnp.maximum(s - 2, 0), 0, 0, 0, 0))),
    ]


def full(shape):
    return pl.BlockSpec(shape, lambda *_: (0,) * len(shape))


def run_attn_fwd(causal, ranks, rows_in, w_own, w_peer, vecs, pairs, deps):
    own, d = rows_in[0].shape
    keys = 2 * own
    blocks = 2 if causal else 1
    ns = [keys // blocks * (b + 1) if causal else keys for b in range(blocks)]
    qn = 2 * own // blocks

    def saved(shape, dtype):
        return (struct((pairs,) + shape, dtype),
                pl.BlockSpec((1,) + shape, lambda s, _: (s, 0, 0)), True)

    outs = [
        saved((own, PAIR), BF), saved((keys, PAIR), BF), saved((keys, PAIR), BF),
        *[saved((n, qn), BF) for n in ns],
        saved((PAIR, own), BF), saved((own, PAIR), BF), saved((8, own), F32),
        (struct((own, d), F32), full((own, d))) + (() if causal else (True,)),
        (struct((own, PAIR), F32), full((own, PAIR))),
    ]
    if causal:
        outs.append((struct((pairs, 16, PAIR), F32), full((pairs, 16, PAIR))))
        outs.append((struct((16, PAIR), F32), full((16, PAIR))))
    ins = [(a, whole(a)) for a in rows_in]
    ins += [(w_own, half_spec(w_own, False), True), (w_peer, half_spec(w_peer, True), True)]
    ins += [(a, whole(a)) for a in vecs]
    scratch = [pltpu.VMEM((keys, d), BF)] + ([] if causal else [pltpu.VMEM((own, d), BF)])
    scratch.append(pltpu.VMEM((own, d), F32))
    scratch += [pltpu.VMEM((pairs, own, PAIR), BF), pltpu.VMEM((pairs, d, PAIR), BF)]

    return launch(
        self_fwd if causal else cross_fwd, "self_fwd" if causal else "cross_fwd",
        (pairs,), ranks, ins, outs, scratch, deps,
        cost=COSTS["self_fwd" if causal else "cross_fwd"],
    )


def run_ffn(ranks, n2, r2, cots, w, bias, vec, n_x, n_z):
    own, d = n2.shape
    dc, parts, _, prows, hid = w.shape
    half = own // 4
    back = lambda p, t, ref: ((p * (t // 2)) ^ ref[2], 0, 0, 0, 0)
    slots = struct((2, n_x, n_z, 2 * prows, hid), BF)
    slot_block = pl.BlockSpec((1, n_x, n_z, 2 * prows, hid), back)
    outs = [(struct((half, d), BF), full((half, d)))] * 4 + [
        (slots, slot_block),
        (slots, slot_block),
        (struct((own, d), F32), full((own, d))),
        (struct((8, d), F32), full((8, d))),
        (struct((16, PAIR), F32), full((16, PAIR))),
    ]
    ins = [(n2, whole(n2), True), (r2, whole(r2))] + [(c, whole(c)) for c in cots] + [
        (w, pl.BlockSpec((dc, 1, 2, prows, hid), lambda p, t, _: (0, t, 0, 0, 0)), True),
        (bias, whole(bias)),
        (vec, whole(vec)),
    ]
    scratch = [
        pltpu.VMEM((own, d), BF),
        pltpu.VMEM((d, own), BF),
        pltpu.VMEM((parts, own, hid), BF),
        pltpu.VMEM((parts, own, hid), F32),
        pltpu.VMEM((own, d), F32),
        pltpu.VMEM((own, d), BF),
        pltpu.VMEM((d, own), BF),
        pltpu.VMEM((own, d), F32),
    ]
    return launch(
        ffn_both, "ffn_both", (2, parts), ranks, ins, outs, scratch,
        cost=COSTS["ffn_both"],
    )


def bwd_scratch(own, keys, d, pairs):
    return [
        pltpu.VMEM((own, d), BF),
        pltpu.VMEM((d, own), BF),
        pltpu.VMEM((d, own), BF),
        pltpu.VMEM((own, d), F32),
        pltpu.VMEM((keys, PAIR), F32),
        pltpu.VMEM((keys, PAIR), F32),
        pltpu.VMEM((pairs, own, PAIR), BF),
        pltpu.VMEM((pairs, d, PAIR), BF),
    ]


def per_pair(a, first=0):
    return (a, pl.BlockSpec((1,) + a.shape[1:], lambda s, _: (s + first, 0, 0)), True)


def run_cross_bwd(ranks, dz, w_own, w_peer, vec, saved, n, r, n_x, n_z, deps):
    pairs, own, _ = saved[0].shape
    keys = saved[1].shape[1]
    d = dz.shape[1]
    prows = w_own.shape[3]
    kv_spec = pl.BlockSpec((2, 1, own, PAIR), lambda s, _: (0, s, 0, 0))
    outs = slot_outs(n_x, n_z, 2 * prows) + [
        (struct((2, pairs, own, PAIR), BF), kv_spec, True),
        (struct((2, pairs, own, PAIR), BF), kv_spec, True),
        (struct((own, d), F32), full((own, d))),
        (struct((8, d), F32), full((8, d))),
        (struct((pairs, 1, PAIR), F32), pl.BlockSpec((1, 1, PAIR), lambda s, _: (s, 0, 0))),
    ]
    ins = [
        (n, whole(n)),
        (r, whole(r)),
        (dz, whole(dz)),
        (w_own, half_spec(w_own, False), True),
        (w_peer, half_spec(w_peer, True), True),
        (vec, whole(vec)),
        *[per_pair(a) for a in saved],
    ]
    return launch(
        cross_bwd, "cross_bwd", (pairs,), ranks, ins, outs, bwd_scratch(own, keys, d, pairs), deps,
        cost=COSTS["cross_bwd"],
    )


def run_self_bwd(first, ranks, act, dz, part, w, saved, n_x, n_z, deps):
    _, own, _ = saved[0].shape
    keys = saved[1].shape[1]
    d = dz.shape[1]
    prows = w.shape[3]
    pairs = 2
    kv_spec = pl.BlockSpec((2, 1, own, PAIR), lambda s, _: (0, s, 0, 0))
    slots = (1, n_x, n_z, 2 * prows, PAIR)
    outs = [
        (struct((2,) + slots[1:], BF), pl.BlockSpec(slots, lambda s, _: (s, 0, 0, 0, 0))),
        (struct((2, pairs, own, PAIR), BF), kv_spec, True),
        (struct((2, pairs, own, PAIR), BF), kv_spec, True),
        (struct((own, d), F32), full((own, d)), True),
        (struct((pairs, 1, PAIR), F32), pl.BlockSpec((1, 1, PAIR), lambda s, _: (s, 0, 0))),
    ]
    ins = [
        (act, whole(act)),
        (dz, whole(dz)) if first else (dz, whole(dz), True),
        (part, whole(part)) if first else (part, whole(part), True),
        (w, pl.BlockSpec((1,) + w.shape[1:], lambda s, _: (s, 0, 0, 0, 0)), True),
        *[per_pair(a, first) for a in saved],
    ]
    return launch(
        self_bwd, "self_bwd", (pairs,), ranks, ins, outs, bwd_scratch(own, keys, d, pairs), deps,
        cost=COSTS["self_bwd"],
    )


def run_kv_back(name, ranks, act, parts, w_own, w_peer, extra, lanes, blen, n_x, n_z, deps):
    own, d = act.shape
    pairs = 2 * w_own.shape[0]
    prows = w_own.shape[3]
    final = bool(extra)
    rows = 2 * prows + (16 if final else 0)
    half = own // 4
    slots = struct((2, n_x, n_z, rows, PAIR), BF)
    outs = [(struct((half, d), BF), full((half, d)))] * 4 + [(slots, whole(slots))] * 2
    scratch = [pltpu.VMEM((own, d), F32)]
    if final:
        scratch.append(pltpu.VMEM((pairs, 16, PAIR), F32))
    else:
        outs.append((struct((pairs, 1, PAIR), F32), full((pairs, 1, PAIR))))

    def mat(w, i):
        block = (w.shape[0], 1) + w.shape[2:]
        return (w, pl.BlockSpec(block, lambda *_: (0, i, 0, 0, 0)), True)

    ins = [
        (act, whole(act)),
        mat(w_own, 1), mat(w_own, 2), mat(w_peer, 1), mat(w_peer, 2),
        *[(a, whole(a), True) for a in parts],
        *[(a, whole(a), True) if i == 0 else (a, whole(a)) for i, a in enumerate(extra)],
    ]
    return launch(
        functools.partial(kv_back, final, lanes, blen), name, (1,), ranks, ins, outs,
        scratch, deps, cost=COSTS[name],
    )


ALL = ("dp", "ctx", "ty", "tc")


def shards(
    inputs, memory, cotangent, wq_self, wk_self, wv_self, wo_self, wq_cross, wk_cross, wv_cross,
    wo_cross, w_in, w_out, gains, shifts, ffn_bias,
):
    seqs, block, d = inputs.shape
    n_x, n_z, n_y, n_c = (lax.axis_size(a) for a in ALL)
    pairs = n_y * n_c
    half = block // n_c
    own = n_z * half
    x_rank, z_rank, y_rank, c_rank = (lax.axis_index(a) for a in ALL)
    ranks = jnp.stack([x_rank, z_rank, y_rank, c_rank, y_rank * n_c + c_rank]).astype(jnp.int32)
    prows, lanes, blen = wq_self.shape[0], gains.shape[1], ffn_bias.shape[0]
    hid = w_in.shape[1]
    x_bits = [1 << i for i in range((n_x - 1).bit_length())]

    def send(array, axis, bit):
        return lax.ppermute(array, axis, [(i, i ^ bit) for i in range(lax.axis_size(axis))])

    def rows_of(r):
        return pl.BlockSpec((1, half, d), lambda i, ref: (ref[2] * 4 + (ref[1] ^ r), ref[3], 0))

    def packed_rows(array):
        return [(array, rows_of(r), True) for r in range(n_z)]

    def around_z(parts):
        return [parts[0]] + [send(parts[r], "ctx", r) for r in range(1, n_z)]

    row_part = struct((half, d), BF)

    def sent_rows(array, name, deps):
        *parts, token = launch(
            pack_rows, name, (1,), ranks, packed_rows(array), [(row_part, whole(row_part))] * n_z,
            deps=deps, limit=SMALL_LIMIT,
        )
        return around_z(parts), token

    x_got, token = sent_rows(inputs, "pack_x", [])
    f_shape = struct((2, prows, hid), BF)
    s_pack, c_pack, f_pack, token = local(
        functools.partial(pack_weights, lanes, blen), "pack_weights",
        [struct((4 * prows + 32, PAIR), BF), struct((4 * prows, PAIR), BF), f_shape],
        wq_self, wk_self, wv_self, wo_self.T, wq_cross, wk_cross, wv_cross, wo_cross.T,
        w_in, w_out.T, gains, shifts, ffn_bias.reshape(1, -1), ranks=ranks, deps=[token],
        pinned=(2,),
        scratch=[pltpu.VMEM((16, PAIR), F32), pltpu.VMEM((16, PAIR), F32)],
    )
    s_got = around_z([s_pack] * n_z)
    w_ffn = lax.all_gather(f_pack, ALL, axis=0, tiled=False).reshape(
        n_x * n_z, pairs, 2, prows, hid
    )
    cuts_s = ((0, 2 * prows), (2 * prows, 4 * prows + 32))
    cuts_c = ((0, 2 * prows), (2 * prows, 4 * prows))

    def z_slots(cuts):
        return [struct((1, 1, n_z, hi - lo, PAIR), BF) for lo, hi in cuts]

    def doubled(array, axis):
        shape = list(array.shape)
        shape[axis] *= 2
        return struct(tuple(shape), BF)

    steps_a = [("dp", bit) for bit in x_bits] + [("ty", 1)]
    steps_b = [("ty", 1)] + [("dp", bit) for bit in x_bits]
    axis_of = {"ty": 0, "dp": 1}
    axes_at = [(axis_of[sa[0]], axis_of[sb[0]]) for sa, sb in zip(steps_a, steps_b)]

    def step(i, a, b):
        return [a, send(a, *steps_a[i]), b, send(b, *steps_b[i])]

    def more(ins, deps):
        for i in range(len(steps_a) - 1):
            a, b, token = local(
                functools.partial(double_both, axes_at[i]), "double",
                [doubled(ins[0], axes_at[i][0]), doubled(ins[2], axes_at[i][1])], *ins, deps=deps,
            )
            ins, deps = step(i + 1, a, b), [token]
        return ins, token

    sa, sb, xo, token = local(
        functools.partial(start_one, cuts_s), "start_one",
        z_slots(cuts_s) + [struct((own, d), BF)], *s_got, *x_got, ranks=ranks,
    )
    xp = send(xo, "tc", 1)
    c_got = around_z([c_pack] * n_z)
    sa, sb, ca, cb, token = local(
        functools.partial(start_two, axes_at[0], cuts_c), "start_two",
        [doubled(sa, axes_at[0][0]), doubled(sb, axes_at[0][1])] + z_slots(cuts_c),
        *step(0, sa, sb), *c_got, deps=[token],
    )
    s_last = step(1, sa, sb)
    c_last = step(0, ca, cb)
    for i in range(1, len(steps_a) - 1):
        sa, sb, token = local(
            functools.partial(double_both, axes_at[i]), "double",
            [doubled(s_last[0], axes_at[i][0]), doubled(s_last[2], axes_at[i][1])],
            *s_last, deps=[token],
        )
        s_last = step(i + 1, sa, sb)
    *packed, token = launch(
        pack_rest, "pack_rest", (1,), ranks, packed_rows(memory) + packed_rows(cotangent),
        [(row_part, whole(row_part))] * (2 * n_z), deps=[token], limit=SMALL_LIMIT,
    )
    m_got, cots = around_z(packed[:n_z]), around_z(packed[n_z:])
    c_last, token = more(c_last, [token])
    w_shape = struct((2, 4, n_x * n_z, prows, PAIR), BF)
    ws_own, v_own, token = local(
        functools.partial(assemble, lanes), "assemble",
        [w_shape, struct((pairs + 1, 16, PAIR), BF)], *s_last, ranks=ranks,
        scratch=[pltpu.VMEM((pairs + 1, 16, PAIR), F32)], deps=[token], pinned=(0,),
    )
    v_peer, ws_peer = send(v_own, "tc", 1), send(ws_own, "tc", 1)
    *saved_self, n1, r1, vec, bias, token = run_attn_fwd(
        True, ranks, (xo, xp), ws_own, ws_peer, (v_own, v_peer), pairs, [token]
    )
    wc_own, mo, token = local(
        functools.partial(start_five, lanes), "start_five", [w_shape, struct((own, d), BF)],
        *c_last, *m_got, ranks=ranks, deps=[token], pinned=(0,),
    )
    wc_peer, mp = send(wc_own, "tc", 1), send(mo, "tc", 1)
    *saved_cross, n2, r2, token = run_attn_fwd(
        False, ranks, (n1, mo, mp), wc_own, wc_peer, (vec,), pairs, [token]
    )
    *out_rows, f_keep, f_send, dz2, vg_ffn, bg, token = run_ffn(
        ranks, n2, r2, cots, w_ffn, bias, vec, n_x, n_z
    )

    def home_rows(got, deps, cost=SMALL_COST):
        here, token = local(
            order_home, "order_home", [struct((own, d), BF)], *got, ranks=ranks, deps=deps,
            cost=cost,
        )
        return here.reshape(n_z, half, d), token

    def home_all(here):
        return lax.all_gather(here, ("ty", "tc"), axis=0, tiled=False)

    def home_last(every, dtype, deps):
        return launch(
            home_body, "home", (n_y,), None,
            [(every, pl.BlockSpec((n_c, n_z, half, d), lambda y: (y, 0, 0, 0)), True)],
            [(struct((seqs, block, d), dtype),
              pl.BlockSpec((n_z, block, d), lambda y: (y, 0, 0)), True)],
            deps=deps, limit=2 * SMALL_LIMIT,
        )

    def to_core(*arrays):
        return [send(a, "tc", 1) for a in arrays]

    back_a = [("ty", 1)] + [("dp", bit) for bit in reversed(x_bits)]
    back_b = [("dp", bit) for bit in reversed(x_bits)] + [("ty", 1)]
    rounds = len(back_a)

    def shape_at(i, rows, lanes_in, steps):
        shape = [2, n_x, n_z, rows, lanes_in]
        for axis, _ in steps[: i + 1]:
            shape[axis_of[axis]] //= 2
        return tuple(shape)

    def halve(i, ins, cuts, rows, deps, cost=SMALL_COST):
        width = ins[0].shape[4]
        shape_a = shape_at(i, rows[0], width, back_a)
        shape_b = shape_at(i, rows[1], width, back_b)
        to_a, keep_a, to_b, keep_b, token = local(
            functools.partial(
                halve_body, axis_of[back_a[i][0]], axis_of[back_b[i][0]], cuts
            ),
            "halve",
            [struct(shape_a, BF), struct(shape_a, F32), struct(shape_b, BF), struct(shape_b, F32)],
            *ins, deps=deps, limit=2 * SMALL_LIMIT, cost=cost,
        )
        return [keep_a, send(to_a, *back_a[i]), keep_b, send(to_b, *back_b[i])], token

    def halve_more(groups, rows, deps, cost=SMALL_COST):
        ins, cuts = sum(groups, []), (None,) * len(groups)
        for i in range(1, rounds):
            ins, token = halve(i, ins, cuts, rows, deps, cost)
            cuts, deps = (None,), [token]
        return ins, token

    def spread(ins, deps):
        rows, width = sum(a.shape[3] for a in ins[::2]), ins[0].shape[4]
        *sends, keep, token = local(
            spread_body, "spread",
            [struct((rows, width), BF)] * 3 + [struct((rows, width), F32)], *ins, deps=deps,
        )
        return [keep] + [send(sends[r - 1], "ctx", r) for r in range(1, n_z)], token

    def finish(ins, plan, extra, deps):
        width = ins[0].shape[1]
        outs = [struct((size, width), F32) for turn, size in plan if turn != 2] + extra
        return local(
            functools.partial(finish_body, plan, lanes, blen), "finish", outs, *ins,
            ranks=ranks, deps=deps,
        )

    out_got = around_z(out_rows)
    rows_f = (prows, prows)
    ffn, token = halve(0, [f_keep, to_core(f_send)[0]], (prows,), rows_f, [token])
    c_keep, c_send, c_own, c_peer, dz1, vg_cross, qgc, token = run_cross_bwd(
        ranks, dz2, wc_own, wc_peer, vec, saved_cross, n1, r1, n_x, n_z, [token]
    )
    c_got, c_add = to_core(c_peer, c_send)
    ffn, token = halve_more([ffn], rows_f, [token])
    s_send, own_hi, peer_hi, base, qgs_hi, token = run_self_bwd(
        2, ranks, xo, dz1, dz1, ws_peer, saved_self, n_x, n_z, [token]
    )
    out_here, token = home_rows(out_got, [token])
    out_every = home_all(out_here)
    ffn, token = spread(ffn, [token])
    *mem_rows, m_keep, m_send, vgc, token = run_kv_back(
        "mem_back", ranks, mo, (c_own, c_got), wc_own, wc_peer, (), lanes, blen, n_x, n_z, [token]
    )
    mem_got = around_z(mem_rows)
    got_low, s_add = to_core(peer_hi, s_send)
    s_keep, own_low, peer_low, base, qgs, token = run_self_bwd(
        0, ranks, xo, dz1, base, ws_own, saved_self, n_x, n_z, [token]
    )
    (m_add,) = to_core(m_send)
    rows_one = (3 * prows, 3 * prows)
    one, token = halve(
        0, [c_keep, c_add, m_keep, m_add, s_keep, s_add], (prows,) * 3, rows_one, [token]
    )
    mem_here, token = home_rows(mem_got, [token], COVER)
    mem_every = home_all(mem_here)
    (got_hi,) = to_core(peer_low)
    *in_rows, i_keep, i_send, token = run_kv_back(
        "in_back", ranks, xo, (own_low, got_low, own_hi, got_hi), ws_own, ws_peer,
        (base, vg_cross, vg_ffn, bg, qgs, qgs_hi, qgc, vgc), lanes, blen, n_x, n_z, [token],
    )
    in_got = around_z(in_rows)
    one, token = halve_more([one], rows_one, [token], COVER)
    rows_two = (prows, prows + 16)
    two, token = halve(0, [i_keep, to_core(i_send)[0]], (prows,), rows_two, [token])
    in_here, token = home_rows(in_got, [token], COVER)
    in_every = home_all(in_here)
    two, token = halve_more([two], rows_two, [token])
    out, token = home_last(out_every, BF, [token])
    g_in, g_out, token = finish(ffn, ((0, prows),) * 2, [], [token])
    grad_memory, token = home_last(mem_every, F32, [token])
    sums, token = spread(one + two, [token])
    grad_inputs, token = home_last(in_every, F32, [token])
    gqc, gkc, gqs, goc, gvc, gos, gks, gvs, g_gains, g_shifts, g_bias, _ = finish(
        sums, ((0, prows),) * 8 + ((2, 16),),
        [struct(gains.shape, F32), struct(shifts.shape, F32), struct((1, blen), F32)], [token],
    )
    return (
        out, grad_inputs, grad_memory, gqs, gks, gvs, gos.T, gqc, gkc, gvc, goc.T,
        g_in, g_out.T, g_gains, g_shifts, g_bias.reshape(-1),
    )


def solution(mesh):
    sizes = mesh.devices.shape
    inner = jax.sharding.Mesh(
        mesh.devices.reshape(sizes[0], sizes[1], sizes[2] // 2, 2), ALL
    )
    rows = P("dp", "ctx", None)
    tp = ("ty", "tc")
    col = P(("dp", "ctx"), tp)
    row = P(tp, ("dp", "ctx"))
    small = P(None, ALL)
    weights = (col, col, col, row, col, col, col, row, col, row)
    tail = (small, small, P(ALL))
    return jax.shard_map(
        shards,
        mesh=inner,
        in_specs=(rows, rows, rows) + weights + tail,
        out_specs=(rows, rows, rows) + weights + tail,
        check_vma=False,
    )
```
